32 devices in a mesh: dp: 8 (over y, x, core), seq: 4 (over z).
Axes of the slice: x: 2, y: 2, z: 4, core: 2. Of those that a mesh axis runs over, the one named last changes fastest.
Arguments:
- inputs: bfloat16 [8, 3, 1024, 1024], P('dp', None, 'seq'), may hold values from -6 to 6
- encoded: bfloat16 [8, 1024, 1024], P('dp', 'seq'), may hold values from -6 to 6
- target_lengths: int32 [8, 4], P('dp'), may hold values from 1 to 512, 960 in all within a row
- source_lengths: int32 [8, 4], P('dp'), may hold values from 1 to 512, 960 in all within a row
- query_key_value: bfloat16 [1024, 3072], replicated, may hold values from -0.1875 to 0.1875
- bucket_weight: bfloat16 [1024, 512], replicated, may hold values from -0.1875 to 0.1875
- self_output: bfloat16 [1024, 1024], replicated, may hold values from -1.5 to 1.5
- cross_query: bfloat16 [1024, 1024], replicated, may hold values from -0.1875 to 0.1875
- cross_key_value: bfloat16 [1024, 2048], replicated, may hold values from -0.1875 to 0.1875
- cross_output: bfloat16 [1024, 1024], replicated, may hold values from -1.5 to 1.5
- up_weight: bfloat16 [1024, 4096], replicated, may hold values from -0.1875 to 0.1875
- up_bias: float32 [4096], replicated, may hold values from -3 to 3
- down_weight: bfloat16 [4096, 1024], replicated, may hold values from -0.09375 to 0.09375
- down_bias: float32 [1024], replicated, may hold values from -2 to 2
- norm_gain: float32 [3, 1024], replicated, may hold values from 0.5 to 1.5
- norm_shift: float32 [3, 1024], replicated, may hold values from -2 to 2
- cotangent: bfloat16 [8, 3, 1024, 1024], P('dp', None, 'seq'), may hold values from -6 to 6
Outputs:
- outputs: bfloat16 [8, 3, 1024, 1024], P('dp', None, 'seq')
- inputs_gradient: bfloat16 [8, 3, 1024, 1024], P('dp', None, 'seq')
- encoded_gradient: bfloat16 [8, 1024, 1024], P('dp', 'seq')
- query_key_value_gradient: float32 [1024, 3072], P(('dp', 'seq'))
- bucket_weight_gradient: float32 [1024, 512], P(('dp', 'seq'))
- self_output_gradient: float32 [1024, 1024], P(('dp', 'seq'))
- cross_query_gradient: float32 [1024, 1024], P(('dp', 'seq'))
- cross_key_value_gradient: float32 [1024, 2048], P(('dp', 'seq'))
- cross_output_gradient: float32 [1024, 1024], P(('dp', 'seq'))
- up_weight_gradient: float32 [1024, 4096], P(('dp', 'seq'))
- up_bias_gradient: float32 [4096], P(('dp', 'seq'))
- down_weight_gradient: float32 [4096, 1024], P(('dp', 'seq'))
- down_bias_gradient: float32 [1024], P(('dp', 'seq'))
- norm_gain_gradient: float32 [3, 1024], P(None, ('dp', 'seq'))
- norm_shift_gradient: float32 [3, 1024], P(None, ('dp', 'seq'))
The draws below stay inside these ranges and needn't reach their ends.
Inputs may be any that keep to these rules, and one draw needn't show every extreme that they name: `target_lengths`: each row's 4 documents fill its first 960 positions; the rest is padding. `source_lengths`: each row's 4 documents fill its first 960 positions; the rest is padding.
All inputs are finite; a program needn't handle non-finite values.
Results may differ from the reference program's by a relative error of at most 0.025.
Values may be sent and summed in bfloat16 or wider, within the bound.
A program may use at most 960 MiB of HBM per device.

```python
import math
from functools import partial
import jax
import jax.numpy as jnp
import numpy as np
from jax import lax

D = 1024
HEADS = 16
HEAD_DIM = 64
FF = 4096
BUCKETS = 32
NGRAM = 2
SEQ_LEN = 1024
DOCS = 4
ROWS = 8
PAD = 64
MOST = 512


def block_scale(key, shape, split, least, largest):
    loudness = 1.0
    for position, parts in split:
        draws = jax.random.uniform(jax.random.fold_in(jax.random.fold_in(key, 6), position), (parts,), jnp.float32, least / len(split), largest / len(split))
        loudness = loudness * jnp.repeat(jnp.exp(draws), shape[position] // parts).reshape((-1,) + (1,) * (len(shape) - 1 - position))
    return loudness


def length_profile(count, total, limit, lean):
    portions = [(1 << 20) // math.isqrt(grade ** lean) + 1 for grade in range(2, count + 1)]
    spare, holding = total - limit - (count - 1), [1] * (count - 1)
    while spare > 0:
        free = [i for i in range(count - 1) if holding[i] < limit]
        whole, remaining = sum([portions[i] for i in free]), spare
        for i in free:
            more = min(limit - holding[i], max(1, remaining * portions[i] // whole), spare)
            holding[i] = holding[i] + more
            spare = spare - more
    return np.array([limit] + holding)


def ragged_sizes(own_key, count, total, most, skew):
    if count == 2:
        one = jax.random.randint(own_key, (), max(1, total - most), min(most, total - 1) + 1)
        return jnp.stack([one, total - one])
    sizes = jnp.asarray(length_profile(count, total, most, skew), jnp.int32)
    pairs = (count - 1) // 2
    donor, taker = sizes[1:1 + 2 * pairs:2], sizes[2:2 + 2 * pairs:2]
    margin = jnp.minimum(donor - 1, most - taker)
    moved = jax.random.randint(jax.random.fold_in(own_key, 1), (pairs,), 0, 1 << 20) % (margin + 1)
    sizes = sizes.at[1:1 + 2 * pairs:2].set(donor - moved).at[2:2 + 2 * pairs:2].set(taker + moved)
    return sizes[jax.random.permutation(jax.random.fold_in(own_key, 2), count)]


def scatter_about(key, extent, deviation, reach, cuts=(), kind=jnp.bfloat16):
    values = deviation * jax.random.normal(key, extent, jnp.float32)
    if cuts:
        values = values * block_scale(key, extent, cuts, -0.22, 0.18)
    return jnp.clip(values, -reach, reach).astype(kind)


def setup_inputs(seed: int = 0) -> dict:
    key_list = jax.random.split(jax.random.key(seed), 18)
    inputs = scatter_about(key_list[0], (ROWS, NGRAM + 1, SEQ_LEN, D), 1.0, 6.0, ((0, 8), (2, 4)))
    encoded = scatter_about(key_list[1], (ROWS, SEQ_LEN, D), 1.0, 6.0, ((0, 8), (1, 4)))
    target_lengths = jax.vmap(lambda own: ragged_sizes(own, DOCS, SEQ_LEN - PAD, MOST, 1))(jax.random.split(key_list[2], ROWS)).reshape((ROWS, DOCS)).astype(jnp.int32)
    source_lengths = jax.vmap(lambda own: ragged_sizes(own, DOCS, SEQ_LEN - PAD, MOST, 1))(jax.random.split(key_list[3], ROWS)).reshape((ROWS, DOCS)).astype(jnp.int32)
    query_key_value = scatter_about(key_list[4], (D, 3 * D), D ** -0.5, 0.1875)
    bucket_weight = scatter_about(key_list[5], (D, HEADS * BUCKETS), D ** -0.5, 0.1875)
    self_output = scatter_about(key_list[6], (D, D), (D // 64) ** -0.5, 1.5)
    cross_query = scatter_about(key_list[7], (D, D), D ** -0.5, 0.1875)
    cross_key_value = scatter_about(key_list[8], (D, 2 * D), D ** -0.5, 0.1875)
    cross_output = scatter_about(key_list[9], (D, D), (D // 64) ** -0.5, 1.5)
    up_weight = scatter_about(key_list[10], (D, FF), D ** -0.5, 0.1875)
    up_bias = scatter_about(key_list[11], (FF,), 0.5, 3.0, (), jnp.float32)
    down_weight = scatter_about(key_list[12], (FF, D), FF ** -0.5, 0.09375)
    down_bias = scatter_about(key_list[13], (D,), 0.3, 2.0, (), jnp.float32)
    norm_gain = jnp.clip(1.0 + 0.1 * jax.random.normal(key_list[14], (3, D), jnp.float32), 0.5, 1.5)
    norm_shift = scatter_about(key_list[15], (3, D), 0.3, 2.0, (), jnp.float32)
    cotangent = scatter_about(key_list[16], (ROWS, NGRAM + 1, SEQ_LEN, D), 1.0, 6.0, ((0, 8), (2, 4)))
    return dict(inputs=inputs, encoded=encoded, target_lengths=target_lengths, source_lengths=source_lengths, query_key_value=query_key_value, bucket_weight=bucket_weight, self_output=self_output, cross_query=cross_query, cross_key_value=cross_key_value, cross_output=cross_output, up_weight=up_weight, up_bias=up_bias, down_weight=down_weight, down_bias=down_bias, norm_gain=norm_gain, norm_shift=norm_shift, cotangent=cotangent)


@jax.custom_vjp
def low(v):
    return lax.optimization_barrier(v.astype(jnp.bfloat16)).astype(jnp.float32)

@jax.custom_vjp
def low_back(v):
    return v

def low_keep(v):
    return (low(v), None)

def low_pass(kept, grad):
    return (grad,)

def back_keep(v):
    return (v, None)

def back_low(kept, grad):
    return (low(grad),)
low.defvjp(low_keep, low_pass)
low_back.defvjp(back_keep, back_low)
bucket_edges = [int(math.ceil(16.0 * 8.0 ** (bucket_level / 16.0))) for bucket_level in range(1, 16)]

def bucket_of(distance):
    forward_gap = jnp.maximum(distance, 0)
    far_bucket = jnp.full_like(forward_gap, 16)
    for bucket_edge in bucket_edges:
        far_bucket = far_bucket + (forward_gap >= bucket_edge).astype(jnp.int32)
    return jnp.where(forward_gap < 16, forward_gap, far_bucket)

def rounded(value):
    return low_back(low(value))

def highest(left, right):
    return jnp.dot(left, right, precision=lax.Precision.HIGHEST, preferred_element_type=jnp.float32)

def segment_ids(lengths, positions):
    ends = jnp.cumsum(lengths, axis=1)
    return lax.optimization_barrier(jnp.sum((positions[None, :, None] >= ends[:, None, :]).astype(jnp.int32), axis=2))

def normalize(hidden, gain, shift):
    centre = hidden - lax.optimization_barrier(jnp.mean(hidden, axis=-1, keepdims=True))
    scale_inv = lax.rsqrt(lax.optimization_barrier(jnp.mean(centre * centre, axis=-1, keepdims=True)) + 1e-05)
    return centre * scale_inv * gain + shift

def self_row(item):
    projected_row, relative_row, segment_row = item
    stream_total = NGRAM + 1
    query_count = stream_total * SEQ_LEN
    queries = projected_row[:, :, :D].reshape(query_count, HEADS, HEAD_DIM)
    own_keys = projected_row[:, :, D:2 * D].reshape(query_count, HEADS, HEAD_DIM)
    own_values = projected_row[:, :, 2 * D:].reshape(query_count, HEADS, HEAD_DIM)
    key_rows = own_keys[:SEQ_LEN]
    value_rows = own_values[:SEQ_LEN]
    table = relative_row.reshape(query_count, HEADS, BUCKETS)
    key_pos = jnp.arange(SEQ_LEN, dtype=jnp.int32)
    query_pos = jnp.tile(key_pos, stream_total)
    stream_of = jnp.repeat(jnp.arange(stream_total, dtype=jnp.int32), SEQ_LEN)
    query_seg = jnp.tile(segment_row, stream_total)
    scale = HEAD_DIM ** (-0.5)
    mixed = scale * jnp.einsum('qhd,khd->qhk', queries, key_rows, precision=lax.Precision.HIGHEST)
    index = jnp.broadcast_to(bucket_of(query_pos[:, None] - key_pos[None, :])[:, None, :], mixed.shape)
    raw = mixed + jnp.take_along_axis(table, index, axis=2)
    allowed = (query_seg[:, None] == segment_row[None, :]) & (key_pos[None, :] <= query_pos[:, None] - (stream_of[:, None] > 0).astype(jnp.int32))
    scores = jnp.where(allowed[:, None, :], low_back(raw), -1000000000.0)
    own_raw = scale * lax.optimization_barrier(jnp.sum(queries * own_keys, axis=-1)) + table[:, :, 0]
    own_score = jnp.where((stream_of > 0)[:, None], low_back(own_raw), -1000000000.0)
    probs = low(jax.nn.softmax(jnp.concatenate([scores, own_score[..., None]], axis=-1), axis=-1))
    mixed_out = jnp.einsum('qhk,khd->qhd', probs[..., :SEQ_LEN], value_rows, precision=lax.Precision.HIGHEST)
    mixed_out = mixed_out + probs[..., SEQ_LEN:] * own_values
    return rounded(mixed_out).reshape(stream_total, SEQ_LEN, D)

def cross_row(item):
    query_row, source_row, target_row, source_seg = item
    stream_total = NGRAM + 1
    query_count = stream_total * SEQ_LEN
    queries = query_row.reshape(query_count, HEADS, HEAD_DIM)
    key_rows = source_row[:, :D].reshape(SEQ_LEN, HEADS, HEAD_DIM)
    value_rows = source_row[:, D:].reshape(SEQ_LEN, HEADS, HEAD_DIM)
    query_seg = jnp.tile(target_row, stream_total)
    raw = HEAD_DIM ** (-0.5) * jnp.einsum('qhd,khd->qhk', queries, key_rows, precision=lax.Precision.HIGHEST)
    allowed = query_seg[:, None] == source_seg[None, :]
    scores = jnp.where(allowed[:, None, :], low_back(raw), -1000000000.0)
    probs = low(jax.nn.softmax(scores, axis=-1))
    mixed_out = jnp.einsum('qhk,khd->qhd', probs, value_rows, precision=lax.Precision.HIGHEST)
    return rounded(mixed_out).reshape(stream_total, SEQ_LEN, D)

def forward(inputs, encoded, query_key_value, bucket_weight, self_output, cross_query, cross_key_value, cross_output, up_weight, up_bias, down_weight, down_bias, norm_gain, norm_shift, target_seg, source_seg):
    row_total = inputs.shape[0]
    stream_total = NGRAM + 1
    flat_in = rounded(inputs.reshape(-1, D))
    projected = rounded(highest(flat_in, query_key_value)).reshape(row_total, stream_total, SEQ_LEN, 3 * D)
    relative = low_back(highest(flat_in, bucket_weight)).reshape(row_total, stream_total, SEQ_LEN, HEADS * BUCKETS)
    self_mix = lax.map(jax.checkpoint(self_row), (projected, relative, target_seg))
    branch_one = low_back(highest(self_mix.reshape(-1, D), self_output))
    hidden_one = normalize(inputs.reshape(-1, D) + branch_one, norm_gain[0], norm_shift[0])
    low_one = rounded(hidden_one)
    cross_q = rounded(highest(low_one, cross_query)).reshape(row_total, stream_total, SEQ_LEN, D)
    source_kv = rounded(highest(rounded(encoded.reshape(-1, D)), cross_key_value)).reshape(row_total, SEQ_LEN, 2 * D)
    cross_mix = lax.map(jax.checkpoint(cross_row), (cross_q, source_kv, target_seg, source_seg))
    branch_two = low_back(highest(cross_mix.reshape(-1, D), cross_output))
    hidden_two = normalize(hidden_one + branch_two, norm_gain[1], norm_shift[1])
    low_two = rounded(hidden_two)
    pre_act = low_back(highest(low_two, up_weight)) + up_bias
    activated = rounded(jax.nn.gelu(pre_act, approximate=False))
    branch_three = low_back(highest(activated, down_weight)) + down_bias
    result = normalize(hidden_two + branch_three, norm_gain[2], norm_shift[2])
    return result.reshape(inputs.shape)

def reference(inputs, encoded, target_lengths, source_lengths, query_key_value, bucket_weight, self_output, cross_query, cross_key_value, cross_output, up_weight, up_bias, down_weight, down_bias, norm_gain, norm_shift, cotangent):
    positions = jnp.arange(SEQ_LEN, dtype=jnp.int32)
    target_seg = segment_ids(target_lengths, positions)
    source_seg = segment_ids(source_lengths, positions)
    floats = [array_in.astype(jnp.float32) for array_in in (inputs, encoded, query_key_value, bucket_weight, self_output, cross_query, cross_key_value, cross_output, up_weight, up_bias, down_weight, down_bias, norm_gain, norm_shift)]
    layer = partial(forward, target_seg=target_seg, source_seg=source_seg)
    result, pull = jax.vjp(layer, *floats)
    grads = pull(cotangent.astype(jnp.float32))
    return (result.astype(jnp.bfloat16), grads[0].astype(jnp.bfloat16), grads[1].astype(jnp.bfloat16), grads[2], grads[3], grads[4], grads[5], grads[6], grads[7], grads[8], grads[9], grads[10], grads[11], grads[12], grads[13])
```

```python
import functools
import math

import jax
import jax.numpy as jnp
from jax import lax
from jax.experimental import pallas as pl
from jax.experimental.pallas import tpu as pltpu
from jax.sharding import PartitionSpec as P

HEADS = 16
HEAD_DIM = 64
BUCKETS = 32
HALO = 512
TILE = 128
NEG = -1e30
SCALE = HEAD_DIM ** (-0.5)

bucket_edges = [
    int(math.ceil(16.0 * 8.0 ** (bucket_level / 16.0))) for bucket_level in range(1, 16)
]

def bucket_of(distance):
    forward_gap = jnp.maximum(distance, 0)
    far_bucket = jnp.full_like(forward_gap, 16)
    for bucket_edge in bucket_edges:
        far_bucket = far_bucket + (forward_gap >= bucket_edge).astype(jnp.int32)
    return jnp.where(forward_gap < 16, forward_gap, far_bucket)

def iota(shape, axis):
    return lax.broadcasted_iota(jnp.int32, shape, axis)

def dot(a, b, ca, cb):
    return lax.dot_general(a, b, (((ca,), (cb,)), ((), ())), preferred_element_type=jnp.float32)

def head_masks(dtype):
    lane = iota((TILE, TILE), 1)
    low = (lane < HEAD_DIM).astype(jnp.float32)
    return low.astype(dtype), (1.0 - low).astype(dtype)

def stacked(x, low, high):
    return jnp.concatenate([x * low, x * high], axis=0)

def near_bias(rel, near_ref, head):
    index = near_ref[...] + BUCKETS * head
    return jnp.concatenate(
        [jnp.take_along_axis(rel, index[:, :TILE], axis=1), jnp.take_along_axis(rel, index[:, TILE:], axis=1)],
        axis=1,
    )

def near_tables():
    row = iota((TILE, 2 * TILE), 0)
    col = iota((TILE, 2 * TILE), 1)
    near = bucket_of(row - col + TILE)
    gap = 2 * TILE - 1 - iota((2 * TILE, TILE), 0)
    lanes = iota((2 * TILE, TILE), 1)
    onehots = [(bucket_of(gap) + BUCKETS * h == lanes).astype(jnp.bfloat16) for h in range(4)]
    return near, jnp.concatenate(onehots, axis=0)

WINDOWS = ((-TILE, 2 * TILE), (-3 * TILE, 2 * TILE), (-4 * TILE, TILE))

def self_scores(w, qs, keys, rel, col31, start2, near_ref, heads, base):
    off, width = WINDOWS[w]
    s = dot(qs, keys, 1, 1)
    c = iota((2 * TILE, width), 1)
    if w == 0:
        bias = jnp.concatenate([near_bias(rel, near_ref, h) for h in heads], axis=0)
        r = iota((2 * TILE, width), 0) % TILE
        valid = (c >= start2 - (base + off)) & (c < r + TILE)
    else:
        bias = col31
        valid = c >= start2 - (base + off)
    return s + bias, valid

def self_fwd_kernel(nq, need_ref, q_ref, ko_ref, vo_ref, kh_ref, vh_ref, rel_ref, start_ref, near_ref,
                    mix_ref, lse_ref, kx, vx):
    local = nq * TILE
    kx[:HALO, :] = kh_ref[...]
    vx[:HALO, :] = vh_ref[...]
    kx[HALO:, :] = ko_ref[:local, :]
    vx[HALO:, :] = vo_ref[:local, :]
    low, high = head_masks(jnp.bfloat16)
    lane = iota((TILE, TILE), 1)

    def tile(t, _):
        i = lax.rem(t, nq)
        row0 = pl.multiple_of(t * TILE, TILE)
        base = pl.multiple_of(HALO + i * TILE, TILE)
        rows = pl.ds(row0, TILE)
        start = start_ref[pl.ds(pl.multiple_of(i * TILE, TILE), TILE), 0:1]
        start2 = jnp.concatenate([start, start], axis=0)
        rel = rel_ref[rows, :]

        def path(count):
            lses = []
            for p in range(2):
                lanes = slice(p * TILE, (p + 1) * TILE)
                heads = (2 * p, 2 * p + 1)
                q = q_ref[rows, lanes] * jnp.bfloat16(SCALE)
                qs = stacked(q, low, high)
                ko = ko_ref[rows, lanes]
                vo = vo_ref[rows, lanes]
                rel0 = jnp.concatenate([rel[:, BUCKETS * h : BUCKETS * h + 1] for h in heads], axis=0)
                col31 = jnp.concatenate([rel[:, BUCKETS * h + 31 : BUCKETS * h + 32] for h in heads], axis=0)
                own = jnp.sum(qs.astype(jnp.float32) * jnp.concatenate([ko, ko], axis=0).astype(jnp.float32), axis=1, keepdims=True) + rel0
                ss = []
                top = own
                for w in range(count):
                    off, width = WINDOWS[w]
                    keys = kx[pl.ds(pl.multiple_of(base + off, TILE), width), lanes]
                    s, valid = self_scores(w, qs, keys, rel, col31, start2, near_ref, heads, base)
                    s = jnp.where(valid, s, NEG)
                    ss.append(s)
                    top = jnp.maximum(top, jnp.max(s, axis=1, keepdims=True))
                pown = jnp.exp(own - top)
                total = pown
                acc = None
                for w in range(count):
                    off, width = WINDOWS[w]
                    pr = jnp.exp(ss[w] - top)
                    total = total + jnp.sum(pr, axis=1, keepdims=True)
                    vals = vx[pl.ds(pl.multiple_of(base + off, TILE), width), lanes]
                    o = dot(pr.astype(jnp.bfloat16), vals, 1, 0)
                    acc = o if acc is None else acc + o
                inv = 1.0 / total
                acc = acc * inv
                pown = (pown * inv)
                mixed = jnp.where(lane < HEAD_DIM, acc[:TILE], acc[TILE:])
                ow = jnp.where(lane < HEAD_DIM, pown[:TILE], pown[TILE:])
                mix_ref[rows, lanes] = (mixed + ow * vo.astype(jnp.float32)).astype(jnp.bfloat16)
                lse = top + jnp.log(total)
                lses += [lse[:TILE], lse[TILE:]]
            out = jnp.where(lane < 64, jnp.where(lane < 32, lses[0], lses[1]), jnp.where(lane < 96, lses[2], lses[3]))
            lse_ref[rows, :] = out

        for count in range(1, 4):
            @pl.when(need_ref[i] == count)
            def _():
                path(count)
        return 0

    lax.fori_loop(0, 3 * nq, tile, 0)

def self_forward(need, proj, halo_kv, rel, start, near):
    tokens = proj.shape[0]
    local = tokens // 3
    nq = local // TILE
    W = 256
    spec = lambda rows, base: pl.BlockSpec((rows, W), lambda g, *_: (0, base + g))
    return pl.pallas_call(
        functools.partial(self_fwd_kernel, nq),
        grid_spec=pltpu.PrefetchScalarGridSpec(
            num_scalar_prefetch=1, grid=(4,),
            in_specs=[spec(tokens, 0), spec(tokens, 4), spec(tokens, 8), spec(HALO, 0), spec(HALO, 4),
                      pl.BlockSpec((tokens, TILE), lambda g, *_: (0, g)),
                      pl.BlockSpec((local, TILE), lambda g, *_: (0, 0)),
                      pl.BlockSpec((TILE, 2 * TILE), lambda g, *_: (0, 0))],
            out_specs=[spec(tokens, 0), pl.BlockSpec((tokens, TILE), lambda g, *_: (0, g))],
            scratch_shapes=[pltpu.VMEM((HALO + local, W), jnp.bfloat16)] * 2),
        out_shape=[jax.ShapeDtypeStruct((tokens, 1024), jnp.bfloat16), jax.ShapeDtypeStruct((tokens, 512), jnp.float32)],
        compiler_params=pltpu.CompilerParams(vmem_limit_bytes=40 << 20),
        cost_estimate=pl.CostEstimate(flops=6_000_000_000, bytes_accessed=12_000_000, transcendentals=6_000_000),
        name="self_forward",
    )(need, proj, proj, proj, halo_kv, halo_kv, rel, start, near)

def self_bwd_kernel(nq, need_ref, q_ref, ko_ref, vo_ref, kh_ref, vh_ref, rel_ref, start_ref, near_ref, hot_ref,
                    mix_ref, lse_ref, up_ref, dproj_ref, dhalo_ref, drel_ref, kx, vx, dkt, dvt, dqa, dro):
    g = pl.program_id(0)
    local = nq * TILE
    kx[:HALO, :] = kh_ref[...]
    vx[:HALO, :] = vh_ref[...]
    kx[HALO:, :] = ko_ref[:local, :]
    vx[HALO:, :] = vo_ref[:local, :]
    dkt[...] = jnp.zeros_like(dkt)
    dvt[...] = jnp.zeros_like(dvt)
    low, high = head_masks(jnp.bfloat16)
    lane = iota((TILE, TILE), 1)
    gl = pl.multiple_of(g * 256, 256)
    flip = (iota((TILE, TILE), 0) + iota((TILE, TILE), 1) == TILE - 1).astype(jnp.float32).astype(jnp.bfloat16)

    def tile(t, _):
        i = lax.rem(t, nq)
        row0 = pl.multiple_of(t * TILE, TILE)
        base = pl.multiple_of(HALO + i * TILE, TILE)
        rows = pl.ds(row0, TILE)
        start = start_ref[pl.ds(pl.multiple_of(i * TILE, TILE), TILE), 0:1]
        start2 = jnp.concatenate([start, start], axis=0)
        rel = rel_ref[rows, :]
        need = need_ref[i]
        for p in range(2):
            lanes = slice(p * TILE, (p + 1) * TILE)
            heads = (2 * p, 2 * p + 1)
            q = q_ref[rows, lanes] * jnp.bfloat16(SCALE)
            qs = stacked(q, low, high)
            up = up_ref[rows, lanes]
            ups = stacked(up, low, high)
            ko = ko_ref[rows, lanes]
            vo = vo_ref[rows, lanes]
            rel0 = jnp.concatenate([rel[:, BUCKETS * h : BUCKETS * h + 1] for h in heads], axis=0)
            col31 = jnp.concatenate([rel[:, BUCKETS * h + 31 : BUCKETS * h + 32] for h in heads], axis=0)
            lse = jnp.concatenate([lse_ref[rows, BUCKETS * h : BUCKETS * h + 1] for h in heads], axis=0)
            qf = qs.astype(jnp.float32)
            upf = ups.astype(jnp.float32)
            own = jnp.sum(qf * jnp.concatenate([ko, ko], axis=0).astype(jnp.float32), axis=1, keepdims=True) + rel0
            mixf = mix_ref[rows, lanes].astype(jnp.float32)
            centre = jnp.sum(upf * jnp.concatenate([mixf, mixf], axis=0), axis=1, keepdims=True)
            pown = jnp.exp(own - lse)
            dpown = jnp.sum(upf * jnp.concatenate([vo, vo], axis=0).astype(jnp.float32), axis=1, keepdims=True)
            dsown = (pown * (dpown - centre)).astype(jnp.bfloat16).astype(jnp.float32)
            pown = pown.astype(jnp.bfloat16).astype(jnp.float32)

            def window(w):
                off, width = WINDOWS[w]
                at = pl.ds(pl.multiple_of(base + off, TILE), width)
                keys = kx[at, lanes]
                vals = vx[at, lanes]
                s, valid = self_scores(w, qs, keys, rel, col31, start2, near_ref, heads, base)
                pr = jnp.exp(jnp.where(valid, s - lse, NEG))
                dp = dot(ups, vals, 1, 1)
                ds = pr * (dp - centre)
                dsb = ds.astype(jnp.bfloat16)
                prb = pr.astype(jnp.bfloat16)
                dq = dot(dsb, keys, 1, 0)
                dkt[p, :, at] += dot(qs, dsb, 0, 0)
                dvt[p, :, at] += dot(ups, prb, 0, 0)
                return ds, dsb, dq

            ds, dsb, dq = window(0)
            dqa[...] = dq
            dr = jnp.zeros((TILE, TILE), jnp.float32)
            for j, h in enumerate(heads):
                turned = dot(flip, dsb[j * TILE : (j + 1) * TILE], 1, 0)
                u = pltpu.roll(turned, 0, 1, stride=1, stride_axis=0)
                dr = dr + dot(u.astype(jnp.bfloat16), hot_ref[h * 2 * TILE : (h + 1) * 2 * TILE, :], 1, 0)
            dr = dot(flip, dr.astype(jnp.bfloat16), 1, 0)
            for j, h in enumerate(heads):
                dr = dr + jnp.where(lane == BUCKETS * h, dsown[j * TILE : (j + 1) * TILE], 0.0)
            dro[...] = dr

            for w in (1, 2):
                @pl.when(need > w)
                def _():
                    ds, dsb, dq = window(w)
                    dqa[...] += dq
                    far = jnp.sum(dsb.astype(jnp.float32), axis=1, keepdims=True)
                    dro[...] += jnp.where(lane == BUCKETS * heads[0] + 31, far[:TILE], 0.0) + jnp.where(lane == BUCKETS * heads[1] + 31, far[TILE:], 0.0)

            dq = dqa[...]
            head0 = lane < HEAD_DIM
            dq = jnp.where(head0, dq[:TILE], dq[TILE:])
            dso = jnp.where(head0, dsown[:TILE], dsown[TILE:])
            pro = jnp.where(head0, pown[:TILE], pown[TILE:])
            col = pl.multiple_of(gl + p * TILE, TILE)
            dproj_ref[rows, pl.ds(col, TILE)] = (SCALE * (dq + dso * ko.astype(jnp.float32))).astype(jnp.bfloat16)
            dproj_ref[rows, pl.ds(col + 1024, TILE)] = (dso * q.astype(jnp.float32)).astype(jnp.bfloat16)
            dproj_ref[rows, pl.ds(col + 2048, TILE)] = (pro * up.astype(jnp.float32)).astype(jnp.bfloat16)
            if p == 0:
                drel_ref[rows, :] = dro[...].astype(jnp.bfloat16)
            else:
                drel_ref[rows, :] = (drel_ref[rows, :].astype(jnp.float32) + dro[...]).astype(jnp.bfloat16)
        return 0

    lax.fori_loop(0, 3 * nq, tile, 0)
    for p in range(2):
        for j, acc in enumerate((dkt, dvt)):
            col = pl.multiple_of(gl + p * TILE + 1024 * j, TILE)
            full = acc[p, :, :].T
            dhalo_ref[:, pl.ds(col, TILE)] = full[:HALO].astype(jnp.bfloat16)
            colp = pl.multiple_of(col + 1024, TILE)
            dproj_ref[:local, pl.ds(colp, TILE)] = (full[HALO:] + dproj_ref[:local, pl.ds(colp, TILE)].astype(jnp.float32)).astype(jnp.bfloat16)

def self_backward(need, proj, halo_kv, rel, start, near, hot, mix, lse, up):
    tokens = proj.shape[0]
    local = tokens // 3
    nq = local // TILE
    W = 256
    spec = lambda rows, base: pl.BlockSpec((rows, W), lambda g, *_: (0, base + g))
    whole = lambda rows, cols: pl.BlockSpec((rows, cols), lambda g, *_: (0, 0))
    return pl.pallas_call(
        functools.partial(self_bwd_kernel, nq),
        grid_spec=pltpu.PrefetchScalarGridSpec(
            num_scalar_prefetch=1, grid=(4,),
            in_specs=[spec(tokens, 0), spec(tokens, 4), spec(tokens, 8), spec(HALO, 0), spec(HALO, 4),
                      pl.BlockSpec((tokens, TILE), lambda g, *_: (0, g)),
                      whole(local, TILE), whole(TILE, 2 * TILE), whole(8 * TILE, TILE),
                      spec(tokens, 0), pl.BlockSpec((tokens, TILE), lambda g, *_: (0, g)), spec(tokens, 0)],
            out_specs=[whole(tokens, 3072), whole(HALO, 2048), pl.BlockSpec((tokens, TILE), lambda g, *_: (0, g))],
            scratch_shapes=[pltpu.VMEM((HALO + local, W), jnp.bfloat16)] * 2
            + [pltpu.VMEM((2, TILE, HALO + local), jnp.float32)] * 2
            + [pltpu.VMEM((2 * TILE, TILE), jnp.float32), pltpu.VMEM((TILE, TILE), jnp.float32)]),
        out_shape=[jax.ShapeDtypeStruct((tokens, 3072), jnp.bfloat16), jax.ShapeDtypeStruct((HALO, 2048), jnp.bfloat16),
                   jax.ShapeDtypeStruct((tokens, 512), jnp.bfloat16)],
        compiler_params=pltpu.CompilerParams(vmem_limit_bytes=48 << 20),
        cost_estimate=pl.CostEstimate(flops=20_000_000_000, bytes_accessed=24_000_000, transcendentals=6_000_000),
        name="self_backward",
    )(need, proj, proj, proj, halo_kv, halo_kv, rel, start, near, hot, mix, lse, up)

def load_shards(z_ref, shards, local, kv_ref, kx):
    for k in range(shards):
        at = lax.rem(z_ref[0] - k + shards, shards) * local
        kx[pl.ds(pl.multiple_of(at, TILE), local), :] = kv_ref[k * local : (k + 1) * local, :]
    kx[shards * local :, :] = jnp.zeros((TILE, kx.shape[1]), kx.dtype)

def cross_fwd_kernel(nq, shards, z_ref, lo_ref, count_ref, q_ref, k_ref, v_ref, from_ref, to_ref, mix_ref, lse_ref, kx, vx):
    local = nq * TILE
    load_shards(z_ref, shards, local, k_ref, kx)
    load_shards(z_ref, shards, local, v_ref, vx)
    low, high = head_masks(jnp.bfloat16)
    lane = iota((TILE, TILE), 1)
    W = 2 * TILE

    def tile(t, _):
        i = lax.rem(t, nq)
        row0 = pl.multiple_of(t * TILE, TILE)
        here = pl.ds(pl.multiple_of(i * TILE, TILE), TILE)
        rows = pl.ds(row0, TILE)
        lo = lo_ref[i]
        first = from_ref[here, 0:1]
        last = to_ref[here, 0:1]
        first = jnp.concatenate([first, first], axis=0)
        last = jnp.concatenate([last, last], axis=0)
        lses = []
        for p in range(2):
            lanes = slice(p * TILE, (p + 1) * TILE)
            qs = stacked(q_ref[rows, lanes] * jnp.bfloat16(SCALE), low, high)

            def step(w, carry):
                top, total, acc = carry
                at = pl.multiple_of(lo + w * W, TILE)
                s = dot(qs, kx[pl.ds(at, W), lanes], 1, 1)
                c = iota((W, W), 1)
                valid = (c >= first - at) & (c < last - at)
                s = jnp.where(valid, s, NEG)
                new = jnp.maximum(top, jnp.max(s, axis=1, keepdims=True))
                fade = jnp.exp(top - new)
                pr = jnp.where(valid, jnp.exp(s - new), 0.0)
                total = total * fade + jnp.sum(pr, axis=1, keepdims=True)
                acc = acc * fade + dot(pr.astype(jnp.bfloat16), vx[pl.ds(at, W), lanes], 1, 0)
                return new, total, acc

            carry = (jnp.full((W, 1), NEG, jnp.float32), jnp.zeros((W, 1), jnp.float32), jnp.zeros((W, TILE), jnp.float32))
            top, total, acc = lax.fori_loop(0, count_ref[i], step, carry)
            acc = acc * (1.0 / total)
            mix_ref[rows, lanes] = jnp.where(lane < HEAD_DIM, acc[:TILE], acc[TILE:]).astype(jnp.bfloat16)
            lse = top + jnp.log(total)
            lses += [lse[:TILE], lse[TILE:]]
        lse_ref[rows, :] = jnp.where(lane < 64, jnp.where(lane < 32, lses[0], lses[1]), jnp.where(lane < 96, lses[2], lses[3]))
        return 0

    lax.fori_loop(0, 3 * nq, tile, 0)

def cross_forward(z, lo, count, q, kv, first, last):
    tokens = q.shape[0]
    local = tokens // 3
    nq = local // TILE
    full = kv.shape[0]
    W = 256
    spec = lambda rows, base: pl.BlockSpec((rows, W), lambda g, *_: (0, base + g))
    whole = lambda rows, cols: pl.BlockSpec((rows, cols), lambda g, *_: (0, 0))
    return pl.pallas_call(
        functools.partial(cross_fwd_kernel, nq, full // local),
        grid_spec=pltpu.PrefetchScalarGridSpec(
            num_scalar_prefetch=3, grid=(4,),
            in_specs=[spec(tokens, 0), spec(full, 0), spec(full, 4), whole(local, TILE), whole(local, TILE)],
            out_specs=[spec(tokens, 0), pl.BlockSpec((tokens, TILE), lambda g, *_: (0, g))],
            scratch_shapes=[pltpu.VMEM((full + TILE, W), jnp.bfloat16)] * 2),
        out_shape=[jax.ShapeDtypeStruct((tokens, 1024), jnp.bfloat16), jax.ShapeDtypeStruct((tokens, 512), jnp.float32)],
        compiler_params=pltpu.CompilerParams(vmem_limit_bytes=40 << 20),
        cost_estimate=pl.CostEstimate(flops=6_000_000_000, bytes_accessed=12_000_000, transcendentals=6_000_000),
        name="cross_forward",
    )(z, lo, count, q, kv, kv, first, last)

def cross_bwd_kernel(nq, shards, z_ref, lo_ref, count_ref, q_ref, k_ref, v_ref, from_ref, to_ref, mix_ref, lse_ref, up_ref,
                     dq_ref, dkv_ref, kx, vx, dkt, dvt, dqa):
    g = pl.program_id(0)
    local = nq * TILE
    load_shards(z_ref, shards, local, k_ref, kx)
    load_shards(z_ref, shards, local, v_ref, vx)
    dkt[...] = jnp.zeros_like(dkt)
    dvt[...] = jnp.zeros_like(dvt)
    low, high = head_masks(jnp.bfloat16)
    lane = iota((TILE, TILE), 1)
    W = 2 * TILE

    def tile(t, _):
        i = lax.rem(t, nq)
        row0 = pl.multiple_of(t * TILE, TILE)
        here = pl.ds(pl.multiple_of(i * TILE, TILE), TILE)
        rows = pl.ds(row0, TILE)
        lo = lo_ref[i]
        first = from_ref[here, 0:1]
        last = to_ref[here, 0:1]
        first = jnp.concatenate([first, first], axis=0)
        last = jnp.concatenate([last, last], axis=0)
        for p in range(2):
            lanes = slice(p * TILE, (p + 1) * TILE)
            heads = (2 * p, 2 * p + 1)
            qs = stacked(q_ref[rows, lanes] * jnp.bfloat16(SCALE), low, high)
            ups = stacked(up_ref[rows, lanes], low, high)
            lse = jnp.concatenate([lse_ref[rows, BUCKETS * h : BUCKETS * h + 1] for h in heads], axis=0)
            mixf = mix_ref[rows, lanes].astype(jnp.float32)
            centre = jnp.sum(ups.astype(jnp.float32) * jnp.concatenate([mixf, mixf], axis=0), axis=1, keepdims=True)
            dqa[...] = jnp.zeros_like(dqa)

            def step(w, _):
                at = pl.multiple_of(lo + w * W, TILE)
                keys = kx[pl.ds(at, W), lanes]
                s = dot(qs, keys, 1, 1)
                c = iota((W, W), 1)
                valid = (c >= first - at) & (c < last - at)
                pr = jnp.exp(jnp.where(valid, s - lse, NEG))
                dp = dot(ups, vx[pl.ds(at, W), lanes], 1, 1)
                dsb = (pr * (dp - centre)).astype(jnp.bfloat16)
                dqa[...] += dot(dsb, keys, 1, 0)
                dkt[p, :, pl.ds(at, W)] += dot(qs, dsb, 0, 0)
                dvt[p, :, pl.ds(at, W)] += dot(ups, pr.astype(jnp.bfloat16), 0, 0)
                return 0

            lax.fori_loop(0, count_ref[i], step, 0)
            dq = dqa[...]
            dq_ref[rows, lanes] = (SCALE * jnp.where(lane < HEAD_DIM, dq[:TILE], dq[TILE:])).astype(jnp.bfloat16)
        return 0

    lax.fori_loop(0, 3 * nq, tile, 0)
    for p in range(2):
        for j, acc in enumerate((dkt, dvt)):
            col = pl.multiple_of(g * 256 + p * TILE + 1024 * j, TILE)
            for k in range(shards):
                at = lax.rem(z_ref[0] - k + shards, shards) * local
                part = acc[p, :, pl.ds(pl.multiple_of(at, TILE), local)].T
                dkv_ref[k * local : (k + 1) * local, pl.ds(col, TILE)] = part.astype(jnp.bfloat16)

def cross_backward(z, lo, count, q, kv, first, last, mix, lse, up):
    tokens = q.shape[0]
    local = tokens // 3
    nq = local // TILE
    full = kv.shape[0]
    W = 256
    spec = lambda rows, base: pl.BlockSpec((rows, W), lambda g, *_: (0, base + g))
    whole = lambda rows, cols: pl.BlockSpec((rows, cols), lambda g, *_: (0, 0))
    return pl.pallas_call(
        functools.partial(cross_bwd_kernel, nq, full // local),
        grid_spec=pltpu.PrefetchScalarGridSpec(
            num_scalar_prefetch=3, grid=(4,),
            in_specs=[spec(tokens, 0), spec(full, 0), spec(full, 4), whole(local, TILE), whole(local, TILE),
                      spec(tokens, 0), pl.BlockSpec((tokens, TILE), lambda g, *_: (0, g)), spec(tokens, 0)],
            out_specs=[spec(tokens, 0), whole(full, 2048)],
            scratch_shapes=[pltpu.VMEM((full + TILE, W), jnp.bfloat16)] * 2
            + [pltpu.VMEM((2, TILE, full + TILE), jnp.float32)] * 2
            + [pltpu.VMEM((W, TILE), jnp.float32)]),
        out_shape=[jax.ShapeDtypeStruct((tokens, 1024), jnp.bfloat16), jax.ShapeDtypeStruct((full, 2048), jnp.bfloat16)],
        compiler_params=pltpu.CompilerParams(vmem_limit_bytes=48 << 20),
        cost_estimate=pl.CostEstimate(flops=20_000_000_000, bytes_accessed=24_000_000, transcendentals=6_000_000),
        name="cross_backward",
    )(z, lo, count, q, kv, kv, first, last, mix, lse, up)

def gelu_parts(x):
    u = jnp.abs(x) * (0.5**0.5)
    t = 1.0 / (1.0 + 0.5 * u)
    poly = jnp.float32(0.17087277)
    for coef in (-0.82215223, 1.48851587, -1.13520398, 0.27886807, -0.18628806, 0.09678418, 0.37409196, 1.00002368, -1.26551223):
        poly = poly * t + coef
    square = u * u
    half = 0.5 * t * jnp.exp(poly - square)
    below = jnp.where(x >= 0, 1.0 - half, half)
    dense = jnp.exp(-square) * (1.0 / math.sqrt(2.0 * math.pi))
    return x * below, below + x * dense


def up_kernel(x_ref, w_ref, b_ref, act_ref, slope_ref):
    rows = x_ref.shape[0]
    step = 256 if rows % 256 == 0 else TILE
    for r in range(0, rows, step):
        pre = dot(x_ref[r : r + step, :], w_ref[...], 1, 0) + b_ref[...]
        value, slope = gelu_parts(pre)
        act_ref[r : r + step, :] = value.astype(jnp.bfloat16)
        slope_ref[r : r + step, :] = slope.astype(jnp.bfloat16)


def up_gelu(x, w, b):
    tokens, width = x.shape
    hidden = w.shape[1]
    block = 512
    out = pl.BlockSpec((tokens, block), lambda j: (0, j))
    return pl.pallas_call(
        up_kernel,
        grid=(hidden // block,),
        in_specs=[
            pl.BlockSpec((tokens, width), lambda j: (0, 0)),
            pl.BlockSpec((width, block), lambda j: (0, j)),
            pl.BlockSpec((1, block), lambda j: (0, j)),
        ],
        out_specs=[out, out],
        out_shape=[jax.ShapeDtypeStruct((tokens, hidden), jnp.bfloat16)] * 2,
        compiler_params=pltpu.CompilerParams(vmem_limit_bytes=40 << 20),
        cost_estimate=pl.CostEstimate(
            flops=2 * tokens * width * hidden * 3, bytes_accessed=22_000_000, transcendentals=6_000_000
        ),
        name="up_gelu",
    )(x, w, b.reshape(1, hidden))


def normalize(hidden, gain, shift):
    centre = hidden - jnp.mean(hidden, axis=-1, keepdims=True)
    scale_inv = lax.rsqrt(jnp.mean(centre * centre, axis=-1, keepdims=True) + 1e-05)
    unit = centre * scale_inv
    return (unit * gain + shift, unit, scale_inv)


def normalize_back(upstream, unit, scale_inv, gain):
    along = upstream * gain
    inner = (
        along
        - jnp.mean(along, axis=-1, keepdims=True)
        - unit * jnp.mean(along * unit, axis=-1, keepdims=True)
    )
    return (scale_inv * inner, jnp.sum(upstream * unit, axis=0), jnp.sum(upstream, axis=0))


def flip_pairs(size, bit):
    return [(i, i ^ (1 << bit)) for i in range(size)]


class Mesh:
    def __init__(self):
        self.dp = lax.axis_size("dp")
        self.seq = lax.axis_size("seq")
        dp_bits = self.dp.bit_length() - 1
        seq_bits = self.seq.bit_length() - 1
        d, z = lax.axis_index("dp"), lax.axis_index("seq")
        self.bits = [("dp", self.dp, k, (d >> k) & 1) for k in reversed(range(dp_bits))]
        self.bits += [("seq", self.seq, k, (z >> k) & 1) for k in reversed(range(seq_bits))]
        core = dp_bits - 1
        rest = list(reversed(range(dp_bits - 1)))
        tail = [dp_bits + k for k in reversed(range(seq_bits))]
        self.orders = ([core] + rest + tail, [core] + rest[::-1] + tail)

    def swap(self, x, bit):
        axis, size, k, _ = self.bits[bit]
        return lax.ppermute(x, axis, flip_pairs(size, k))


def pick(x, axes, bit, index):
    at = axes.index(bit)
    return lax.dynamic_index_in_dim(x, index, at, keepdims=False), axes[:at] + axes[at + 1 :]


def pick_columns(x, mesh, fixed):
    total = len(mesh.bits)
    tokens, width = x.shape
    x = x.reshape((tokens,) + (2,) * total + (width >> total,))
    axes = list(range(total))
    for bit, index in fixed:
        at = axes.index(bit)
        x = lax.dynamic_index_in_dim(x, index, at + 1, keepdims=False)
        axes.pop(at)
    return x.reshape(tokens, -1)


def scatter_sum(mesh, order, terms):
    total = len(mesh.bits)
    width = terms[0][0].shape[1]
    deep = width >> total
    me = [bit[3] for bit in mesh.bits]
    b0, b1 = order[0], order[1]

    def product(fixed):
        out = None
        for left, right in terms:
            part = lax.dot_general(
                pick_columns(left, mesh, fixed), right, (((0,), (0,)), ((), ())), preferred_element_type=jnp.float32
            )
            out = part if out is None else out + part
        return out

    columns = terms[0][1].shape[1]
    axes0 = [b for b in range(total) if b != b0]
    axes1 = [b for b in axes0 if b != b1]
    first = mesh.swap(product([(b0, 1 - me[b0])]).astype(jnp.bfloat16), b0)
    first = first.reshape((2,) * len(axes0) + (deep, columns))
    theirs, _ = pick(first, axes0, b1, 1 - me[b1])
    mine, _ = pick(first, axes0, b1, me[b1])
    rows = deep << len(axes1)
    send = product([(b0, me[b0]), (b1, 1 - me[b1])]) + theirs.reshape(rows, columns).astype(jnp.float32)
    second = mesh.swap(send.astype(jnp.bfloat16), b1)
    keep = product([(b0, me[b0]), (b1, me[b1])]) + mine.reshape(rows, columns).astype(jnp.float32)
    keep = keep + second.astype(jnp.float32)
    return halve(mesh, keep.astype(jnp.bfloat16).reshape((2,) * len(axes1) + (deep, columns)), axes1, order[2:])


def halve(mesh, value, axes, order):
    kind = value.dtype
    last = len(order) - 1
    for n, bit in enumerate(order):
        index = mesh.bits[bit][3]
        theirs, _ = pick(value, axes, bit, 1 - index)
        mine, axes = pick(value, axes, bit, index)
        value = mine.astype(jnp.float32) + mesh.swap(theirs, bit).astype(jnp.float32)
        if n < last:
            value = value.astype(kind)
    return value


def shards(
    inputs,
    encoded,
    target_lengths,
    source_lengths,
    query_key_value,
    bucket_weight,
    self_output,
    cross_query,
    cross_key_value,
    cross_output,
    up_weight,
    up_bias,
    down_weight,
    down_bias,
    norm_gain,
    norm_shift,
    cotangent,
):
    row_count, streams, local, width = inputs.shape
    mesh = Mesh()
    size = mesh.seq
    full = local * size
    z = lax.axis_index("seq")
    begin = z * local
    bf16, f32 = jnp.bfloat16, jnp.float32
    tokens = streams * local
    up_chain = [(i, i + 1) for i in range(size - 1)]
    down_chain = [(i + 1, i) for i in range(size - 1)]

    def mm(left, right):
        return jnp.dot(left, right, preferred_element_type=f32)

    def mm_t(left, right):
        return lax.dot_general(left, right, (((1,), (1,)), ((), ())), preferred_element_type=f32)

    flat = inputs.reshape(tokens, width)
    main = flat[:local]
    hops = HALO // local
    passing, pieces = main, []
    for _ in range(hops):
        passing = lax.ppermute(passing, "seq", up_chain)
        pieces.insert(0, passing)
    halo = jnp.concatenate(pieces, axis=0)
    own_source = encoded.reshape(local, width)
    waiting, halo = lax.optimization_barrier((own_source, halo))
    sources = [own_source] + [
        lax.ppermute(waiting, "seq", [(i, (i + k) % size) for i in range(size)]) for k in range(1, size)
    ]
    source = jnp.concatenate(sources, axis=0)

    here = begin + jnp.arange(local, dtype=jnp.int32)
    ends = jnp.cumsum(target_lengths[0])
    source_ends = jnp.cumsum(source_lengths[0])
    passed = here[:, None] >= ends[None, :]
    number = jnp.sum(passed.astype(jnp.int32), axis=1)
    start = jnp.max(jnp.where(passed, ends[None, :], 0), axis=1) - begin + HALO
    is_doc = number[:, None] == jnp.arange(ends.shape[0] + 1, dtype=jnp.int32)[None, :]
    zero = jnp.zeros((1,), jnp.int32)
    first = jnp.sum(jnp.where(is_doc, jnp.concatenate([zero, source_ends])[None, :], 0), axis=1)
    last = jnp.sum(jnp.where(is_doc, jnp.concatenate([source_ends, zero + full])[None, :], 0), axis=1)
    edge = start[::TILE]
    at = HALO + TILE * jnp.arange(local // TILE, dtype=jnp.int32)
    need = 1 + (edge < at - TILE).astype(jnp.int32) + (edge < at - 3 * TILE).astype(jnp.int32)
    low_key = first[::TILE] // TILE * TILE
    count = (last[TILE - 1 :: TILE] - low_key + 2 * TILE - 1) // (2 * TILE)

    def wide(column):
        return jnp.broadcast_to(column[:, None], (local, TILE))

    start, first, last = wide(start), wide(first), wide(last)
    near, hot = near_tables()
    z_one = z.reshape(1).astype(jnp.int32)

    proj = mm(flat, query_key_value).astype(bf16)
    relative = mm(flat, bucket_weight)
    halo_kv = mm(halo, query_key_value[:, width:]).astype(bf16)
    self_mix, self_log = self_forward(need, proj, halo_kv, relative, start, near)
    hidden_one, unit_one, inv_one = normalize(flat.astype(f32) + mm(self_mix, self_output), norm_gain[0], norm_shift[0])
    low_one = hidden_one.astype(bf16)
    cross_q = mm(low_one, cross_query).astype(bf16)
    source_kv = mm(source, cross_key_value).astype(bf16)
    cross_mix, cross_log = cross_forward(z_one, low_key, count, cross_q, source_kv, first, last)
    hidden_two, unit_two, inv_two = normalize(hidden_one + mm(cross_mix, cross_output), norm_gain[1], norm_shift[1])
    low_two = hidden_two.astype(bf16)
    activated, slope = up_gelu(low_two, up_weight, up_bias)
    branch_three = mm(activated, down_weight) + down_bias
    result, unit_three, inv_three = normalize(hidden_two + branch_three, norm_gain[2], norm_shift[2])

    three_grad, gain_three, shift_three = normalize_back(
        cotangent.reshape(tokens, width).astype(f32), unit_three, inv_three, norm_gain[2]
    )
    three_low = three_grad.astype(bf16)
    down_bias_grad = jnp.sum(three_grad, axis=0)
    down_grad = scatter_sum(mesh, mesh.orders[1], [(activated, three_low)])
    pre_grad = mm_t(three_low, down_weight).astype(bf16).astype(f32) * slope.astype(f32)
    up_bias_grad = jnp.sum(pre_grad, axis=0)
    pre_low = pre_grad.astype(bf16)
    up_grad = scatter_sum(mesh, mesh.orders[0], [(low_two, pre_low)])
    hidden_two_grad = three_grad + mm_t(pre_low, up_weight).astype(bf16).astype(f32)
    two_grad, gain_two, shift_two = normalize_back(hidden_two_grad, unit_two, inv_two, norm_gain[1])
    two_low = two_grad.astype(bf16)
    cross_out_grad = scatter_sum(mesh, mesh.orders[1], [(cross_mix, two_low)])
    cross_up = mm_t(two_low, cross_output).astype(bf16)
    query_low, source_low = cross_backward(
        z_one, low_key, count, cross_q, source_kv, first, last, cross_mix, cross_log, cross_up
    )
    cross_kv_grad = scatter_sum(mesh, mesh.orders[0], [(source, source_low)])
    cross_query_grad = scatter_sum(mesh, mesh.orders[1], [(low_one, query_low)])
    source_back = mm_t(source_low, cross_key_value)
    encoded_grad = source_back[:local]
    back_low = source_back[local:].astype(bf16)
    for k in range(1, size):
        part = back_low[(k - 1) * local : k * local]
        encoded_grad = encoded_grad + lax.ppermute(
            part, "seq", [(i, (i - k) % size) for i in range(size)]
        ).astype(f32)
    hidden_one_grad = two_grad + mm_t(query_low, cross_query).astype(bf16).astype(f32)
    one_grad, gain_one, shift_one = normalize_back(hidden_one_grad, unit_one, inv_one, norm_gain[0])
    one_low = one_grad.astype(bf16)
    self_out_grad = scatter_sum(mesh, mesh.orders[1], [(self_mix, one_low)])
    self_up = mm_t(one_low, self_output).astype(bf16)
    proj_low, halo_low, table_low = self_backward(
        need, proj, halo_kv, relative, start, near, hot, self_mix, self_log, self_up
    )
    halo_back = mm_t(halo_low, query_key_value[:, width:]).astype(bf16)
    passing = halo_back[:local]
    for k in range(hops):
        passing = lax.ppermute(passing, "seq", down_chain)
        if k + 1 < hops:
            passing = (passing.astype(f32) + halo_back[(k + 1) * local : (k + 2) * local].astype(f32)).astype(bf16)
    q_grad = scatter_sum(mesh, mesh.orders[0], [(flat, proj_low[:, :width])])
    k_grad = scatter_sum(
        mesh, mesh.orders[0], [(flat, proj_low[:, width : 2 * width]), (halo, halo_low[:, :width])]
    )
    v_grad = scatter_sum(mesh, mesh.orders[1], [(flat, proj_low[:, 2 * width :]), (halo, halo_low[:, width:])])
    bucket_grad = scatter_sum(mesh, mesh.orders[1], [(flat, table_low)])
    back = mm_t(proj_low, query_key_value) + mm_t(table_low, bucket_weight)
    back = back.reshape(streams, local, width)
    back = jnp.concatenate([back[:1] + passing[None].astype(f32), back[1:]], axis=0).reshape(tokens, width)
    inputs_grad = one_grad + back.astype(bf16).astype(f32)

    devices = mesh.dp * mesh.seq
    gains = jnp.stack([gain_one, gain_two, gain_three]).reshape(3, devices, -1).transpose(1, 0, 2)
    shifts = jnp.stack([shift_one, shift_two, shift_three]).reshape(3, devices, -1).transpose(1, 0, 2)
    each = width // devices
    small = jnp.concatenate(
        [
            up_bias_grad.reshape(devices, -1),
            down_bias_grad.reshape(devices, -1),
            gains.reshape(devices, -1),
            shifts.reshape(devices, -1),
        ],
        axis=1,
    )
    bits = len(mesh.bits)
    small = halve(mesh, small.reshape((2,) * bits + (1, -1)), list(range(bits)), mesh.orders[0])[0]
    wide_each = up_bias_grad.shape[0] // devices
    cuts = [wide_each, wide_each + each, wide_each + 4 * each]
    up_bias_grad, down_bias_grad, gains, shifts = jnp.split(small, cuts)
    return (
        result.astype(bf16).reshape(inputs.shape),
        inputs_grad.astype(bf16).reshape(inputs.shape),
        encoded_grad.astype(bf16).reshape(encoded.shape),
        jnp.concatenate([q_grad, k_grad, v_grad], axis=1),
        bucket_grad,
        self_out_grad,
        cross_query_grad,
        cross_kv_grad,
        cross_out_grad,
        up_grad,
        up_bias_grad,
        down_grad,
        down_bias_grad,
        gains.reshape(3, each),
        shifts.reshape(3, each),
    )


def solution(mesh):
    placed = (
        P("dp", None, "seq", None),
        P("dp", "seq", None),
        P("dp", None),
        P("dp", None),
        P(),
        P(),
        P(),
        P(),
        P(),
        P(),
        P(),
        P(),
        P(),
        P(),
        P(),
        P(),
        P("dp", None, "seq", None),
    )
    return jax.shard_map(
        shards,
        mesh=mesh,
        in_specs=placed,
        out_specs=(
            P("dp", None, "seq", None),
            P("dp", None, "seq", None),
            P("dp", "seq", None),
            P(("dp", "seq"), None),
            P(("dp", "seq"), None),
            P(("dp", "seq"), None),
            P(("dp", "seq"), None),
            P(("dp", "seq"), None),
            P(("dp", "seq"), None),
            P(("dp", "seq"), None),
            P(("dp", "seq")),
            P(("dp", "seq"), None),
            P(("dp", "seq")),
            P(None, ("dp", "seq")),
            P(None, ("dp", "seq")),
        ),
        check_vma=False,
    )
```

```python
import functools
import math

import jax
import jax.numpy as jnp
from jax import lax
from jax.experimental import pallas as pl
from jax.experimental.pallas import tpu as pltpu
from jax.sharding import PartitionSpec as P

HEAD_DIM = 64
BUCKETS = 32
STREAMS = 3
HALO = 512
TILE = 128
PAIR = 2 * TILE
ROWS = 2 * STREAMS * TILE
NEG = -1e30
SCALE = HEAD_DIM ** (-0.5)

bucket_edges = [
    int(math.ceil(16.0 * 8.0 ** (bucket_level / 16.0))) for bucket_level in range(1, 16)
]


def bucket_of(distance):
    forward_gap = jnp.maximum(distance, 0)
    far_bucket = jnp.full_like(forward_gap, 16)
    for bucket_edge in bucket_edges:
        far_bucket = far_bucket + (forward_gap >= bucket_edge).astype(jnp.int32)
    return jnp.where(forward_gap < 16, forward_gap, far_bucket)


def iota(shape, axis):
    return lax.broadcasted_iota(jnp.int32, shape, axis)


def dot(a, b, ca, cb):
    return lax.dot_general(a, b, (((ca,), (cb,)), ((), ())), preferred_element_type=jnp.float32)


def bias_tables():
    col = iota((PAIR, PAIR), 1)
    gap = jnp.where(col < TILE, (TILE - col) % TILE, PAIR)
    row = iota((PAIR, PAIR), 0) % TILE
    back = TILE - 1 - iota((TILE, TILE), 0)
    lane = iota((TILE, TILE), 1)
    skews = [(bucket_of(gap) + BUCKETS * h == row).astype(jnp.bfloat16) for h in range(4)]
    hots = [(bucket_of(back) + BUCKETS * h == lane).astype(jnp.bfloat16) for h in range(4)]
    return jnp.concatenate(skews, axis=0), jnp.concatenate(hots, axis=0)


def head_masks():
    low = (iota((TILE, TILE), 1) < HEAD_DIM).astype(jnp.float32)
    return low.astype(jnp.bfloat16), (1.0 - low).astype(jnp.bfloat16)


def stream_rows(s, local, here):
    return pl.ds(pl.multiple_of(s * local + here, TILE), TILE)


def stack_heads(ref, local, here, lanes, masks, extra=None, scale=None):
    out = []
    for s in range(STREAMS):
        x = ref[stream_rows(s, local, here), lanes]
        if scale is not None:
            x = x * jnp.bfloat16(scale)
        for mask in masks:
            y = x * mask
            out.append(y if extra is None else jnp.concatenate([y, extra], axis=1))
    return jnp.concatenate(out, axis=0)


def part(n):
    return slice(n * TILE, (n + 1) * TILE)


def lane_max(x):
    return jnp.broadcast_to(jnp.max(x, axis=1, keepdims=True), (TILE, TILE))


def lane_sum(x):
    return jnp.broadcast_to(jnp.sum(x, axis=1, keepdims=True), (TILE, TILE))


def roll_rows(x):
    return pltpu.roll(x, 0, 1, stride=1, stride_axis=0)


WINDOWS = ((-TILE, PAIR, 0), (-3 * TILE, PAIR, PAIR), (-4 * TILE, TILE, 2 * PAIR))
REACH = 5 * TILE


def columns(rows, base):
    return pl.BlockSpec((rows, PAIR), lambda g, *_: (0, base + g))


def whole(rows, cols):
    return pl.BlockSpec((rows, cols), lambda g, *_: (0, 0))


def weights_spec(steps, reach):
    return pl.BlockSpec((1, steps, ROWS, reach), lambda g, *_: (g, 0, 0, 0))


def self_fwd_kernel(nq, need_ref, q_ref, ko_ref, vo_ref, kh_ref, vh_ref, rel_ref, doc_ref, aug_ref, skew_ref,
                    mix_ref, pr_ref, kx, vx, sc, st, bz):
    local = nq * TILE
    for p in range(2):
        kx[p, :HALO, :TILE] = kh_ref[:, part(p)]
        kx[p, HALO:, :TILE] = ko_ref[:local, part(p)]
        kx[p, :, TILE:] = aug_ref[...]
    vx[:HALO, :] = vh_ref[...]
    vx[HALO:, :] = vo_ref[:local, :]
    masks = head_masks()
    lane = iota((TILE, TILE), 1)
    row = iota((TILE, TILE), 0)

    def step(n, _):
        i, p = n // 2, n % 2
        here = pl.multiple_of(i * TILE, TILE)
        lanes = pl.ds(pl.multiple_of(p * TILE, TILE), TILE)
        qs = stack_heads(q_ref, local, here, lanes, masks, doc_ref[pl.ds(here, TILE), :], SCALE)
        table = []
        for s in range(STREAMS):
            rel = rel_ref[stream_rows(s, local, here), :]
            high = rel.astype(jnp.bfloat16)
            table.append(jnp.concatenate([high, (rel - high.astype(jnp.float32)).astype(jnp.bfloat16)], axis=1))
        table = jnp.concatenate(table, axis=0)
        for j in range(2):
            bz[j, :, :] = dot(table, skew_ref[pl.ds(pl.multiple_of((2 * p + j) * PAIR, PAIR), PAIR), :], 1, 0)

        def path(count):
            windows = []
            for off, width, at in WINDOWS[:count]:
                keys = pl.ds(pl.multiple_of(here + HALO + off, TILE), width)
                sc[:, at : at + width] = dot(qs, kx[p, keys, :], 1, 1)
                windows.append((at, width, keys))
            reach = windows[-1][0] + windows[-1][1]
            for b in range(2 * STREAMS):
                s, j = b // 2, b % 2
                rows = stream_rows(s, local, here)
                near = roll_rows(bz[j, part(s), :TILE])
                steady = bz[j, part(s), TILE:]
                left = sc[part(b), part(0)] + jnp.where(lane > row, near, steady)
                right = sc[part(b), part(1)]
                if s > 0:
                    own = lane_sum(qs[part(b), :TILE].astype(jnp.float32) * ko_ref[rows, lanes].astype(jnp.float32))
                    right = jnp.where(lane == row, own, right)
                right = right + jnp.where(lane <= row, near, NEG)
                far = [sc[part(b), part(m)] for m in range(2, reach // TILE)]
                top = jnp.maximum(left, right)
                if far:
                    most = far[0]
                    for x in far[1:]:
                        most = jnp.maximum(most, x)
                    top = jnp.maximum(top, most + steady)
                top = lane_max(top)
                base = top - steady
                weights = [jnp.exp(left - top), jnp.exp(right - top)] + [jnp.exp(x - base) for x in far]
                total = weights[0]
                for x in weights[1:]:
                    total = total + x
                inverse = 1.0 / lane_sum(total)
                for m, x in enumerate(weights):
                    x = (x * inverse).astype(jnp.bfloat16)
                    pr_ref[0, n, part(b), part(m)] = x
                    if m == 1 and s > 0:
                        st[part(b), :] = lane_sum(jnp.where(lane == row, x.astype(jnp.float32), 0.0))
            if reach < REACH:
                pr_ref[0, n, :, reach:] = jnp.zeros((ROWS, REACH - reach), jnp.bfloat16)
            acc = None
            for at, width, keys in windows:
                o = dot(pr_ref[0, n, :, at : at + width], vx[keys, lanes], 1, 0)
                acc = o if acc is None else acc + o
            main = vo_ref[stream_rows(0, local, here), lanes].astype(jnp.float32)
            for s in range(STREAMS):
                rows = stream_rows(s, local, here)
                a, b = part(2 * s), part(2 * s + 1)
                mixed = jnp.where(lane < HEAD_DIM, acc[a], acc[b])
                if s > 0:
                    own = jnp.where(lane < HEAD_DIM, st[a, :], st[b, :])
                    mixed = mixed + own * (vo_ref[rows, lanes].astype(jnp.float32) - main)
                mix_ref[rows, lanes] = mixed.astype(jnp.bfloat16)

        for count in range(1, 4):
            @pl.when(need_ref[i] == count)
            def _():
                path(count)
        return 0

    lax.fori_loop(0, 2 * nq, step, 0)


def self_forward(need, proj, halo_kv, rel, doc, aug, skew):
    tokens = proj.shape[0]
    local = tokens // STREAMS
    width = proj.shape[1] // 3
    grid = width // PAIR
    steps = 2 * local // TILE
    return pl.pallas_call(
        functools.partial(self_fwd_kernel, local // TILE),
        grid_spec=pltpu.PrefetchScalarGridSpec(
            num_scalar_prefetch=1, grid=(grid,),
            in_specs=[
                columns(tokens, 0), columns(tokens, grid), columns(tokens, 2 * grid), columns(HALO, 0), columns(HALO, grid),
                pl.BlockSpec((tokens, TILE), lambda g, *_: (0, g)),
                whole(local, TILE), whole(HALO + local, TILE), whole(4 * PAIR, PAIR),
            ],
            out_specs=[columns(tokens, 0), weights_spec(steps, REACH)],
            scratch_shapes=[
                pltpu.VMEM((2, HALO + local, PAIR), jnp.bfloat16), pltpu.VMEM((HALO + local, PAIR), jnp.bfloat16),
                pltpu.VMEM((ROWS, REACH), jnp.float32), pltpu.VMEM((ROWS, TILE), jnp.float32),
                pltpu.VMEM((2, STREAMS * TILE, PAIR), jnp.float32),
            ]),
        out_shape=[jax.ShapeDtypeStruct((tokens, width), jnp.bfloat16),
                   jax.ShapeDtypeStruct((grid, steps, ROWS, REACH), jnp.bfloat16)],
        compiler_params=pltpu.CompilerParams(vmem_limit_bytes=40 << 20),
        cost_estimate=pl.CostEstimate(flops=15_000_000_000, bytes_accessed=20_000_000, transcendentals=8_000_000),
        name="self_forward",
    )(need, proj, proj, proj, halo_kv, halo_kv, rel, doc, aug, skew)


def self_bwd_kernel(nq, plan, q_ref, ko_ref, vo_ref, kh_ref, vh_ref, hot_ref, mix_ref, up_ref, pr_ref, *refs):
    arrays, handed, refs = refs[: plan.many], refs[plan.many], refs[plan.many + 1 :]
    dproj_ref, dhalo_ref, drel_ref, sums_ref, got, kx, vx, dp, pz, ds, cb, st, dkt, dvt, dqa = refs[:15]
    g = pl.program_id(0)
    comm = Comm(plan, arrays, sums_ref, refs[15:-1])
    hand = Handing(handed.shape[0] + 1, handed.shape[0], True, handed, got, refs[-1])

    @pl.when(g == 0)
    def _():
        comm.barrier()
        hand.start()

    local = nq * TILE
    kx[:HALO, :] = kh_ref[...]
    kx[HALO:, :] = ko_ref[:local, :]
    vx[:HALO, :] = vh_ref[...]
    vx[HALO:, :] = vo_ref[:local, :]
    dkt[...] = jnp.zeros_like(dkt)
    dvt[...] = jnp.zeros_like(dvt)
    masks = head_masks()
    lane = iota((TILE, TILE), 1)
    row = iota((TILE, TILE), 0)
    flip = (row + lane == TILE - 1).astype(jnp.float32).astype(jnp.bfloat16)
    gl = pl.multiple_of(g * PAIR, PAIR)
    third = q_ref.shape[1] * pl.num_programs(0)

    def step(n, _):
        i, p = n // 2, n % 2
        here = pl.multiple_of(i * TILE, TILE)
        lanes = pl.ds(pl.multiple_of(p * TILE, TILE), TILE)
        comm.step(g * 2 * nq + n)
        qs = stack_heads(q_ref, local, here, lanes, masks, None, SCALE)
        ups = stack_heads(up_ref, local, here, lanes, masks)
        qt = qs.T
        upt = ups.T

        def window(w):
            off, width, at = WINDOWS[w]
            keys = pl.ds(pl.multiple_of(here + HALO + off, TILE), width)
            dp[:, :width] = dot(ups, vx[keys, lanes], 1, 1)
            for b in range(2 * STREAMS):
                s = b // 2
                rows = stream_rows(s, local, here)
                if w == 0:
                    upf = ups[part(b)].astype(jnp.float32)
                    centre = lane_sum(upf * mix_ref[rows, lanes].astype(jnp.float32))
                    st[0, part(b), :] = centre
                else:
                    centre = st[0, part(b), :]
                far = None
                for m in range(width // TILE):
                    x = pr_ref[0, n, part(b), slice(at + m * TILE, at + (m + 1) * TILE)]
                    xf = x.astype(jnp.float32)
                    y = (xf * (dp[part(b), part(m)] - centre)).astype(jnp.bfloat16)
                    if w > 0:
                        ds[part(b), part(m)] = y
                        far = y.astype(jnp.float32) if far is None else far + y.astype(jnp.float32)
                        continue
                    yf = y.astype(jnp.float32)
                    if m == 0:
                        ds[part(b), part(0)] = y
                        pz[part(b), part(0)] = x
                        band = jnp.where(lane > row, yf, 0.0)
                        st[3, part(b), :] = yf - band
                        continue
                    if s > 0:
                        own_weight = lane_sum(jnp.where(lane == row, xf, 0.0))
                        own_grad = own_weight * (lane_sum(upf * vo_ref[rows, lanes].astype(jnp.float32)) - centre)
                        own_grad = own_grad.astype(jnp.bfloat16).astype(jnp.float32)
                        st[1, part(b), :] = own_weight
                        st[2, part(b), :] = own_grad
                        xf = jnp.where(lane == row, 0.0, xf)
                        yf = jnp.where(lane == row, 0.0, yf)
                        band = band + jnp.where(lane == row, own_grad, yf)
                        pz[part(b), part(1)] = xf.astype(jnp.bfloat16)
                        ds[part(b), part(1)] = yf.astype(jnp.bfloat16)
                    else:
                        band = band + yf
                        pz[part(b), part(1)] = x
                        ds[part(b), part(1)] = y
                    cb[:, part(b)] = band.astype(jnp.bfloat16)
                if w > 0:
                    st[3, part(b), :] += far
            grad = ds[:, :width]
            weights = pz[...] if w == 0 else pr_ref[0, n, :, at : at + width]
            dkt[p, :, keys] += dot(qt, grad, 1, 0)
            dvt[p, :, keys] += dot(upt, weights, 1, 0)
            return dot(grad, kx[keys, lanes], 1, 0)

        dqa[...] = window(0)
        turned = dot(flip, cb[...], 1, 0)
        rolled = [roll_rows(turned[:, part(b)]).astype(jnp.bfloat16) for b in range(2 * STREAMS)]
        rolled = jnp.concatenate([jnp.concatenate(rolled[2 * s : 2 * s + 2], axis=1) for s in range(STREAMS)], axis=0)
        table = dot(rolled, hot_ref[pl.ds(pl.multiple_of(p * PAIR, PAIR), PAIR), :], 1, 0).astype(jnp.bfloat16)
        table = dot(flip, jnp.concatenate([table[part(s)] for s in range(STREAMS)], axis=1), 1, 0)

        dq = dqa[...] + window(1) + window(2)
        for s in range(STREAMS):
            rows = stream_rows(s, local, here)
            a, b = part(2 * s), part(2 * s + 1)
            dqs = jnp.where(lane < HEAD_DIM, dq[a], dq[b])
            col = pl.multiple_of(gl + p * TILE, TILE)
            if s > 0:
                own_weight = jnp.where(lane < HEAD_DIM, st[1, a, :], st[1, b, :])
                own_grad = jnp.where(lane < HEAD_DIM, st[2, a, :], st[2, b, :])
                dqs = dqs + own_grad * ko_ref[rows, lanes].astype(jnp.float32)
                dproj_ref[rows, pl.ds(pl.multiple_of(col + third, TILE), TILE)] = (
                    own_grad * (SCALE * q_ref[rows, lanes].astype(jnp.float32))
                ).astype(jnp.bfloat16)
                dproj_ref[rows, pl.ds(pl.multiple_of(col + 2 * third, TILE), TILE)] = (
                    own_weight * up_ref[rows, lanes].astype(jnp.float32)
                ).astype(jnp.bfloat16)
            dproj_ref[rows, pl.ds(col, TILE)] = (SCALE * dqs).astype(jnp.bfloat16)
            dr = table[:, part(s)]
            for j, blk in enumerate((a, b)):
                dr = dr + jnp.where(lane == BUCKETS * (2 * p + j) + BUCKETS - 1, lane_sum(st[3, blk, :]), 0.0)

            @pl.when(p == 0)
            def _():
                drel_ref[rows, :] = dr.astype(jnp.bfloat16)

            @pl.when(p == 1)
            def _():
                drel_ref[rows, :] = (drel_ref[rows, :].astype(jnp.float32) + dr).astype(jnp.bfloat16)
        return 0

    lax.fori_loop(0, 2 * nq, step, 0)
    for p in range(2):
        for j, acc in enumerate((dkt, dvt)):
            col = pl.multiple_of(gl + p * TILE + third * j, TILE)
            full = acc[p, :, :].T.astype(jnp.bfloat16)
            dhalo_ref[:, pl.ds(col, TILE)] = full[:HALO]
            dproj_ref[:local, pl.ds(pl.multiple_of(col + third, TILE), TILE)] = full[HALO:]

    @pl.when(g == pl.num_programs(0) - 1)
    def _():
        comm.rest(4 * 2 * nq)
        hand.wait()


def self_backward(plan, arrays, handed, proj, halo_kv, hot, mix, up, weights):
    tokens = proj.shape[0]
    local = tokens // STREAMS
    width = proj.shape[1] // 3
    grid = width // PAIR
    steps = 2 * local // TILE
    return pl.pallas_call(
        functools.partial(self_bwd_kernel, local // TILE, plan),
        grid=(grid,),
        in_specs=[
            columns(tokens, 0), columns(tokens, grid), columns(tokens, 2 * grid), columns(HALO, 0), columns(HALO, grid),
            whole(4 * TILE, TILE), columns(tokens, 0), columns(tokens, 0), weights_spec(steps, REACH),
        ] + plan.in_specs() + [pl.BlockSpec(memory_space=pl.ANY)],
        out_specs=[
            whole(tokens, 3 * width), whole(HALO, 2 * width), pl.BlockSpec((tokens, TILE), lambda g, *_: (0, g)), plan.out_spec(),
            pl.BlockSpec(memory_space=pl.ANY),
        ],
        scratch_shapes=[
            pltpu.VMEM((HALO + local, PAIR), jnp.bfloat16), pltpu.VMEM((HALO + local, PAIR), jnp.bfloat16),
            pltpu.VMEM((ROWS, PAIR), jnp.float32), pltpu.VMEM((ROWS, PAIR), jnp.bfloat16),
            pltpu.VMEM((ROWS, PAIR), jnp.bfloat16), pltpu.VMEM((TILE, ROWS), jnp.bfloat16),
            pltpu.VMEM((4, ROWS, TILE), jnp.float32),
            pltpu.VMEM((2, TILE, HALO + local), jnp.float32), pltpu.VMEM((2, TILE, HALO + local), jnp.float32),
            pltpu.VMEM((ROWS, TILE), jnp.float32),
        ] + plan.scratch() + handing_scratch(handed.shape[0]),
        out_shape=[
            jax.ShapeDtypeStruct((tokens, 3 * width), jnp.bfloat16), jax.ShapeDtypeStruct((HALO, 2 * width), jnp.bfloat16),
            jax.ShapeDtypeStruct((tokens, width // 2), jnp.bfloat16), plan.out_shape(),
            jax.ShapeDtypeStruct(handed.shape, handed.dtype),
        ],
        compiler_params=pltpu.CompilerParams(collective_id=plan.number, has_side_effects=True, vmem_limit_bytes=56 << 20),
        cost_estimate=pl.CostEstimate(flops=40_000_000_000, bytes_accessed=30_000_000, transcendentals=8_000_000),
        name="self_backward",
    )(proj, proj, proj, halo_kv, halo_kv, hot, mix, up, weights, *plan.views(arrays), handed)


def gather_shards(local, ref, place):
    shards = ref.shape[0] // local
    z = lax.axis_index("seq")
    for k in range(shards):
        at = pl.ds(pl.multiple_of(lax.rem(z - k + shards, shards) * local, TILE), local)
        place(at, ref[k * local : (k + 1) * local, :])


def cross_fwd_kernel(nq, lo_ref, count_ref, q_ref, k_ref, v_ref, doc_ref, aug_ref, mix_ref, pr_ref, kx, vx, sc):
    local = nq * TILE
    across = k_ref.shape[0] // PAIR

    def place_key(at, block):
        for p in range(2):
            kx[p, at, :TILE] = block[:, part(p)]

    def place_value(at, block):
        vx[at, :] = block

    gather_shards(local, k_ref, place_key)
    gather_shards(local, v_ref, place_value)
    for p in range(2):
        kx[p, :, TILE:] = aug_ref[...]
    masks = head_masks()
    lane = iota((TILE, TILE), 1)

    def step(n, _):
        i, p = n // 2, n % 2
        here = pl.multiple_of(i * TILE, TILE)
        lanes = pl.ds(pl.multiple_of(p * TILE, TILE), TILE)
        qs = stack_heads(q_ref, local, here, lanes, masks, doc_ref[pl.ds(here, TILE), :], SCALE)

        def window(w):
            return pl.ds(pl.multiple_of((lo_ref[i] + w) * PAIR, PAIR), PAIR)

        def path(count):
            for w in range(count):
                sc[:, w * PAIR : (w + 1) * PAIR] = dot(qs, kx[p, window(w), :], 1, 1)
            for b in range(2 * STREAMS):
                xs = [sc[part(b), part(m)] for m in range(2 * count)]
                top = xs[0]
                for x in xs[1:]:
                    top = jnp.maximum(top, x)
                top = lane_max(top)
                xs = [jnp.exp(x - top) for x in xs]
                total = xs[0]
                for x in xs[1:]:
                    total = total + x
                inverse = 1.0 / lane_sum(total)
                xs = [(x * inverse).astype(jnp.bfloat16) for x in xs]
                for w in range(count):
                    pr_ref[0, n, part(b), window(w)] = jnp.concatenate(xs[2 * w : 2 * w + 2], axis=1)
            total = None
            for w in range(count):
                o = dot(pr_ref[0, n, :, window(w)], vx[window(w), lanes], 1, 0)
                total = o if total is None else total + o
            for s in range(STREAMS):
                mixed = jnp.where(lane < HEAD_DIM, total[part(2 * s)], total[part(2 * s + 1)])
                mix_ref[stream_rows(s, local, here), lanes] = mixed.astype(jnp.bfloat16)

        for count in range(1, across + 1):
            @pl.when(count_ref[i] == count)
            def _():
                path(count)

        for w in range(across):
            @pl.when((w < lo_ref[i]) | (w >= lo_ref[i] + count_ref[i]))
            def _():
                pr_ref[0, n, :, w * PAIR : (w + 1) * PAIR] = jnp.zeros((ROWS, PAIR), jnp.bfloat16)
        return 0

    lax.fori_loop(0, 2 * nq, step, 0)


def cross_forward(lo, count, q, kv, doc, aug):
    tokens, width = q.shape
    local = tokens // STREAMS
    full = kv.shape[0]
    grid = width // PAIR
    steps = 2 * local // TILE
    return pl.pallas_call(
        functools.partial(cross_fwd_kernel, local // TILE),
        grid_spec=pltpu.PrefetchScalarGridSpec(
            num_scalar_prefetch=2, grid=(grid,),
            in_specs=[columns(tokens, 0), columns(full, 0), columns(full, grid), whole(local, TILE), whole(full, TILE)],
            out_specs=[columns(tokens, 0), weights_spec(steps, full)],
            scratch_shapes=[
                pltpu.VMEM((2, full, PAIR), jnp.bfloat16), pltpu.VMEM((full, PAIR), jnp.bfloat16),
                pltpu.VMEM((ROWS, full), jnp.float32),
            ]),
        out_shape=[jax.ShapeDtypeStruct((tokens, width), jnp.bfloat16), jax.ShapeDtypeStruct((grid, steps, ROWS, full), jnp.bfloat16)],
        compiler_params=pltpu.CompilerParams(vmem_limit_bytes=48 << 20),
        cost_estimate=pl.CostEstimate(flops=15_000_000_000, bytes_accessed=20_000_000, transcendentals=8_000_000),
        name="cross_forward",
    )(lo, count, q, kv, kv, doc, aug)


def cross_bwd_kernel(nq, plan, q_ref, k_ref, v_ref, mix_ref, up_ref, pr_ref, *refs):
    arrays, refs = refs[: plan.many], refs[plan.many :]
    dq_ref, dkv_ref, sums_ref, kx, vx, dp, ds, st, dkt, dvt, dqa = refs[:11]
    g = pl.program_id(0)
    comm = Comm(plan, arrays, sums_ref, refs[11:])

    @pl.when(g == 0)
    def _():
        comm.barrier()

    local = nq * TILE

    def place_key(at, block):
        kx[at, :] = block

    def place_value(at, block):
        vx[at, :] = block

    gather_shards(local, k_ref, place_key)
    gather_shards(local, v_ref, place_value)
    dkt[...] = jnp.zeros_like(dkt)
    dvt[...] = jnp.zeros_like(dvt)
    masks = head_masks()
    lane = iota((TILE, TILE), 1)

    def step(n, _):
        i, p = n // 2, n % 2
        here = pl.multiple_of(i * TILE, TILE)
        lanes = pl.ds(pl.multiple_of(p * TILE, TILE), TILE)
        comm.step(g * 2 * nq + n)
        qs = stack_heads(q_ref, local, here, lanes, masks, None, SCALE)
        ups = stack_heads(up_ref, local, here, lanes, masks)
        qt = qs.T
        upt = ups.T
        for b in range(2 * STREAMS):
            rows = stream_rows(b // 2, local, here)
            st[part(b), :] = lane_sum(ups[part(b)].astype(jnp.float32) * mix_ref[rows, lanes].astype(jnp.float32))
        dqa[...] = jnp.zeros_like(dqa)

        def window(w, _):
            at = pl.ds(pl.multiple_of(w * PAIR, PAIR), PAIR)
            dp[...] = dot(ups, vx[at, lanes], 1, 1)
            for b in range(2 * STREAMS):
                x = pr_ref[0, n, part(b), at].astype(jnp.float32)
                for m in range(2):
                    ds[part(b), part(m)] = (x[:, part(m)] * (dp[part(b), part(m)] - st[part(b), :])).astype(jnp.bfloat16)
            dkt[p, :, at] += dot(qt, ds[...], 1, 0)
            dvt[p, :, at] += dot(upt, pr_ref[0, n, :, at], 1, 0)
            dqa[...] += dot(ds[...], kx[at, lanes], 1, 0)
            return 0

        lax.fori_loop(0, k_ref.shape[0] // PAIR, window, 0)
        for s in range(STREAMS):
            dq = jnp.where(lane < HEAD_DIM, dqa[part(2 * s), :], dqa[part(2 * s + 1), :])
            dq_ref[stream_rows(s, local, here), lanes] = (SCALE * dq).astype(jnp.bfloat16)
        return 0

    lax.fori_loop(0, 2 * nq, step, 0)
    third = q_ref.shape[1] * pl.num_programs(0)
    shards = k_ref.shape[0] // local
    z = lax.axis_index("seq")
    for p in range(2):
        for j, acc in enumerate((dkt, dvt)):
            col = pl.multiple_of(g * PAIR + p * TILE + third * j, TILE)
            for k in range(shards):
                at = pl.ds(pl.multiple_of(lax.rem(z - k + shards, shards) * local, TILE), local)
                dkv_ref[k * local : (k + 1) * local, pl.ds(col, TILE)] = acc[p, :, at].T.astype(jnp.bfloat16)

    @pl.when(g == pl.num_programs(0) - 1)
    def _():
        comm.rest(4 * 2 * nq)


def cross_backward(plan, arrays, q, kv, mix, up, weights):
    tokens, width = q.shape
    local = tokens // STREAMS
    full = kv.shape[0]
    grid = width // PAIR
    steps = 2 * local // TILE
    return pl.pallas_call(
        functools.partial(cross_bwd_kernel, local // TILE, plan),
        grid=(grid,),
        in_specs=[
            columns(tokens, 0), columns(full, 0), columns(full, grid),
            columns(tokens, 0), columns(tokens, 0), weights_spec(steps, full),
        ] + plan.in_specs(),
        out_specs=[columns(tokens, 0), whole(full, 2 * width), plan.out_spec()],
        scratch_shapes=[
            pltpu.VMEM((full, PAIR), jnp.bfloat16), pltpu.VMEM((full, PAIR), jnp.bfloat16),
            pltpu.VMEM((ROWS, PAIR), jnp.float32), pltpu.VMEM((ROWS, PAIR), jnp.bfloat16),
            pltpu.VMEM((ROWS, TILE), jnp.float32),
            pltpu.VMEM((2, TILE, full), jnp.float32), pltpu.VMEM((2, TILE, full), jnp.float32),
            pltpu.VMEM((ROWS, TILE), jnp.float32),
        ] + plan.scratch(),
        out_shape=[
            jax.ShapeDtypeStruct((tokens, width), jnp.bfloat16), jax.ShapeDtypeStruct((full, 2 * width), jnp.bfloat16),
            plan.out_shape(),
        ],
        compiler_params=pltpu.CompilerParams(collective_id=plan.number, has_side_effects=True, vmem_limit_bytes=58 << 20),
        cost_estimate=pl.CostEstimate(flops=40_000_000_000, bytes_accessed=30_000_000, transcendentals=8_000_000),
        name="cross_backward",
    )(q, kv, kv, mix, up, weights, *plan.views(arrays))


CHUNK = 256
SLOTS = 8


class Route:
    def __init__(self, dp, seq):
        self.dp_bits = dp.bit_length() - 1
        self.bits = self.dp_bits + seq.bit_length() - 1
        core = self.dp_bits - 1
        rest = list(reversed(range(core)))
        tail = list(reversed(range(self.dp_bits, self.bits)))
        self.orders = ([core] + rest + tail, [core] + rest[::-1] + tail)
        steps = self.bits
        self.lags = [0, 1] + [min(1 + 2 * k, 5) + max(0, k - 2) for k in range(1, steps)]

    def place(self, bit):
        if bit < self.dp_bits:
            return "dp", self.dp_bits - 1 - bit
        return "seq", self.bits - 1 - bit

    def mine(self, bit):
        axis, k = self.place(bit)
        return lax.rem(lax.axis_index(axis) // (1 << k), 2)

    def partner(self, bit):
        axis, k = self.place(bit)
        index = lax.axis_index(axis)
        return {axis: index + (1 - 2 * self.mine(bit)) * (1 << k)}

    def left(self, kind, k):
        return sorted(set(range(self.bits)) - set(self.orders[kind][:k]))


class Plan:
    def __init__(self, route, shapes, number, chunk=CHUNK, kind=jnp.bfloat16):
        self.route, self.number, self.chunk, self.kind = route, number, chunk, kind
        rows = min(shape[0] for shape in shapes)
        self.deep = rows >> route.bits
        self.subs = [shape[0] // rows for shape in shapes]
        self.pairs = [sub * (shape[1] // (2 * chunk)) for sub, shape in zip(self.subs, shapes)]
        self.total, self.many = sum(self.pairs), len(shapes)
        self.iterations = self.total + route.lags[route.bits]

    def views(self, arrays):
        lead = lambda sub: (2,) * self.route.bits + ((sub,) if sub > 1 else ())
        return [a.reshape(lead(sub) + (self.deep, a.shape[1])) for a, sub in zip(arrays, self.subs)]

    def in_specs(self):
        return [pl.BlockSpec(memory_space=pl.ANY)] * self.many

    def out_shape(self):
        return jax.ShapeDtypeStruct((self.deep, self.total * 2 * self.chunk), jnp.float32)

    def out_spec(self):
        return pl.BlockSpec(self.out_shape().shape, lambda *_: (0, 0))

    def scratch(self):
        bits = self.route.bits
        shape = lambda lead: (SLOTS, 2) + (2,) * lead + (self.deep, self.chunk)
        own = [pltpu.VMEM(shape(bits - 1), self.kind)]
        got = [pltpu.VMEM(shape(bits - 1 - k), self.kind) for k in range(bits)]
        out = [pltpu.VMEM(shape(bits - 1 - k), self.kind) for k in range(1, bits)]
        kept = [pltpu.VMEM(shape(bits - 1 - k), jnp.float32) for k in range(1, bits)]
        sems = [pltpu.SemaphoreType.DMA((2, SLOTS))] + [pltpu.SemaphoreType.DMA((bits, 2, SLOTS))] * 2
        return own + got + out + kept + sems

    def blocks(self, sums):
        out, at = [], 0
        for sub, pairs in zip(self.subs, self.pairs):
            span = pairs * 2 * self.chunk
            block = sums[:, at : at + span]
            at += span
            if sub > 1:
                block = block.reshape(-1, sub, span // sub).transpose(1, 0, 2).reshape(-1, span // sub)
            out.append(block)
        return out


class Comm:
    def __init__(self, plan, arrays, result, scratch):
        route = plan.route
        bits = route.bits
        self.plan, self.route, self.arrays, self.result = plan, route, arrays, result
        self.pairs, self.subs, self.chunk, self.total = plan.pairs, plan.subs, plan.chunk, plan.total
        self.own = scratch[0]
        self.got = scratch[1 : 1 + bits]
        self.out = (None,) + tuple(scratch[1 + bits : 2 * bits])
        self.kept = (None,) + tuple(scratch[2 * bits : 3 * bits - 1])
        self.own_sem, self.send_sem, self.got_sem = scratch[3 * bits - 1 : 3 * bits + 2]

    def barrier(self):
        sem = pltpu.get_barrier_semaphore()
        size = 1 << (self.route.bits - self.route.dp_bits)
        others = [self.route.partner(bit) for bit in range(self.route.dp_bits)]
        others += [{"seq": lax.rem(lax.axis_index("seq") + k, size)} for k in range(1, size)]
        for other in others:
            pl.semaphore_signal(sem, inc=1, device_id=other, device_id_type=pl.DeviceIdType.MESH)
        pl.semaphore_wait(sem, len(others))

    def source(self, n, pair, kind, side):
        core = self.route.dp_bits - 1
        ref, subs = self.arrays[n], self.subs[n]
        across = ref.shape[-1] // (2 * self.chunk)
        col = pl.ds(pl.multiple_of(lax.rem(pair, across) * 2 * self.chunk + kind * self.chunk, self.chunk), self.chunk)
        index = [slice(None)] * self.route.bits
        index[core] = side
        if subs > 1:
            index.append(pair // across)
        return ref.at[tuple(index) + (slice(None), col)]

    def copy(self, k, kind, slot, src):
        return pltpu.make_async_remote_copy(
            src_ref=src,
            dst_ref=self.got[k].at[slot, kind],
            send_sem=self.send_sem.at[k, kind, slot],
            recv_sem=self.got_sem.at[k, kind, slot],
            device_id=self.route.partner(self.route.orders[kind][k]),
            device_id_type=pl.DeviceIdType.MESH,
        )

    def fetch(self, kind, slot, src):
        return pltpu.make_async_copy(src, self.own.at[slot, kind], self.own_sem.at[kind, slot])

    def begin(self, u):
        slot = lax.rem(u, SLOTS)
        side = self.route.mine(self.route.dp_bits - 1)
        first = 0
        for n, pairs in enumerate(self.pairs):
            @pl.when((u >= first) & (u < first + pairs))
            def _():
                for kind in range(2):
                    self.copy(0, kind, slot, self.source(n, u - first, kind, 1 - side)).start()
                    self.fetch(kind, slot, self.source(n, u - first, kind, side)).start()

            first += pairs

    def advance(self, k, u):
        route = self.route
        slot = lax.rem(u, SLOTS)
        for kind in range(2):
            if k == 1:
                filler = self.source(0, 0, kind, 0)
                self.fetch(kind, slot, filler).wait()
                self.copy(0, kind, slot, filler).wait()
                held = self.own
            else:
                self.copy(k - 1, kind, slot, self.out[k - 1].at[slot, kind]).wait()
                held = self.kept[k - 1]
            came = self.got[k - 1]
            if k == route.bits:
                total = held[slot, kind].astype(jnp.float32) + came[slot, kind].astype(jnp.float32)
                at = pl.multiple_of((2 * u + kind) * self.chunk, self.chunk)
                self.result[:, pl.ds(at, self.chunk)] = total
                continue
            bit = route.orders[kind][k]
            at = route.left(kind, k).index(bit)
            me = route.mine(bit)
            where = lambda side: (slot, kind) + (slice(None),) * at + (side,)
            theirs = where(1 - me)
            sent = held[theirs].astype(jnp.float32) + came[theirs].astype(jnp.float32)
            self.out[k][slot, kind] = sent.astype(self.out[k].dtype)
            self.copy(k, kind, slot, self.out[k].at[slot, kind]).start()
            ours = where(me)
            self.kept[k][slot, kind] = held[ours].astype(jnp.float32) + came[ours].astype(jnp.float32)

    def step(self, t):
        @pl.when(t < self.total)
        def _():
            self.begin(t)

        for k in range(1, self.route.bits + 1):
            u = t - self.route.lags[k]

            @pl.when((u >= 0) & (u < self.total))
            def _():
                self.advance(k, u)


    def rest(self, begin):
        def body(t, _):
            self.step(t)
            return 0

        lax.fori_loop(begin, self.plan.iterations, body, 0)


class Handing:
    def __init__(self, size, count, wraps, source, target, sems):
        self.size, self.count, self.wraps = size, count, wraps
        self.source, self.target, self.sems = source, target, sems

    def copies(self):
        z = lax.axis_index("seq")
        for k in range(1, self.count + 1):
            copy = pltpu.make_async_remote_copy(
                src_ref=self.source.at[k - 1],
                dst_ref=self.target.at[k - 1],
                send_sem=self.sems.at[0, k - 1],
                recv_sem=self.sems.at[1, k - 1],
                device_id={"seq": lax.rem(z - k + self.size, self.size)},
                device_id_type=pl.DeviceIdType.MESH,
            )
            yield copy, z >= k, z + k < self.size

    def start(self):
        for copy, sends, _ in self.copies():
            if self.wraps:
                copy.start()
            else:
                pl.when(sends)(copy.start)

    def wait(self):
        for copy, sends, gets in self.copies():
            if self.wraps:
                copy.wait()
            else:
                pl.when(sends)(copy.wait_send)
                pl.when(gets)(copy.wait_recv)


def handing_scratch(count):
    return [pltpu.SemaphoreType.DMA((2, count))]


def scatter_kernel(plan, few, size, *refs):
    many = plan.many
    arrays, small, handed = refs[:many], refs[many], refs[many + 1]
    result, small_result, got = refs[many + 2 : many + 5]
    scratch = refs[many + 5 : -1]
    half = len(scratch) // 2
    comm = Comm(plan, arrays, result, scratch[:half])
    other = Comm(few, [small], small_result, scratch[half:])
    hand = Handing(size, handed.shape[0], False, handed, got, refs[-1])
    comm.barrier()
    hand.start()

    def body(t, _):
        other.step(t)
        comm.step(t)
        return 0

    lax.fori_loop(0, plan.iterations, body, 0)
    hand.wait()


def scatter_sums(plan, few, size, arrays, small, handed):
    anywhere = pl.BlockSpec(memory_space=pl.ANY)
    return pl.pallas_call(
        functools.partial(scatter_kernel, plan, few, size),
        grid=(1,),
        in_specs=plan.in_specs() + few.in_specs() + [anywhere],
        out_specs=[plan.out_spec(), few.out_spec(), anywhere],
        out_shape=[plan.out_shape(), few.out_shape(), jax.ShapeDtypeStruct(handed.shape, handed.dtype)],
        scratch_shapes=plan.scratch() + few.scratch() + handing_scratch(handed.shape[0]),
        compiler_params=pltpu.CompilerParams(
            collective_id=plan.number, has_side_effects=True, vmem_limit_bytes=56 << 20
        ),
        cost_estimate=pl.CostEstimate(flops=20_000_000_000, bytes_accessed=60_000_000, transcendentals=0),
        name="weight_sums",
    )(*plan.views(arrays), *few.views([small]), handed)


def gelu_parts(x):
    u = jnp.abs(x) * (0.5**0.5)
    t = 1.0 / (1.0 + 0.5 * u)
    poly = jnp.float32(0.17087277)
    for coef in (-0.82215223, 1.48851587, -1.13520398, 0.27886807, -0.18628806, 0.09678418, 0.37409196, 1.00002368, -1.26551223):
        poly = poly * t + coef
    square = u * u
    half = 0.5 * t * jnp.exp(poly - square)
    below = jnp.where(x >= 0, 1.0 - half, half)
    dense = jnp.exp(-square) * (1.0 / math.sqrt(2.0 * math.pi))
    return x * below, below + x * dense


def up_kernel(x_ref, w_ref, b_ref, act_ref, slope_ref):
    rows = x_ref.shape[0]
    step = 256 if rows % 256 == 0 else TILE
    for r in range(0, rows, step):
        pre = dot(x_ref[r : r + step, :], w_ref[...], 1, 0) + b_ref[...]
        value, slope = gelu_parts(pre)
        act_ref[r : r + step, :] = value.astype(jnp.bfloat16)
        slope_ref[r : r + step, :] = slope.astype(jnp.bfloat16)


def up_gelu(x, w, b):
    tokens, width = x.shape
    hidden = w.shape[1]
    block = 512
    out = pl.BlockSpec((tokens, block), lambda j: (0, j))
    return pl.pallas_call(
        up_kernel,
        grid=(hidden // block,),
        in_specs=[
            pl.BlockSpec((tokens, width), lambda j: (0, 0)),
            pl.BlockSpec((width, block), lambda j: (0, j)),
            pl.BlockSpec((1, block), lambda j: (0, j)),
        ],
        out_specs=[out, out],
        out_shape=[jax.ShapeDtypeStruct((tokens, hidden), jnp.bfloat16)] * 2,
        compiler_params=pltpu.CompilerParams(vmem_limit_bytes=40 << 20),
        cost_estimate=pl.CostEstimate(
            flops=2 * tokens * width * hidden * 3, bytes_accessed=22_000_000, transcendentals=6_000_000
        ),
        name="up_gelu",
    )(x, w, b.reshape(1, hidden))


def normalize(hidden, gain, shift):
    centre = hidden - jnp.mean(hidden, axis=-1, keepdims=True)
    scale_inv = lax.rsqrt(jnp.mean(centre * centre, axis=-1, keepdims=True) + 1e-05)
    unit = centre * scale_inv
    return (unit * gain + shift, unit, scale_inv)


def normalize_back(upstream, unit, scale_inv, gain):
    along = upstream * gain
    inner = (
        along
        - jnp.mean(along, axis=-1, keepdims=True)
        - unit * jnp.mean(along * unit, axis=-1, keepdims=True)
    )
    return (scale_inv * inner, jnp.sum(upstream * unit, axis=0), jnp.sum(upstream, axis=0))


def gate(value, *others):
    return lax.optimization_barrier((value,) + others)[0]


def shards(
    inputs,
    encoded,
    target_lengths,
    source_lengths,
    query_key_value,
    bucket_weight,
    self_output,
    cross_query,
    cross_key_value,
    cross_output,
    up_weight,
    up_bias,
    down_weight,
    down_bias,
    norm_gain,
    norm_shift,
    cotangent,
):
    row_count, streams, local, width = inputs.shape
    parts, size = lax.axis_size("dp"), lax.axis_size("seq")
    route = Route(parts, size)
    full = local * size
    z = lax.axis_index("seq")
    begin = z * local
    bf16, f32 = jnp.bfloat16, jnp.float32
    tokens = streams * local
    up_chain = [(i, i + 1) for i in range(size - 1)]
    down_chain = [(i + 1, i) for i in range(size - 1)]

    def mm(left, right):
        return jnp.dot(left, right, preferred_element_type=f32)

    def mm_t(left, right):
        return lax.dot_general(left, right, (((1,), (1,)), ((), ())), preferred_element_type=f32)

    def wgrad(left, right):
        return dot(left, right, 0, 0).astype(bf16)

    flat = inputs.reshape(tokens, width)
    main = flat[:local]
    hops = HALO // local
    passing, pieces = main, []
    for _ in range(hops):
        passing = lax.ppermute(passing, "seq", up_chain)
        pieces.insert(0, passing)
    halo = jnp.concatenate(pieces, axis=0)
    own_source = encoded.reshape(local, width)
    waiting, halo = lax.optimization_barrier((own_source, halo))
    sources = [own_source] + [
        lax.ppermute(waiting, "seq", [(i, (i + k) % size) for i in range(size)]) for k in range(1, size)
    ]
    source = jnp.concatenate(sources, axis=0)

    here = begin + jnp.arange(local, dtype=jnp.int32)
    ends = jnp.cumsum(target_lengths[0])
    source_ends = jnp.cumsum(source_lengths[0])
    passed = here[:, None] >= ends[None, :]
    number = jnp.sum(passed.astype(jnp.int32), axis=1)
    start = jnp.max(jnp.where(passed, ends[None, :], 0), axis=1) - begin + HALO
    is_doc = number[:, None] == jnp.arange(ends.shape[0] + 1, dtype=jnp.int32)[None, :]
    zero = jnp.zeros((1,), jnp.int32)
    first = jnp.sum(jnp.where(is_doc, jnp.concatenate([zero, source_ends])[None, :], 0), axis=1)
    last = jnp.sum(jnp.where(is_doc, jnp.concatenate([source_ends, zero + full])[None, :], 0), axis=1)
    edge = start[::TILE]
    at = HALO + TILE * jnp.arange(local // TILE, dtype=jnp.int32)
    need = 1 + (edge < at - TILE).astype(jnp.int32) + (edge < at - 3 * TILE).astype(jnp.int32)
    low_key = first[::TILE] // PAIR
    count = (last[TILE - 1 :: TILE] + PAIR - 1) // PAIR - low_key

    names = jnp.arange(TILE, dtype=jnp.int32)[None, :]
    place = begin - HALO + jnp.arange(HALO + local, dtype=jnp.int32)
    key_doc = jnp.where(place >= 0, jnp.sum((place[:, None] >= ends[None, :]).astype(jnp.int32), axis=1), TILE)
    place = jnp.arange(full, dtype=jnp.int32)
    source_doc = jnp.sum((place[:, None] >= source_ends[None, :]).astype(jnp.int32), axis=1)
    doc = (number[:, None] == names).astype(bf16)
    block = lambda of: jnp.where((names < 8) & (of[:, None] != names), NEG, 0.0).astype(bf16)
    target_aug, source_aug = block(key_doc), block(source_doc)
    skew, hot = bias_tables()

    query_main = mm(flat, query_key_value).astype(bf16)
    relative = mm(flat, bucket_weight)
    proj = query_main
    halo_kv = mm(halo, query_key_value[:, width:]).astype(bf16)
    self_mix, self_weights = self_forward(need, proj, halo_kv, relative, doc, target_aug, skew)
    hidden_one, unit_one, inv_one = normalize(flat.astype(f32) + mm(self_mix, self_output), norm_gain[0], norm_shift[0])
    low_one = hidden_one.astype(bf16)
    cross_q = mm(low_one, cross_query).astype(bf16)
    source_kv = mm(source, cross_key_value).astype(bf16)
    cross_mix, cross_weights = cross_forward(low_key, count, cross_q, source_kv, doc, source_aug)
    hidden_two, unit_two, inv_two = normalize(hidden_one + mm(cross_mix, cross_output), norm_gain[1], norm_shift[1])
    low_two = hidden_two.astype(bf16)
    activated, slope = up_gelu(low_two, up_weight, up_bias)
    branch_three = mm(activated, down_weight) + down_bias
    result, unit_three, inv_three = normalize(hidden_two + branch_three, norm_gain[2], norm_shift[2])

    three_grad, gain_three, shift_three = normalize_back(
        cotangent.reshape(tokens, width).astype(f32), unit_three, inv_three, norm_gain[2]
    )
    three_low = three_grad.astype(bf16)
    down_bias_grad = jnp.sum(three_grad, axis=0)
    down_part = wgrad(activated, three_low)
    pre_grad = mm_t(three_low, down_weight).astype(bf16).astype(f32) * slope.astype(f32)
    up_bias_grad = jnp.sum(pre_grad, axis=0)
    pre_low = pre_grad.astype(bf16)
    up_part = wgrad(low_two, pre_low)
    hidden_two_grad = three_grad + mm_t(pre_low, up_weight).astype(bf16).astype(f32)
    two_grad, gain_two, shift_two = normalize_back(hidden_two_grad, unit_two, inv_two, norm_gain[1])
    two_low = two_grad.astype(bf16)
    cross_up = mm_t(two_low, cross_output).astype(bf16)
    wide = [up_part, down_part]
    wide_plan = Plan(route, [a.shape for a in wide], 0)
    query_low, source_low, wide_sums = cross_backward(
        wide_plan, wide, cross_q, source_kv, cross_mix, cross_up, cross_weights
    )
    up_grad, down_grad = wide_plan.blocks(wide_sums)
    source_back = mm_t(source_low, cross_key_value)
    back_low = source_back[local:].astype(bf16).reshape(size - 1, local, width)
    hidden_one_grad = two_grad + mm_t(query_low, cross_query).astype(bf16).astype(f32)
    one_grad, gain_one, shift_one = normalize_back(hidden_one_grad, unit_one, inv_one, norm_gain[0])
    one_low = one_grad.astype(bf16)
    self_up = mm_t(one_low, self_output).astype(bf16)
    square = [
        wgrad(source, source_low),
        wgrad(cross_mix, two_low),
        wgrad(low_one, query_low),
        wgrad(self_mix, one_low),
    ]
    square_plan = Plan(route, [a.shape for a in square], 1)
    proj_low, halo_low, table_low, square_sums, came = self_backward(
        square_plan, square, back_low, proj, halo_kv, hot, self_mix, self_up, self_weights
    )
    cross_kv_grad, cross_out_grad, cross_query_grad, self_out_grad = square_plan.blocks(square_sums)
    encoded_grad = source_back[:local] + jnp.sum(came.astype(f32), axis=0)
    halo_back = mm_t(halo_low, query_key_value[:, width:]).astype(bf16)
    handed = halo_back.reshape(hops, local, width)[::-1]
    back = mm_t(proj_low, query_key_value) + mm_t(table_low, bucket_weight)
    devices = parts * size
    gains = jnp.stack([gain_one, gain_two, gain_three]).reshape(3, devices, -1).transpose(1, 0, 2)
    shifts = jnp.stack([shift_one, shift_two, shift_three]).reshape(3, devices, -1).transpose(1, 0, 2)
    each = width // devices
    small = jnp.concatenate(
        [
            up_bias_grad.reshape(devices, -1),
            down_bias_grad.reshape(devices, -1),
            gains.reshape(devices, -1),
            shifts.reshape(devices, -1),
        ],
        axis=1,
    )
    used = small.shape[1]
    small = jnp.pad(small, ((0, 0), (0, 16 * TILE - used))).reshape(devices * 8, 2 * TILE)
    arrays = [
        wgrad(flat, proj_low[:, :width]),
        (dot(flat, proj_low[:, width:], 0, 0) + dot(halo, halo_low, 0, 0)).astype(bf16),
        wgrad(flat, table_low),
    ]
    plan = Plan(route, [a.shape for a in arrays], 2)
    few = Plan(route, [small.shape], 2, TILE, f32)
    sums, small, returned = scatter_sums(plan, few, size, arrays, small, handed)
    back = back.reshape(streams, local, width)
    behind = (jnp.arange(1, hops + 1, dtype=jnp.int32) + z < size)[:, None, None]
    passing = jnp.sum(jnp.where(behind, returned.astype(f32), 0.0), axis=0)
    back = jnp.concatenate([back[:1] + passing[None], back[1:]], axis=0).reshape(tokens, width)
    inputs_grad = one_grad + back.astype(bf16).astype(f32)
    q_grad, kv_grad, bucket_grad = plan.blocks(sums)
    small = small.reshape(-1)
    wide_each = up_bias_grad.shape[0] // devices
    cuts = [wide_each, wide_each + each, wide_each + 4 * each, used]
    up_bias_grad, down_bias_grad, gains, shifts, _ = jnp.split(small, cuts)
    return (
        result.astype(bf16).reshape(inputs.shape),
        inputs_grad.astype(bf16).reshape(inputs.shape),
        encoded_grad.astype(bf16).reshape(encoded.shape),
        jnp.concatenate([q_grad, kv_grad], axis=1),
        bucket_grad,
        self_out_grad,
        cross_query_grad,
        cross_kv_grad,
        cross_out_grad,
        up_grad,
        up_bias_grad,
        down_grad,
        down_bias_grad,
        gains.reshape(3, each),
        shifts.reshape(3, each),
    )


def solution(mesh):
    placed = (
        P("dp", None, "seq", None),
        P("dp", "seq", None),
        P("dp", None),
        P("dp", None),
        P(),
        P(),
        P(),
        P(),
        P(),
        P(),
        P(),
        P(),
        P(),
        P(),
        P(),
        P(),
        P("dp", None, "seq", None),
    )
    return jax.shard_map(
        shards,
        mesh=mesh,
        in_specs=placed,
        out_specs=(
            P("dp", None, "seq", None),
            P("dp", None, "seq", None),
            P("dp", "seq", None),
            P(("dp", "seq"), None),
            P(("dp", "seq"), None),
            P(("dp", "seq"), None),
            P(("dp", "seq"), None),
            P(("dp", "seq"), None),
            P(("dp", "seq"), None),
            P(("dp", "seq"), None),
            P(("dp", "seq")),
            P(("dp", "seq"), None),
            P(("dp", "seq")),
            P(None, ("dp", "seq")),
            P(None, ("dp", "seq")),
        ),
        check_vma=False,
    )
```

```python
import functools
import math

import jax
import jax.numpy as jnp
from jax import lax
from jax.experimental import pallas as pl
from jax.experimental.pallas import tpu as pltpu
from jax.sharding import PartitionSpec as P

HEAD_DIM = 64
BUCKETS = 32
STREAMS = 3
HALO = 512
TILE = 128
PAIR = 2 * TILE
ROWS = 2 * STREAMS * TILE
NEG = -1e30
SCALE = HEAD_DIM ** (-0.5)

bucket_edges = [
    int(math.ceil(16.0 * 8.0 ** (bucket_level / 16.0))) for bucket_level in range(1, 16)
]


def bucket_of(distance):
    forward_gap = jnp.maximum(distance, 0)
    far_bucket = jnp.full_like(forward_gap, 16)
    for bucket_edge in bucket_edges:
        far_bucket = far_bucket + (forward_gap >= bucket_edge).astype(jnp.int32)
    return jnp.where(forward_gap < 16, forward_gap, far_bucket)


def iota(shape, axis):
    return lax.broadcasted_iota(jnp.int32, shape, axis)


def dot(a, b, ca, cb):
    return lax.dot_general(a, b, (((ca,), (cb,)), ((), ())), preferred_element_type=jnp.float32)


def bias_tables():
    col = iota((PAIR, PAIR), 1)
    gap = jnp.where(col < TILE, (TILE - col) % TILE, PAIR)
    row = iota((PAIR, PAIR), 0) % TILE
    back = TILE - 1 - iota((TILE, TILE), 0)
    lane = iota((TILE, TILE), 1)
    skews = [(bucket_of(gap) + BUCKETS * h == row).astype(jnp.bfloat16) for h in range(4)]
    hots = [(bucket_of(back) + BUCKETS * h == lane).astype(jnp.bfloat16) for h in range(4)]
    return jnp.concatenate(skews, axis=0), jnp.concatenate(hots, axis=0)


def halves(a, b, ca, cb):
    half = a.shape[0] // 2
    return jnp.concatenate([dot(a[:half], b, ca, cb), dot(a[half:], b, ca, cb)], axis=0)


def head_masks():
    low = (iota((TILE, TILE), 1) < HEAD_DIM).astype(jnp.float32)
    return low.astype(jnp.bfloat16), (1.0 - low).astype(jnp.bfloat16)


def stream_rows(s, local, here):
    return pl.ds(pl.multiple_of(s * local + here, TILE), TILE)


def stack_heads(ref, local, here, lanes, masks, extra=None, scale=None):
    out = []
    for s in range(STREAMS):
        x = ref[stream_rows(s, local, here), lanes]
        if scale is not None:
            x = x * jnp.bfloat16(scale)
        for mask in masks:
            y = x * mask
            out.append(y if extra is None else jnp.concatenate([y, extra], axis=1))
    return jnp.concatenate(out, axis=0)


def part(n):
    return slice(n * TILE, (n + 1) * TILE)


def lane_max(x):
    return jnp.broadcast_to(jnp.max(x, axis=1, keepdims=True), (TILE, TILE))


def lane_sum(x):
    return jnp.broadcast_to(jnp.sum(x, axis=1, keepdims=True), (TILE, TILE))


def roll_rows(x):
    return pltpu.roll(x, 0, 1, stride=1, stride_axis=0)


REACH = HALO + TILE
FIRST = (3 * TILE, TILE, 0)


def columns(rows, base):
    return pl.BlockSpec((rows, PAIR), lambda g, *_: (0, base + g))


def whole(rows, cols):
    return pl.BlockSpec((rows, cols), lambda g, *_: (0, 0))


def weights_spec(steps, reach):
    return pl.BlockSpec((1, steps, ROWS, reach), lambda g, *_: (g, 0, 0, 0))


def self_fwd_kernel(nq, need_ref, q_ref, ko_ref, vo_ref, kh_ref, vh_ref, rel_ref, doc_ref, aug_ref, skew_ref,
                    mix_ref, pr_ref, kx, vx, sc, st, bz):
    local = nq * TILE
    for p in range(2):
        kx[p, :HALO, :TILE] = kh_ref[:, part(p)]
        kx[p, HALO:, :TILE] = ko_ref[:local, part(p)]
        kx[p, :, TILE:] = aug_ref[...]
    vx[:HALO, :] = vh_ref[...]
    vx[HALO:, :] = vo_ref[:local, :]
    masks = head_masks()
    lane = iota((TILE, TILE), 1)
    row = iota((TILE, TILE), 0)

    def step(n, _):
        i, p = n // 2, n % 2
        here = pl.multiple_of(i * TILE, TILE)
        lanes = pl.ds(pl.multiple_of(p * TILE, TILE), TILE)
        qs = stack_heads(q_ref, local, here, lanes, masks, doc_ref[pl.ds(here, TILE), :], SCALE)
        table = []
        for s in range(STREAMS):
            rel = rel_ref[stream_rows(s, local, here), :]
            high = rel.astype(jnp.bfloat16)
            table.append(jnp.concatenate([high, (rel - high.astype(jnp.float32)).astype(jnp.bfloat16)], axis=1))
        table = jnp.concatenate(table, axis=0)
        for j in range(2):
            bz[j, :, :] = halves(table, skew_ref[pl.ds(pl.multiple_of((2 * p + j) * PAIR, PAIR), PAIR), :], 1, 0)

        def path(count):
            first = FIRST[count - 1]
            keys = pl.ds(pl.multiple_of(here + first, TILE), REACH - first)
            sc[:, first:] = halves(qs, kx[p, keys, :], 1, 1)
            for b in range(2 * STREAMS):
                s, j = b // 2, b % 2
                rows = stream_rows(s, local, here)
                near = roll_rows(bz[j, part(s), :TILE])
                steady = bz[j, part(s), TILE:]
                left = sc[part(b), part(3)] + jnp.where(lane > row, near, steady)
                right = sc[part(b), part(4)]
                if s > 0:
                    own = lane_sum(qs[part(b), :TILE].astype(jnp.float32) * ko_ref[rows, lanes].astype(jnp.float32))
                    right = jnp.where(lane == row, own, right)
                right = right + jnp.where(lane <= row, near, NEG)
                far = [sc[part(b), part(m)] for m in range(first // TILE, 3)]
                top = jnp.maximum(left, right)
                if far:
                    most = far[0]
                    for x in far[1:]:
                        most = jnp.maximum(most, x)
                    top = jnp.maximum(top, most + steady)
                top = lane_max(top)
                base = top - steady
                weights = [jnp.exp(x - base) for x in far] + [jnp.exp(left - top), jnp.exp(right - top)]
                total = weights[0]
                for x in weights[1:]:
                    total = total + x
                inverse = 1.0 / lane_sum(total)
                for m, x in enumerate(weights, first // TILE):
                    x = (x * inverse).astype(jnp.bfloat16)
                    pr_ref[0, n, part(b), part(m)] = x
                    if m == 4 and s > 0:
                        st[part(b), :] = lane_sum(jnp.where(lane == row, x.astype(jnp.float32), 0.0))
            if first:
                pr_ref[0, n, :, :first] = jnp.zeros((ROWS, first), jnp.bfloat16)
            acc = halves(pr_ref[0, n, :, first:], vx[keys, lanes], 1, 0)
            main = vo_ref[stream_rows(0, local, here), lanes].astype(jnp.float32)
            for s in range(STREAMS):
                rows = stream_rows(s, local, here)
                a, b = part(2 * s), part(2 * s + 1)
                mixed = jnp.where(lane < HEAD_DIM, acc[a], acc[b])
                if s > 0:
                    own = jnp.where(lane < HEAD_DIM, st[a, :], st[b, :])
                    mixed = mixed + own * (vo_ref[rows, lanes].astype(jnp.float32) - main)
                mix_ref[rows, lanes] = mixed.astype(jnp.bfloat16)

        for count in range(1, 4):
            @pl.when(need_ref[i] == count)
            def _():
                path(count)
        return 0

    lax.fori_loop(0, 2 * nq, step, 0)


def self_forward(need, proj, halo_kv, rel, doc, aug, skew):
    tokens = proj.shape[0]
    local = tokens // STREAMS
    width = proj.shape[1] // 3
    grid = width // PAIR
    steps = 2 * local // TILE
    return pl.pallas_call(
        functools.partial(self_fwd_kernel, local // TILE),
        grid_spec=pltpu.PrefetchScalarGridSpec(
            num_scalar_prefetch=1, grid=(grid,),
            in_specs=[
                columns(tokens, 0), columns(tokens, grid), columns(tokens, 2 * grid), columns(HALO, 0), columns(HALO, grid),
                pl.BlockSpec((tokens, TILE), lambda g, *_: (0, g)),
                whole(local, TILE), whole(HALO + local, TILE), whole(4 * PAIR, PAIR),
            ],
            out_specs=[columns(tokens, 0), weights_spec(steps, REACH)],
            scratch_shapes=[
                pltpu.VMEM((2, HALO + local, PAIR), jnp.bfloat16), pltpu.VMEM((HALO + local, PAIR), jnp.bfloat16),
                pltpu.VMEM((ROWS, REACH), jnp.float32), pltpu.VMEM((ROWS, TILE), jnp.float32),
                pltpu.VMEM((2, STREAMS * TILE, PAIR), jnp.float32),
            ]),
        out_shape=[jax.ShapeDtypeStruct((tokens, width), jnp.bfloat16),
                   jax.ShapeDtypeStruct((grid, steps, ROWS, REACH), jnp.bfloat16)],
        compiler_params=pltpu.CompilerParams(vmem_limit_bytes=40 << 20),
        cost_estimate=pl.CostEstimate(flops=15_000_000_000, bytes_accessed=20_000_000, transcendentals=8_000_000),
        name="self_forward",
    )(need, proj, proj, proj, halo_kv, halo_kv, rel, doc, aug, skew)


def self_bwd_kernel(nq, plan, shifts, q_ref, ko_ref, vo_ref, kh_ref, vh_ref, hot_ref, mix_ref, up_ref, pr_ref, *refs):
    arrays, handed, refs = refs[: plan.many], refs[plan.many], refs[plan.many + 1 :]
    (dq_ref, dkv_ref, drel_ref, got), refs = refs[:4], refs[4:]
    outs = len(plan.out_shapes())
    results, (kx, vx, dp, ds, cb, st, dkt, dvt, cv), scratch = refs[:outs], refs[outs : outs + 9], refs[outs + 9 :]
    g = pl.program_id(0)
    comm = Comm(plan, arrays, results, scratch[:-1])
    hand = Handing(shifts, 8 * nq, handed, got, scratch[-1])

    @pl.when(g == 0)
    def _():
        comm.barrier()

    local = nq * TILE
    kx[:HALO, :] = kh_ref[...]
    kx[HALO:, :] = ko_ref[:local, :]
    vx[:HALO, :] = vh_ref[...]
    vx[HALO:, :] = vo_ref[:local, :]
    dkt[...] = jnp.zeros_like(dkt)
    dvt[...] = jnp.zeros_like(dvt)
    masks = head_masks()
    lane = iota((TILE, TILE), 1)
    row = iota((TILE, TILE), 0)
    flip = (row + lane == TILE - 1).astype(jnp.float32).astype(jnp.bfloat16)
    gl = pl.multiple_of(g * PAIR, PAIR)
    third = q_ref.shape[1] * pl.num_programs(0)

    def step(n, _):
        i, p = n // 2, n % 2
        here = pl.multiple_of(i * TILE, TILE)
        lanes = pl.ds(pl.multiple_of(p * TILE, TILE), TILE)
        hand.step(g * 2 * nq + n)
        comm.step(g * 2 * nq + n)
        qs = stack_heads(q_ref, local, here, lanes, masks, None, SCALE)
        ups = stack_heads(up_ref, local, here, lanes, masks)
        qt = qs.T
        upt = ups.T

        keys = pl.ds(pl.multiple_of(here, TILE), REACH)
        dp[...] = halves(ups, vx[keys, lanes], 1, 1)
        for b in range(2 * STREAMS):
            s = b // 2
            rows = stream_rows(s, local, here)
            upf = ups[part(b)].astype(jnp.float32)
            centre = lane_sum(upf * mix_ref[rows, lanes].astype(jnp.float32))
            xs = [pr_ref[0, n, part(b), part(m)].astype(jnp.float32) for m in range(5)]
            ys = [(xs[m] * (dp[part(b), part(m)] - centre)).astype(jnp.bfloat16) for m in range(5)]
            for m in range(4):
                ds[part(b), part(m)] = ys[m]
            ys = [y.astype(jnp.float32) for y in ys]
            band = jnp.where(lane > row, ys[3], 0.0)
            st[2, part(b), :] = ys[0] + ys[1] + ys[2] + (ys[3] - band)
            if s > 0:
                own_weight = lane_sum(jnp.where(lane == row, xs[4], 0.0))
                own_grad = own_weight * (lane_sum(upf * vo_ref[rows, lanes].astype(jnp.float32)) - centre)
                own_grad = own_grad.astype(jnp.bfloat16).astype(jnp.float32)
                st[0, part(b), :] = own_weight
                st[1, part(b), :] = own_grad
                band = band + jnp.where(lane == row, own_grad, ys[4])
                ds[part(b), part(4)] = jnp.where(lane == row, 0.0, ys[4]).astype(jnp.bfloat16)
            else:
                band = band + ys[4]
                ds[part(b), part(4)] = ys[4].astype(jnp.bfloat16)
            cb[:, part(b)] = band.astype(jnp.bfloat16)
        dkt[p, :, keys] += dot(qt, ds[...], 1, 0)
        dvt[p, :, keys] += dot(upt, pr_ref[0, n], 1, 0)
        dq = dot(ds[...], kx[keys, lanes], 1, 0)
        turned = dot(flip, cb[...], 1, 0)
        rolled = [roll_rows(turned[:, part(b)]).astype(jnp.bfloat16) for b in range(2 * STREAMS)]
        rolled = jnp.concatenate([jnp.concatenate(rolled[2 * s : 2 * s + 2], axis=1) for s in range(STREAMS)], axis=0)
        table = dot(rolled, hot_ref[pl.ds(pl.multiple_of(p * PAIR, PAIR), PAIR), :], 1, 0).astype(jnp.bfloat16)
        table = dot(flip, jnp.concatenate([table[part(s)] for s in range(STREAMS)], axis=1), 1, 0)

        excess = None
        for s in range(STREAMS):
            rows = stream_rows(s, local, here)
            a, b = part(2 * s), part(2 * s + 1)
            dqs = jnp.where(lane < HEAD_DIM, dq[a], dq[b])
            col = pl.multiple_of(gl + p * TILE, TILE)
            kept = pl.ds(pl.multiple_of(HALO + s * local + here, TILE), TILE)
            if s > 0:
                own_weight = jnp.where(lane < HEAD_DIM, st[0, a, :], st[0, b, :])
                own_grad = jnp.where(lane < HEAD_DIM, st[1, a, :], st[1, b, :])
                dqs = dqs + own_grad * ko_ref[rows, lanes].astype(jnp.float32)
                own_value = own_weight * up_ref[rows, lanes].astype(jnp.float32)
                excess = own_value if excess is None else excess + own_value
                dkv_ref[kept, pl.ds(col, TILE)] = (
                    own_grad * (SCALE * q_ref[rows, lanes].astype(jnp.float32))
                ).astype(jnp.bfloat16)
                dkv_ref[kept, pl.ds(pl.multiple_of(col + third, TILE), TILE)] = own_value.astype(jnp.bfloat16)
            dq_ref[rows, lanes] = (SCALE * dqs).astype(jnp.bfloat16)
            dr = table[:, part(s)]
            for j, blk in enumerate((a, b)):
                dr = dr + jnp.where(lane == BUCKETS * (2 * p + j) + BUCKETS - 1, lane_sum(st[2, blk, :]), 0.0)

            @pl.when(p == 0)
            def _():
                drel_ref[rows, :] = dr.astype(jnp.bfloat16)

            @pl.when(p == 1)
            def _():
                drel_ref[rows, :] = (drel_ref[rows, :].astype(jnp.float32) + dr).astype(jnp.bfloat16)
        cv[pl.ds(here, TILE), lanes] = excess
        return 0

    lax.fori_loop(0, 2 * nq, step, 0)
    for p in range(2):
        for j, acc in enumerate((dkt, dvt)):
            col = pl.multiple_of(gl + p * TILE + third * j, TILE)
            full = acc[p, :, :].T
            main = full[HALO:] if j == 0 else full[HALO:] - cv[:, part(p)]
            dkv_ref[:HALO, pl.ds(col, TILE)] = full[:HALO].astype(jnp.bfloat16)
            dkv_ref[HALO : HALO + local, pl.ds(col, TILE)] = main.astype(jnp.bfloat16)

    @pl.when(g == pl.num_programs(0) - 1)
    def _():
        hand.step(4 * 2 * nq)
        comm.rest(4 * 2 * nq)


def self_backward(plan, arrays, shifts, handed, proj, halo_kv, hot, mix, up, weights):
    tokens = proj.shape[0]
    local = tokens // STREAMS
    width = proj.shape[1] // 3
    grid = width // PAIR
    steps = 2 * local // TILE
    return pl.pallas_call(
        functools.partial(self_bwd_kernel, local // TILE, plan, shifts),
        grid=(grid,),
        in_specs=[
            columns(tokens, 0), columns(tokens, grid), columns(tokens, 2 * grid), columns(HALO, 0), columns(HALO, grid),
            whole(4 * TILE, TILE), columns(tokens, 0), columns(tokens, 0), weights_spec(steps, REACH),
        ] + plan.in_specs() + [pl.BlockSpec(memory_space=pl.ANY)],
        out_specs=[
            columns(tokens, 0), whole(HALO + tokens, 2 * width), pl.BlockSpec((tokens, TILE), lambda g, *_: (0, g)),
            pl.BlockSpec(memory_space=pl.ANY),
        ] + plan.out_specs(),
        scratch_shapes=[
            pltpu.VMEM((HALO + local, PAIR), jnp.bfloat16), pltpu.VMEM((HALO + local, PAIR), jnp.bfloat16),
            pltpu.VMEM((ROWS, REACH), jnp.float32), pltpu.VMEM((ROWS, REACH), jnp.bfloat16),
            pltpu.VMEM((TILE, ROWS), jnp.bfloat16), pltpu.VMEM((3, ROWS, TILE), jnp.float32),
            pltpu.VMEM((2, TILE, HALO + local), jnp.float32), pltpu.VMEM((2, TILE, HALO + local), jnp.float32),
            pltpu.VMEM((local, PAIR), jnp.float32),
        ] + plan.scratch() + handing_scratch(len(shifts), 8 * local // TILE),
        out_shape=[
            jax.ShapeDtypeStruct((tokens, width), jnp.bfloat16), jax.ShapeDtypeStruct((HALO + tokens, 2 * width), jnp.bfloat16),
            jax.ShapeDtypeStruct((tokens, width // 2), jnp.bfloat16), jax.ShapeDtypeStruct(handed.shape, handed.dtype),
        ] + plan.out_shapes(),
        compiler_params=pltpu.CompilerParams(collective_id=plan.number, has_side_effects=True, vmem_limit_bytes=56 << 20),
        cost_estimate=pl.CostEstimate(flops=40_000_000_000, bytes_accessed=30_000_000, transcendentals=8_000_000),
        name="self_backward",
    )(proj, proj, proj, halo_kv, halo_kv, hot, mix, up, weights, *plan.views(arrays), handed)


def gather_shards(local, ref, place):
    shards = ref.shape[0] // local
    z = lax.axis_index("seq")
    for k in range(shards):
        at = pl.ds(pl.multiple_of(lax.rem(z - k + shards, shards) * local, TILE), local)
        place(at, ref[k * local : (k + 1) * local, :])


def cross_fwd_kernel(nq, lo_ref, count_ref, q_ref, k_ref, v_ref, doc_ref, aug_ref, mix_ref, pr_ref, kx, vx, sc):
    local = nq * TILE
    across = k_ref.shape[0] // PAIR

    def place_key(at, block):
        for p in range(2):
            kx[p, at, :TILE] = block[:, part(p)]

    def place_value(at, block):
        vx[at, :] = block

    gather_shards(local, k_ref, place_key)
    gather_shards(local, v_ref, place_value)
    for p in range(2):
        kx[p, :, TILE:] = aug_ref[...]
    masks = head_masks()
    lane = iota((TILE, TILE), 1)

    def step(n, _):
        i, p = n // 2, n % 2
        here = pl.multiple_of(i * TILE, TILE)
        lanes = pl.ds(pl.multiple_of(p * TILE, TILE), TILE)
        qs = stack_heads(q_ref, local, here, lanes, masks, doc_ref[pl.ds(here, TILE), :], SCALE)

        def window(w):
            return pl.ds(pl.multiple_of((lo_ref[i] + w) * PAIR, PAIR), PAIR)

        def path(count):
            keys = pl.ds(pl.multiple_of(lo_ref[i] * PAIR, PAIR), count * PAIR)
            sc[:, : count * PAIR] = halves(qs, kx[p, keys, :], 1, 1)
            for b in range(2 * STREAMS):
                xs = [sc[part(b), part(m)] for m in range(2 * count)]
                top = xs[0]
                for x in xs[1:]:
                    top = jnp.maximum(top, x)
                top = lane_max(top)
                xs = [jnp.exp(x - top) for x in xs]
                total = xs[0]
                for x in xs[1:]:
                    total = total + x
                inverse = 1.0 / lane_sum(total)
                xs = [(x * inverse).astype(jnp.bfloat16) for x in xs]
                for w in range(count):
                    pr_ref[0, n, part(b), window(w)] = jnp.concatenate(xs[2 * w : 2 * w + 2], axis=1)
            total = halves(pr_ref[0, n, :, keys], vx[keys, lanes], 1, 0)
            for s in range(STREAMS):
                mixed = jnp.where(lane < HEAD_DIM, total[part(2 * s)], total[part(2 * s + 1)])
                mix_ref[stream_rows(s, local, here), lanes] = mixed.astype(jnp.bfloat16)

        for count in range(1, across + 1):
            @pl.when(count_ref[i] == count)
            def _():
                path(count)

        for w in range(across):
            @pl.when((w < lo_ref[i]) | (w >= lo_ref[i] + count_ref[i]))
            def _():
                pr_ref[0, n, :, w * PAIR : (w + 1) * PAIR] = jnp.zeros((ROWS, PAIR), jnp.bfloat16)
        return 0

    lax.fori_loop(0, 2 * nq, step, 0)


def cross_forward(lo, count, q, kv, doc, aug):
    tokens, width = q.shape
    local = tokens // STREAMS
    full = kv.shape[0]
    grid = width // PAIR
    steps = 2 * local // TILE
    return pl.pallas_call(
        functools.partial(cross_fwd_kernel, local // TILE),
        grid_spec=pltpu.PrefetchScalarGridSpec(
            num_scalar_prefetch=2, grid=(grid,),
            in_specs=[columns(tokens, 0), columns(full, 0), columns(full, grid), whole(local, TILE), whole(full, TILE)],
            out_specs=[columns(tokens, 0), weights_spec(steps, full)],
            scratch_shapes=[
                pltpu.VMEM((2, full, PAIR), jnp.bfloat16), pltpu.VMEM((full, PAIR), jnp.bfloat16),
                pltpu.VMEM((ROWS, full), jnp.float32),
            ]),
        out_shape=[jax.ShapeDtypeStruct((tokens, width), jnp.bfloat16), jax.ShapeDtypeStruct((grid, steps, ROWS, full), jnp.bfloat16)],
        compiler_params=pltpu.CompilerParams(vmem_limit_bytes=48 << 20),
        cost_estimate=pl.CostEstimate(flops=15_000_000_000, bytes_accessed=20_000_000, transcendentals=8_000_000),
        name="cross_forward",
    )(lo, count, q, kv, kv, doc, aug)


def cross_bwd_kernel(nq, plan, q_ref, k_ref, v_ref, mix_ref, up_ref, pr_ref, *refs):
    arrays, (dq_ref, dkv_ref), refs = refs[: plan.many], refs[plan.many : plan.many + 2], refs[plan.many + 2 :]
    outs = len(plan.out_shapes())
    results, (kx, vx, dp, ds, st, dkt, dvt), scratch = refs[:outs], refs[outs : outs + 7], refs[outs + 7 :]
    g = pl.program_id(0)
    comm = Comm(plan, arrays, results, scratch)

    @pl.when(g == 0)
    def _():
        comm.barrier()

    local = nq * TILE

    def place_key(at, block):
        kx[at, :] = block

    def place_value(at, block):
        vx[at, :] = block

    gather_shards(local, k_ref, place_key)
    gather_shards(local, v_ref, place_value)
    dkt[...] = jnp.zeros_like(dkt)
    dvt[...] = jnp.zeros_like(dvt)
    masks = head_masks()
    lane = iota((TILE, TILE), 1)

    def step(n, _):
        i, p = n // 2, n % 2
        here = pl.multiple_of(i * TILE, TILE)
        lanes = pl.ds(pl.multiple_of(p * TILE, TILE), TILE)
        comm.step(g * 2 * nq + n)
        qs = stack_heads(q_ref, local, here, lanes, masks, None, SCALE)
        ups = stack_heads(up_ref, local, here, lanes, masks)
        qt = qs.T
        upt = ups.T
        for b in range(2 * STREAMS):
            rows = stream_rows(b // 2, local, here)
            st[part(b), :] = lane_sum(ups[part(b)].astype(jnp.float32) * mix_ref[rows, lanes].astype(jnp.float32))
        dp[...] = halves(ups, vx[:, lanes], 1, 1)
        for b in range(2 * STREAMS):
            for m in range(dp.shape[1] // TILE):
                x = pr_ref[0, n, part(b), part(m)].astype(jnp.float32)
                ds[part(b), part(m)] = (x * (dp[part(b), part(m)] - st[part(b), :])).astype(jnp.bfloat16)
        dkt[p, :, :] += dot(qt, ds[...], 1, 0)
        dvt[p, :, :] += dot(upt, pr_ref[0, n], 1, 0)
        dqa = dot(ds[...], kx[:, lanes], 1, 0)
        for s in range(STREAMS):
            dq = jnp.where(lane < HEAD_DIM, dqa[part(2 * s)], dqa[part(2 * s + 1)])
            dq_ref[stream_rows(s, local, here), lanes] = (SCALE * dq).astype(jnp.bfloat16)
        return 0

    lax.fori_loop(0, 2 * nq, step, 0)
    third = q_ref.shape[1] * pl.num_programs(0)
    shards = k_ref.shape[0] // local
    z = lax.axis_index("seq")
    for p in range(2):
        for j, acc in enumerate((dkt, dvt)):
            col = pl.multiple_of(g * PAIR + p * TILE + third * j, TILE)
            for k in range(shards):
                at = pl.ds(pl.multiple_of(lax.rem(z - k + shards, shards) * local, TILE), local)
                dkv_ref[k * local : (k + 1) * local, pl.ds(col, TILE)] = acc[p, :, at].T.astype(jnp.bfloat16)

    @pl.when(g == pl.num_programs(0) - 1)
    def _():
        comm.rest(4 * 2 * nq)


def cross_backward(plan, arrays, q, kv, mix, up, weights):
    tokens, width = q.shape
    local = tokens // STREAMS
    full = kv.shape[0]
    grid = width // PAIR
    steps = 2 * local // TILE
    return pl.pallas_call(
        functools.partial(cross_bwd_kernel, local // TILE, plan),
        grid=(grid,),
        in_specs=[
            columns(tokens, 0), columns(full, 0), columns(full, grid),
            columns(tokens, 0), columns(tokens, 0), weights_spec(steps, full),
        ] + plan.in_specs(),
        out_specs=[columns(tokens, 0), whole(full, 2 * width)] + plan.out_specs(),
        scratch_shapes=[
            pltpu.VMEM((full, PAIR), jnp.bfloat16), pltpu.VMEM((full, PAIR), jnp.bfloat16),
            pltpu.VMEM((ROWS, full), jnp.float32), pltpu.VMEM((ROWS, full), jnp.bfloat16),
            pltpu.VMEM((ROWS, TILE), jnp.float32),
            pltpu.VMEM((2, TILE, full), jnp.float32), pltpu.VMEM((2, TILE, full), jnp.float32),
        ] + plan.scratch(),
        out_shape=[
            jax.ShapeDtypeStruct((tokens, width), jnp.bfloat16), jax.ShapeDtypeStruct((full, 2 * width), jnp.bfloat16),
        ] + plan.out_shapes(),
        compiler_params=pltpu.CompilerParams(collective_id=plan.number, has_side_effects=True, vmem_limit_bytes=58 << 20),
        cost_estimate=pl.CostEstimate(flops=40_000_000_000, bytes_accessed=30_000_000, transcendentals=8_000_000),
        name="cross_backward",
    )(q, kv, kv, mix, up, weights, *plan.views(arrays))


CHUNK = 256
SLOTS = 8


class Route:
    def __init__(self, dp, seq):
        self.dp_bits = dp.bit_length() - 1
        self.bits = self.dp_bits + seq.bit_length() - 1
        core = self.dp_bits - 1
        rest = list(reversed(range(core)))
        tail = list(reversed(range(self.dp_bits, self.bits)))
        self.orders = ([core] + rest + tail, [core] + rest[::-1] + tail)
        steps = self.bits
        self.lags = [0, 1] + [min(1 + 2 * k, 5) + max(0, k - 2) for k in range(1, steps)]

    def place(self, bit):
        if bit < self.dp_bits:
            return "dp", self.dp_bits - 1 - bit
        return "seq", self.bits - 1 - bit

    def mine(self, bit):
        axis, k = self.place(bit)
        return lax.rem(lax.axis_index(axis) // (1 << k), 2)

    def partner(self, bit):
        axis, k = self.place(bit)
        index = lax.axis_index(axis)
        return {axis: index + (1 - 2 * self.mine(bit)) * (1 << k)}

    def left(self, kind, k):
        return sorted(set(range(self.bits)) - set(self.orders[kind][:k]))


class Plan:
    def __init__(self, route, shapes, number, outs=None, chunk=CHUNK, kind=jnp.bfloat16):
        self.route, self.number, self.chunk, self.kind = route, number, chunk, kind
        self.outs = outs or [(n, 0) for n in range(len(shapes))]
        rows = min(shape[0] for shape in shapes)
        self.deep = rows >> route.bits
        self.subs = [shape[0] // rows for shape in shapes]
        self.pairs = [sub * (shape[1] // (2 * chunk)) for sub, shape in zip(self.subs, shapes)]
        self.total, self.many = sum(self.pairs), len(shapes)
        self.iterations = self.total + route.lags[route.bits]

    def views(self, arrays):
        lead = lambda sub: (2,) * self.route.bits + ((sub,) if sub > 1 else ())
        return [a.reshape(lead(sub) + (self.deep, a.shape[1])) for a, sub in zip(arrays, self.subs)]

    def in_specs(self):
        return [pl.BlockSpec(memory_space=pl.ANY)] * self.many

    def out_shapes(self):
        shapes = {}
        for (out, first), sub, pairs in zip(self.outs, self.subs, self.pairs):
            columns = first + pairs * 2 * self.chunk // sub
            shapes[out] = (sub * self.deep, max(columns, shapes.get(out, (0, 0))[1]))
        return [jax.ShapeDtypeStruct(shapes[out], jnp.float32) for out in sorted(shapes)]

    def out_specs(self):
        return [pl.BlockSpec(shape.shape, lambda *_: (0, 0)) for shape in self.out_shapes()]

    def scratch(self):
        bits = self.route.bits
        shape = lambda lead: (SLOTS, 2) + (2,) * lead + (self.deep, self.chunk)
        own = [pltpu.VMEM(shape(bits - 1), self.kind)]
        got = [pltpu.VMEM(shape(bits - 1 - k), self.kind) for k in range(bits)]
        out = [pltpu.VMEM(shape(bits - 1 - k), self.kind) for k in range(1, bits)]
        kept = [pltpu.VMEM(shape(bits - 1 - k), jnp.float32) for k in range(1, bits)]
        sems = [pltpu.SemaphoreType.DMA((2, SLOTS))] + [pltpu.SemaphoreType.DMA((bits, 2, SLOTS))] * 2
        return own + got + out + kept + sems


class Comm:
    def __init__(self, plan, arrays, results, scratch):
        route = plan.route
        bits = route.bits
        self.plan, self.route, self.arrays, self.results = plan, route, arrays, results
        self.pairs, self.subs, self.chunk, self.total = plan.pairs, plan.subs, plan.chunk, plan.total
        self.own = scratch[0]
        self.got = scratch[1 : 1 + bits]
        self.out = (None,) + tuple(scratch[1 + bits : 2 * bits])
        self.kept = (None,) + tuple(scratch[2 * bits : 3 * bits - 1])
        self.own_sem, self.send_sem, self.got_sem = scratch[3 * bits - 1 : 3 * bits + 2]

    def barrier(self):
        sem = pltpu.get_barrier_semaphore()
        size = 1 << (self.route.bits - self.route.dp_bits)
        others = [self.route.partner(bit) for bit in range(self.route.dp_bits)]
        others += [{"seq": lax.rem(lax.axis_index("seq") + k, size)} for k in range(1, size)]
        for other in others:
            pl.semaphore_signal(sem, inc=1, device_id=other, device_id_type=pl.DeviceIdType.MESH)
        pl.semaphore_wait(sem, len(others))

    def source(self, n, pair, kind, side):
        core = self.route.dp_bits - 1
        ref, subs = self.arrays[n], self.subs[n]
        across = ref.shape[-1] // (2 * self.chunk)
        col = pl.ds(pl.multiple_of(lax.rem(pair, across) * 2 * self.chunk + kind * self.chunk, self.chunk), self.chunk)
        index = [slice(None)] * self.route.bits
        index[core] = side
        if subs > 1:
            index.append(pair // across)
        return ref.at[tuple(index) + (slice(None), col)]

    def copy(self, k, kind, slot, src):
        return pltpu.make_async_remote_copy(
            src_ref=src,
            dst_ref=self.got[k].at[slot, kind],
            send_sem=self.send_sem.at[k, kind, slot],
            recv_sem=self.got_sem.at[k, kind, slot],
            device_id=self.route.partner(self.route.orders[kind][k]),
            device_id_type=pl.DeviceIdType.MESH,
        )

    def fetch(self, kind, slot, src):
        return pltpu.make_async_copy(src, self.own.at[slot, kind], self.own_sem.at[kind, slot])

    def begin(self, u):
        slot = lax.rem(u, SLOTS)
        side = self.route.mine(self.route.dp_bits - 1)
        first = 0
        for n, pairs in enumerate(self.pairs):
            @pl.when((u >= first) & (u < first + pairs))
            def _():
                for kind in range(2):
                    self.copy(0, kind, slot, self.source(n, u - first, kind, 1 - side)).start()
                    self.fetch(kind, slot, self.source(n, u - first, kind, side)).start()

            first += pairs

    def advance(self, k, u):
        route = self.route
        slot = lax.rem(u, SLOTS)
        for kind in range(2):
            if k == 1:
                filler = self.source(0, 0, kind, 0)
                self.fetch(kind, slot, filler).wait()
                self.copy(0, kind, slot, filler).wait()
                held = self.own
            else:
                self.copy(k - 1, kind, slot, self.out[k - 1].at[slot, kind]).wait()
                held = self.kept[k - 1]
            came = self.got[k - 1]
            if k == route.bits:
                total = held[slot, kind].astype(jnp.float32) + came[slot, kind].astype(jnp.float32)
                self.store(u, kind, total)
                continue
            bit = route.orders[kind][k]
            at = route.left(kind, k).index(bit)
            me = route.mine(bit)
            where = lambda side: (slot, kind) + (slice(None),) * at + (side,)
            theirs = where(1 - me)
            sent = held[theirs].astype(jnp.float32) + came[theirs].astype(jnp.float32)
            self.out[k][slot, kind] = sent.astype(self.out[k].dtype)
            self.copy(k, kind, slot, self.out[k].at[slot, kind]).start()
            ours = where(me)
            self.kept[k][slot, kind] = held[ours].astype(jnp.float32) + came[ours].astype(jnp.float32)

    def store(self, u, kind, value):
        first, deep = 0, self.plan.deep
        for n, pairs in enumerate(self.pairs):
            out, column = self.plan.outs[n]
            across = pairs // self.subs[n]

            @pl.when((u >= first) & (u < first + pairs))
            def _():
                pair = u - first
                at = pl.multiple_of(column + (2 * lax.rem(pair, across) + kind) * self.chunk, self.chunk)
                rows = pl.ds(pl.multiple_of(pair // across * deep, deep), deep)
                self.results[out][rows, pl.ds(at, self.chunk)] = value

            first += pairs

    def step(self, t):
        @pl.when(t < self.total)
        def _():
            self.begin(t)

        for k in range(1, self.route.bits + 1):
            u = t - self.route.lags[k]

            @pl.when((u >= 0) & (u < self.total))
            def _():
                self.advance(k, u)


    def rest(self, begin):
        def body(t, _):
            self.step(t)
            return 0

        lax.fori_loop(begin, self.plan.iterations, body, 0)


class Handing:
    def __init__(self, shifts, pieces, source, target, sems):
        self.shifts, self.pieces = shifts, pieces
        self.source, self.target, self.sems = source, target, sems

    def copies(self, piece):
        z, size = lax.axis_index("seq"), lax.axis_size("seq")
        deep = self.source.shape[1] // self.pieces
        rows = pl.ds(pl.multiple_of(piece * deep, deep), deep)
        for n, shift in enumerate(self.shifts):
            yield pltpu.make_async_remote_copy(
                src_ref=self.source.at[n, rows],
                dst_ref=self.target.at[n, rows],
                send_sem=self.sems.at[0, n, piece],
                recv_sem=self.sems.at[1, n, piece],
                device_id={"seq": lax.rem(z - shift + size, size)},
                device_id_type=pl.DeviceIdType.MESH,
            )

    def step(self, t):
        @pl.when((t > 0) & (t <= self.pieces))
        def _():
            for copy in self.copies(t - 1):
                copy.wait()

        @pl.when(t < self.pieces)
        def _():
            for copy in self.copies(t):
                copy.start()


def handing_scratch(count, pieces):
    return [pltpu.SemaphoreType.DMA((2, count, pieces))]


def scatter_kernel(plan, few, shifts, *refs):
    many, outs = plan.many, len(plan.out_shapes())
    arrays, small, handed = refs[:many], refs[many], refs[many + 1]
    results, small_result, got = refs[many + 2 : many + 2 + outs], refs[many + 2 + outs], refs[many + 3 + outs]
    scratch = refs[many + 4 + outs : -1]
    half = len(scratch) // 2
    comm = Comm(plan, arrays, results, scratch[:half])
    other = Comm(few, [small], [small_result], scratch[half:])
    hand = Handing(shifts, 8, handed, got, refs[-1])
    comm.barrier()

    def body(t, _):
        hand.step(t)
        other.step(t)
        comm.step(t)
        return 0

    lax.fori_loop(0, plan.iterations, body, 0)


def scatter_sums(plan, few, shifts, arrays, small, handed):
    anywhere = pl.BlockSpec(memory_space=pl.ANY)
    return pl.pallas_call(
        functools.partial(scatter_kernel, plan, few, shifts),
        grid=(1,),
        in_specs=plan.in_specs() + few.in_specs() + [anywhere],
        out_specs=plan.out_specs() + few.out_specs() + [anywhere],
        out_shape=plan.out_shapes() + few.out_shapes() + [jax.ShapeDtypeStruct(handed.shape, handed.dtype)],
        scratch_shapes=plan.scratch() + few.scratch() + handing_scratch(len(shifts), 8),
        compiler_params=pltpu.CompilerParams(
            collective_id=plan.number, has_side_effects=True, vmem_limit_bytes=56 << 20
        ),
        cost_estimate=pl.CostEstimate(flops=20_000_000_000, bytes_accessed=60_000_000, transcendentals=0),
        name="weight_sums",
    )(*plan.views(arrays), *few.views([small]), handed)


def gelu_parts(x):
    t = 1.0 / (1.0 + jnp.abs(x) * (0.43 * 0.5**0.5))
    poly = jnp.float32(0.5 * 0.0709100743822703)
    for coef in (
        -0.2990317761502629, 0.3647352526676159, -0.06881910419857572, 0.23820862557883588,
        0.2074695458910066, 0.24398848761768033, 0.2425387164715943,
    ):
        poly = poly * t + 0.5 * coef
    bell = jnp.exp(x * x * -0.5)
    half = poly * t * bell
    below = jnp.where(x >= 0, 1.0 - half, half)
    return x * below, below + x * (bell * (1.0 / math.sqrt(2.0 * math.pi)))


def row_mean(x):
    return jnp.mean(x, axis=1, keepdims=True)


def column_sum(x):
    return jnp.sum(x, axis=0, keepdims=True)


def norm_back(upstream, unit, scale_inv, gain):
    along = upstream * gain
    return scale_inv * (along - row_mean(along) - unit * row_mean(along * unit))


def row_blocks(rows):
    return [slice(r, r + TILE) for r in range(0, rows, TILE)]


def mlp_fwd_kernel(x_ref, wu_ref, bu_ref, wd_ref, bd_ref, hidden_ref, gain_ref, shift_ref, cot_ref,
                   act_ref, slope_ref, result_ref, grad_ref, low_ref, sums_ref, acc):
    j = pl.program_id(0)
    rows = x_ref.shape[0]

    @pl.when(j == 0)
    def _():
        acc[...] = jnp.zeros_like(acc)

    step = 3 * TILE if rows % (3 * TILE) == 0 else TILE
    for r in range(0, rows, step):
        at = slice(r, r + step)
        pre = halves(x_ref[at, :], wu_ref[...], 1, 0) + bu_ref[...]
        value, slope = gelu_parts(pre)
        value = value.astype(jnp.bfloat16)
        act_ref[at, :] = value
        slope_ref[at, :] = slope.astype(jnp.bfloat16)
        acc[at, :] += halves(value, wd_ref[...], 1, 0)

    @pl.when(j == pl.num_programs(0) - 1)
    def _():
        sums_ref[...] = jnp.zeros_like(sums_ref)
        for at in row_blocks(rows):
            hidden = hidden_ref[at, :] + (acc[at, :] + bd_ref[...])
            centre = hidden - row_mean(hidden)
            scale_inv = lax.rsqrt(row_mean(centre * centre) + 1e-05)
            unit = centre * scale_inv
            result_ref[at, :] = (unit * gain_ref[...] + shift_ref[...]).astype(jnp.bfloat16)
            upstream = cot_ref[at, :].astype(jnp.float32)
            grad = norm_back(upstream, unit, scale_inv, gain_ref[...])
            grad_ref[at, :] = grad
            low_ref[at, :] = grad.astype(jnp.bfloat16)
            sums_ref[0:1, :] += column_sum(upstream * unit)
            sums_ref[1:2, :] += column_sum(upstream)
            sums_ref[2:3, :] += column_sum(grad)


HIDDEN_BLOCK = 512


def mlp_forward(x, wu, bu, wd, bd, hidden, gain, shift, cot):
    tokens, width = x.shape
    inner = wu.shape[1]
    block = HIDDEN_BLOCK
    full = lambda r, c: pl.BlockSpec((r, c), lambda j: (0, 0))
    across = pl.BlockSpec((tokens, block), lambda j: (0, j))
    return pl.pallas_call(
        mlp_fwd_kernel,
        grid=(inner // block,),
        in_specs=[
            full(tokens, width), pl.BlockSpec((width, block), lambda j: (0, j)), pl.BlockSpec((1, block), lambda j: (0, j)),
            pl.BlockSpec((block, width), lambda j: (j, 0)), full(1, width), full(tokens, width), full(1, width),
            full(1, width), full(tokens, width),
        ],
        out_specs=[across, across, full(tokens, width), full(tokens, width), full(tokens, width), full(8, width)],
        out_shape=[
            jax.ShapeDtypeStruct((tokens, inner), jnp.bfloat16), jax.ShapeDtypeStruct((tokens, inner), jnp.bfloat16),
            jax.ShapeDtypeStruct((tokens, width), jnp.bfloat16), jax.ShapeDtypeStruct((tokens, width), jnp.float32),
            jax.ShapeDtypeStruct((tokens, width), jnp.bfloat16), jax.ShapeDtypeStruct((8, width), jnp.float32),
        ],
        scratch_shapes=[pltpu.VMEM((tokens, width), jnp.float32)],
        compiler_params=pltpu.CompilerParams(vmem_limit_bytes=56 << 20),
        cost_estimate=pl.CostEstimate(flops=4 * tokens * width * inner, bytes_accessed=50_000_000, transcendentals=6_000_000),
        name="mlp_forward",
    )(x, wu, bu.reshape(1, -1), wd, bd.reshape(1, -1), hidden, gain.reshape(1, -1), shift.reshape(1, -1), cot)


def mlp_bwd_kernel(low_ref, wd_ref, slope_ref, act_ref, x_ref, wu_ref, grad_ref, unit_ref, inv_ref, gain_ref,
                   up_ref, down_ref, bias_ref, two_ref, two_low_ref, sums_ref, xt, acc):
    j = pl.program_id(0)
    rows = x_ref.shape[0]

    @pl.when(j == 0)
    def _():
        acc[...] = jnp.zeros_like(acc)
        for c in range(0, x_ref.shape[1], TILE):
            xt[c : c + TILE, :] = x_ref[:, c : c + TILE].T

    grad = dot(low_ref[...], wd_ref[...], 1, 1).astype(jnp.bfloat16).astype(jnp.float32)
    grad = grad * slope_ref[...].astype(jnp.float32)
    bias_ref[...] = column_sum(grad)
    grad = grad.astype(jnp.bfloat16)
    acc[...] += dot(grad, wu_ref[...], 1, 1)
    up_ref[...] = dot(xt[...], grad, 1, 0).astype(jnp.bfloat16)
    down_ref[...] = dot(act_ref[...].T, low_ref[...], 1, 0).astype(jnp.bfloat16)

    @pl.when(j == pl.num_programs(0) - 1)
    def _():
        sums_ref[...] = jnp.zeros_like(sums_ref)
        for at in row_blocks(rows):
            upstream = grad_ref[at, :] + acc[at, :].astype(jnp.bfloat16).astype(jnp.float32)
            unit = unit_ref[at, :]
            two = norm_back(upstream, unit, inv_ref[at, :], gain_ref[...])
            two_ref[at, :] = two
            two_low_ref[at, :] = two.astype(jnp.bfloat16)
            sums_ref[0:1, :] += column_sum(upstream * unit)
            sums_ref[1:2, :] += column_sum(upstream)


def mlp_backward(low, wd, slope, act, x, wu, grad, unit, inv, gain):
    tokens, width = x.shape
    inner = wu.shape[1]
    block = HIDDEN_BLOCK
    full = lambda r, c: pl.BlockSpec((r, c), lambda j: (0, 0))
    across = lambda r: pl.BlockSpec((r, block), lambda j: (0, j))
    down = pl.BlockSpec((block, width), lambda j: (j, 0))
    return pl.pallas_call(
        mlp_bwd_kernel,
        grid=(inner // block,),
        in_specs=[
            full(tokens, width), down, across(tokens), across(tokens), full(tokens, width), across(width),
            full(tokens, width), full(tokens, width), full(tokens, 1), full(1, width),
        ],
        out_specs=[across(width), down, across(1), full(tokens, width), full(tokens, width), full(8, width)],
        out_shape=[
            jax.ShapeDtypeStruct((width, inner), jnp.bfloat16), jax.ShapeDtypeStruct((inner, width), jnp.bfloat16),
            jax.ShapeDtypeStruct((1, inner), jnp.float32), jax.ShapeDtypeStruct((tokens, width), jnp.float32),
            jax.ShapeDtypeStruct((tokens, width), jnp.bfloat16), jax.ShapeDtypeStruct((8, width), jnp.float32),
        ],
        scratch_shapes=[pltpu.VMEM((width, tokens), jnp.bfloat16), pltpu.VMEM((tokens, width), jnp.float32)],
        compiler_params=pltpu.CompilerParams(vmem_limit_bytes=58 << 20),
        cost_estimate=pl.CostEstimate(flops=8 * tokens * width * inner, bytes_accessed=70_000_000, transcendentals=0),
        name="mlp_backward",
    )(low, wd, slope, act, x, wu, grad, unit, inv, gain.reshape(1, -1))


def normalize(hidden, gain, shift):
    centre = hidden - jnp.mean(hidden, axis=-1, keepdims=True)
    scale_inv = lax.rsqrt(jnp.mean(centre * centre, axis=-1, keepdims=True) + 1e-05)
    unit = centre * scale_inv
    return (unit * gain + shift, unit, scale_inv)


def normalize_back(upstream, unit, scale_inv, gain):
    along = upstream * gain
    inner = (
        along
        - jnp.mean(along, axis=-1, keepdims=True)
        - unit * jnp.mean(along * unit, axis=-1, keepdims=True)
    )
    return (scale_inv * inner, jnp.sum(upstream * unit, axis=0), jnp.sum(upstream, axis=0))


def gate(value, *others):
    return lax.optimization_barrier((value,) + others)[0]


def shards(
    inputs,
    encoded,
    target_lengths,
    source_lengths,
    query_key_value,
    bucket_weight,
    self_output,
    cross_query,
    cross_key_value,
    cross_output,
    up_weight,
    up_bias,
    down_weight,
    down_bias,
    norm_gain,
    norm_shift,
    cotangent,
):
    row_count, streams, local, width = inputs.shape
    parts, size = lax.axis_size("dp"), lax.axis_size("seq")
    route = Route(parts, size)
    full = local * size
    z = lax.axis_index("seq")
    begin = z * local
    bf16, f32 = jnp.bfloat16, jnp.float32
    tokens = streams * local
    up_chain = [(i, i + 1) for i in range(size - 1)]
    down_chain = [(i + 1, i) for i in range(size - 1)]

    def mm(left, right):
        return jnp.dot(left, right, preferred_element_type=f32)

    def mm_t(left, right):
        return lax.dot_general(left, right, (((1,), (1,)), ((), ())), preferred_element_type=f32)

    def wgrad(left, right):
        return dot(left, right, 0, 0).astype(bf16)

    flat = inputs.reshape(tokens, width)
    main = flat[:local]
    hops = HALO // local
    passing, pieces = main, []
    for _ in range(hops):
        passing = lax.ppermute(passing, "seq", up_chain)
        pieces.insert(0, passing)
    halo = jnp.concatenate(pieces, axis=0)
    extended = jnp.concatenate([halo, flat], axis=0)
    own_source = encoded.reshape(local, width)
    waiting, halo = lax.optimization_barrier((own_source, halo))
    sources = [own_source] + [
        lax.ppermute(waiting, "seq", [(i, (i + k) % size) for i in range(size)]) for k in range(1, size)
    ]
    source = jnp.concatenate(sources, axis=0)

    here = begin + jnp.arange(local, dtype=jnp.int32)
    ends = jnp.cumsum(target_lengths[0])
    source_ends = jnp.cumsum(source_lengths[0])
    passed = here[:, None] >= ends[None, :]
    number = jnp.sum(passed.astype(jnp.int32), axis=1)
    start = jnp.max(jnp.where(passed, ends[None, :], 0), axis=1) - begin + HALO
    is_doc = number[:, None] == jnp.arange(ends.shape[0] + 1, dtype=jnp.int32)[None, :]
    zero = jnp.zeros((1,), jnp.int32)
    first = jnp.sum(jnp.where(is_doc, jnp.concatenate([zero, source_ends])[None, :], 0), axis=1)
    last = jnp.sum(jnp.where(is_doc, jnp.concatenate([source_ends, zero + full])[None, :], 0), axis=1)
    edge = start[::TILE]
    at = HALO + TILE * jnp.arange(local // TILE, dtype=jnp.int32)
    need = 1 + (edge < at - TILE).astype(jnp.int32) + (edge < at - 3 * TILE).astype(jnp.int32)
    low_key = first[::TILE] // PAIR
    count = (last[TILE - 1 :: TILE] + PAIR - 1) // PAIR - low_key

    names = jnp.arange(TILE, dtype=jnp.int32)[None, :]
    place = begin - HALO + jnp.arange(HALO + local, dtype=jnp.int32)
    key_doc = jnp.where(place >= 0, jnp.sum((place[:, None] >= ends[None, :]).astype(jnp.int32), axis=1), TILE)
    place = jnp.arange(full, dtype=jnp.int32)
    source_doc = jnp.sum((place[:, None] >= source_ends[None, :]).astype(jnp.int32), axis=1)
    doc = (number[:, None] == names).astype(bf16)
    block = lambda of: jnp.where((names < 8) & (of[:, None] != names), NEG, 0.0).astype(bf16)
    target_aug, source_aug = block(key_doc), block(source_doc)
    skew, hot = bias_tables()

    query_main = mm(flat, query_key_value).astype(bf16)
    relative = mm(flat, bucket_weight)
    proj = query_main
    halo_kv = mm(halo, query_key_value[:, width:]).astype(bf16)
    self_mix, self_weights = self_forward(need, proj, halo_kv, relative, doc, target_aug, skew)
    hidden_one, unit_one, inv_one = normalize(flat.astype(f32) + mm(self_mix, self_output), norm_gain[0], norm_shift[0])
    low_one = hidden_one.astype(bf16)
    cross_q = mm(low_one, cross_query).astype(bf16)
    source_kv = mm(source, cross_key_value).astype(bf16)
    cross_mix, cross_weights = cross_forward(low_key, count, cross_q, source_kv, doc, source_aug)
    hidden_two, unit_two, inv_two = normalize(hidden_one + mm(cross_mix, cross_output), norm_gain[1], norm_shift[1])
    low_two = hidden_two.astype(bf16)
    activated, slope, result, three_grad, three_low, three_sums = mlp_forward(
        low_two, up_weight, up_bias, down_weight, down_bias, hidden_two, norm_gain[2], norm_shift[2],
        cotangent.reshape(tokens, width),
    )
    gain_three, shift_three, down_bias_grad = three_sums[0], three_sums[1], three_sums[2]

    up_part, down_part, up_bias_grad, two_grad, two_low, two_sums = mlp_backward(
        three_low, down_weight, slope, activated, low_two, up_weight, three_grad, unit_two, inv_two, norm_gain[1]
    )
    gain_two, shift_two = two_sums[0], two_sums[1]
    up_bias_grad = up_bias_grad.reshape(-1)
    cross_up = mm_t(two_low, cross_output).astype(bf16)
    wide = [up_part, down_part]
    wide_plan = Plan(route, [a.shape for a in wide], 0)
    query_low, source_low, up_grad, down_grad = cross_backward(
        wide_plan, wide, cross_q, source_kv, cross_mix, cross_up, cross_weights
    )
    source_back = mm_t(source_low, cross_key_value)
    far = size // 2
    shifts = [k for k in range(1, size) if k != far]
    block = lambda k: source_back[k * local : (k + 1) * local].astype(bf16)
    hidden_one_grad = two_grad + mm_t(query_low, cross_query).astype(bf16).astype(f32)
    one_grad, gain_one, shift_one = normalize_back(hidden_one_grad, unit_one, inv_one, norm_gain[0])
    one_low = one_grad.astype(bf16)
    self_up = mm_t(one_low, self_output).astype(bf16)
    square = [
        wgrad(source, source_low),
        wgrad(cross_mix, two_low),
        wgrad(low_one, query_low),
        wgrad(self_mix, one_low),
    ]
    square_plan = Plan(route, [a.shape for a in square], 1)
    query_grad, kv_low, table_low, came, *square_sums = self_backward(
        square_plan, square, shifts, jnp.stack([block(k) for k in shifts]), proj, halo_kv, hot, self_mix, self_up, self_weights
    )
    cross_kv_grad, cross_out_grad, cross_query_grad, self_out_grad = square_sums
    halo_back = mm_t(kv_low[:HALO], query_key_value[:, width:]).astype(bf16)
    returned = []
    for k in range(1, hops + 1):
        piece = halo_back[HALO - k * local : HALO - (k - 1) * local]
        returned.append(lax.ppermute(piece, "seq", [(i, i - k) for i in range(k, size)]))
    query_late, kv_late, table_late = lax.optimization_barrier((query_grad, kv_low, table_low, halo_back))[:3]
    back = mm_t(query_late, query_key_value[:, :width]) + mm_t(kv_late[HALO:], query_key_value[:, width:])
    back = (back + mm_t(table_late, bucket_weight)).reshape(streams, local, width)
    passing = sum(got.astype(f32) for got in returned)
    back = jnp.concatenate([back[:1] + passing[None], back[1:]], axis=0).reshape(tokens, width)
    inputs_grad = (one_grad + back.astype(bf16).astype(f32)).astype(bf16)
    devices = parts * size
    gains = jnp.stack([gain_one, gain_two, gain_three]).reshape(3, devices, -1).transpose(1, 0, 2)
    shifts = jnp.stack([shift_one, shift_two, shift_three]).reshape(3, devices, -1).transpose(1, 0, 2)
    each = width // devices
    small = jnp.concatenate(
        [
            up_bias_grad.reshape(devices, -1),
            down_bias_grad.reshape(devices, -1),
            gains.reshape(devices, -1),
            shifts.reshape(devices, -1),
        ],
        axis=1,
    )
    used = small.shape[1]
    small = jnp.pad(small, ((0, 0), (0, 16 * TILE - used))).reshape(devices * 8, 2 * TILE)
    arrays = [
        wgrad(flat, query_late),
        wgrad(extended, kv_late),
        wgrad(flat, gate(table_late, inputs_grad)),
    ]
    plan = Plan(route, [a.shape for a in arrays], 2, [(0, 0), (0, width), (1, 0)])
    few = Plan(route, [small.shape], 2, chunk=TILE, kind=f32)
    qkv_grad, bucket_grad, small, last_came = scatter_sums(plan, few, [far], arrays, small, block(far)[None])
    encoded_grad = source_back[:local] + jnp.sum(came.astype(f32), axis=0) + last_came[0].astype(f32)
    small = small.reshape(-1)
    wide_each = up_bias_grad.shape[0] // devices
    cuts = [wide_each, wide_each + each, wide_each + 4 * each, used]
    up_bias_grad, down_bias_grad, gains, shifts, _ = jnp.split(small, cuts)
    return (
        result.reshape(inputs.shape),
        inputs_grad.reshape(inputs.shape),
        encoded_grad.astype(bf16).reshape(encoded.shape),
        qkv_grad,
        bucket_grad,
        self_out_grad,
        cross_query_grad,
        cross_kv_grad,
        cross_out_grad,
        up_grad,
        up_bias_grad,
        down_grad,
        down_bias_grad,
        gains.reshape(3, each),
        shifts.reshape(3, each),
    )


def solution(mesh):
    placed = (
        P("dp", None, "seq", None),
        P("dp", "seq", None),
        P("dp", None),
        P("dp", None),
        P(),
        P(),
        P(),
        P(),
        P(),
        P(),
        P(),
        P(),
        P(),
        P(),
        P(),
        P(),
        P("dp", None, "seq", None),
    )
    return jax.shard_map(
        shards,
        mesh=mesh,
        in_specs=placed,
        out_specs=(
            P("dp", None, "seq", None),
            P("dp", None, "seq", None),
            P("dp", "seq", None),
            P(("dp", "seq"), None),
            P(("dp", "seq"), None),
            P(("dp", "seq"), None),
            P(("dp", "seq"), None),
            P(("dp", "seq"), None),
            P(("dp", "seq"), None),
            P(("dp", "seq"), None),
            P(("dp", "seq")),
            P(("dp", "seq"), None),
            P(("dp", "seq")),
            P(None, ("dp", "seq")),
            P(None, ("dp", "seq")),
        ),
        check_vma=False,
    )
```

```python
import functools
import math

import jax
import jax.numpy as jnp
from jax import lax
from jax.experimental import pallas as pl
from jax.experimental.pallas import tpu as pltpu
from jax.sharding import PartitionSpec as P

HEAD_DIM = 64
BUCKETS = 32
STREAMS = 3
HALO = 512
TILE = 128
PAIR = 2 * TILE
ROWS = 2 * STREAMS * TILE
NEG = -1e30
SCALE = HEAD_DIM ** (-0.5)

bucket_edges = [
    int(math.ceil(16.0 * 8.0 ** (bucket_level / 16.0))) for bucket_level in range(1, 16)
]


def bucket_of(distance):
    forward_gap = jnp.maximum(distance, 0)
    far_bucket = jnp.full_like(forward_gap, 16)
    for bucket_edge in bucket_edges:
        far_bucket = far_bucket + (forward_gap >= bucket_edge).astype(jnp.int32)
    return jnp.where(forward_gap < 16, forward_gap, far_bucket)


def iota(shape, axis):
    return lax.broadcasted_iota(jnp.int32, shape, axis)


def dot(a, b, ca, cb):
    return lax.dot_general(a, b, (((ca,), (cb,)), ((), ())), preferred_element_type=jnp.float32)


def bias_tables():
    col = iota((PAIR, PAIR), 1)
    gap = jnp.where(col < TILE, (TILE - col) % TILE, PAIR)
    row = iota((PAIR, PAIR), 0) % TILE
    back = TILE - 1 - iota((TILE, TILE), 0)
    lane = iota((TILE, TILE), 1)
    skews = [(bucket_of(gap) + BUCKETS * h == row).astype(jnp.bfloat16) for h in range(4)]
    hots = [(bucket_of(back) + BUCKETS * h == lane).astype(jnp.bfloat16) for h in range(4)]
    return jnp.concatenate(skews, axis=0), jnp.concatenate(hots, axis=0)


def halves(a, b, ca, cb):
    half = a.shape[0] // 2
    return jnp.concatenate([dot(a[:half], b, ca, cb), dot(a[half:], b, ca, cb)], axis=0)


def head_masks():
    low = (iota((TILE, TILE), 1) < HEAD_DIM).astype(jnp.float32)
    return low.astype(jnp.bfloat16), (1.0 - low).astype(jnp.bfloat16)


def stream_rows(s, local, here):
    return pl.ds(pl.multiple_of(s * local + here, TILE), TILE)


def stack_heads(ref, local, here, lanes, masks, extra=None, scale=None):
    out = []
    for s in range(STREAMS):
        x = ref[stream_rows(s, local, here), lanes]
        if scale is not None:
            x = x * jnp.bfloat16(scale)
        for mask in masks:
            y = x * mask
            out.append(y if extra is None else jnp.concatenate([y, extra], axis=1))
    return jnp.concatenate(out, axis=0)


def part(n):
    return slice(n * TILE, (n + 1) * TILE)


def lane_max(x):
    return jnp.broadcast_to(jnp.max(x, axis=1, keepdims=True), (TILE, TILE))


def lane_sum(x):
    return jnp.broadcast_to(jnp.sum(x, axis=1, keepdims=True), (TILE, TILE))


def roll_rows(x):
    return pltpu.roll(x, 0, 1, stride=1, stride_axis=0)


REACH = HALO + TILE
FIRST = (3 * TILE, TILE, 0)


def columns(rows, base):
    return pl.BlockSpec((rows, PAIR), lambda g, *_: (0, base + g))


def whole(rows, cols):
    return pl.BlockSpec((rows, cols), lambda g, *_: (0, 0))


def weights_spec(steps, reach):
    return pl.BlockSpec((1, steps, ROWS, reach), lambda g, *_: (g, 0, 0, 0))


def self_fwd_kernel(nq, need_ref, q_ref, ko_ref, vo_ref, kh_ref, vh_ref, rel_ref, doc_ref, aug_ref, skew_ref,
                    mix_ref, pr_ref, kx, vx, sc, st, bz):
    local = nq * TILE
    for p in range(2):
        kx[p, :HALO, :TILE] = kh_ref[:, part(p)]
        kx[p, HALO:, :TILE] = ko_ref[:local, part(p)]
        kx[p, :, TILE:] = aug_ref[...]
    vx[:HALO, :] = vh_ref[...]
    vx[HALO:, :] = vo_ref[:local, :]
    masks = head_masks()
    lane = iota((TILE, TILE), 1)
    row = iota((TILE, TILE), 0)

    def step(n, _):
        i, p = n // 2, n % 2
        here = pl.multiple_of(i * TILE, TILE)
        lanes = pl.ds(pl.multiple_of(p * TILE, TILE), TILE)
        qs = stack_heads(q_ref, local, here, lanes, masks, doc_ref[pl.ds(here, TILE), :], SCALE)
        table = []
        for s in range(STREAMS):
            rel = rel_ref[stream_rows(s, local, here), :]
            high = rel.astype(jnp.bfloat16)
            table.append(jnp.concatenate([high, (rel - high.astype(jnp.float32)).astype(jnp.bfloat16)], axis=1))
        table = jnp.concatenate(table, axis=0)
        for j in range(2):
            bz[j, :, :] = halves(table, skew_ref[pl.ds(pl.multiple_of((2 * p + j) * PAIR, PAIR), PAIR), :], 1, 0)

        def path(count):
            first = FIRST[count - 1]
            keys = pl.ds(pl.multiple_of(here + first, TILE), REACH - first)
            sc[:, first:] = halves(qs, kx[p, keys, :], 1, 1)
            for b in range(2 * STREAMS):
                s, j = b // 2, b % 2
                rows = stream_rows(s, local, here)
                near = roll_rows(bz[j, part(s), :TILE])
                steady = bz[j, part(s), TILE:]
                left = sc[part(b), part(3)] + jnp.where(lane > row, near, steady)
                right = sc[part(b), part(4)]
                if s > 0:
                    own = lane_sum(qs[part(b), :TILE].astype(jnp.float32) * ko_ref[rows, lanes].astype(jnp.float32))
                    right = jnp.where(lane == row, own, right)
                right = right + jnp.where(lane <= row, near, NEG)
                far = [sc[part(b), part(m)] for m in range(first // TILE, 3)]
                top = jnp.maximum(left, right)
                if far:
                    most = far[0]
                    for x in far[1:]:
                        most = jnp.maximum(most, x)
                    top = jnp.maximum(top, most + steady)
                top = lane_max(top)
                base = top - steady
                weights = [jnp.exp(x - base) for x in far] + [jnp.exp(left - top), jnp.exp(right - top)]
                total = weights[0]
                for x in weights[1:]:
                    total = total + x
                inverse = 1.0 / lane_sum(total)
                for m, x in enumerate(weights, first // TILE):
                    x = (x * inverse).astype(jnp.bfloat16)
                    pr_ref[0, n, part(b), part(m)] = x
                    if m == 4 and s > 0:
                        st[part(b), :] = lane_sum(jnp.where(lane == row, x.astype(jnp.float32), 0.0))
            if first:
                pr_ref[0, n, :, :first] = jnp.zeros((ROWS, first), jnp.bfloat16)
            acc = halves(pr_ref[0, n, :, first:], vx[keys, lanes], 1, 0)
            main = vo_ref[stream_rows(0, local, here), lanes].astype(jnp.float32)
            for s in range(STREAMS):
                rows = stream_rows(s, local, here)
                a, b = part(2 * s), part(2 * s + 1)
                mixed = jnp.where(lane < HEAD_DIM, acc[a], acc[b])
                if s > 0:
                    own = jnp.where(lane < HEAD_DIM, st[a, :], st[b, :])
                    mixed = mixed + own * (vo_ref[rows, lanes].astype(jnp.float32) - main)
                mix_ref[rows, lanes] = mixed.astype(jnp.bfloat16)

        for count in range(1, 4):
            @pl.when(need_ref[i] == count)
            def _():
                path(count)
        return 0

    lax.fori_loop(0, 2 * nq, step, 0)


def self_forward(need, proj, halo_kv, rel, doc, aug, skew):
    tokens = proj.shape[0]
    local = tokens // STREAMS
    width = proj.shape[1] // 3
    grid = width // PAIR
    steps = 2 * local // TILE
    return pl.pallas_call(
        functools.partial(self_fwd_kernel, local // TILE),
        grid_spec=pltpu.PrefetchScalarGridSpec(
            num_scalar_prefetch=1, grid=(grid,),
            in_specs=[
                columns(tokens, 0), columns(tokens, grid), columns(tokens, 2 * grid), columns(HALO, 0), columns(HALO, grid),
                pl.BlockSpec((tokens, TILE), lambda g, *_: (0, g)),
                whole(local, TILE), whole(HALO + local, TILE), whole(4 * PAIR, PAIR),
            ],
            out_specs=[columns(tokens, 0), weights_spec(steps, REACH)],
            scratch_shapes=[
                pltpu.VMEM((2, HALO + local, PAIR), jnp.bfloat16), pltpu.VMEM((HALO + local, PAIR), jnp.bfloat16),
                pltpu.VMEM((ROWS, REACH), jnp.float32), pltpu.VMEM((ROWS, TILE), jnp.float32),
                pltpu.VMEM((2, STREAMS * TILE, PAIR), jnp.float32),
            ]),
        out_shape=[jax.ShapeDtypeStruct((tokens, width), jnp.bfloat16),
                   jax.ShapeDtypeStruct((grid, steps, ROWS, REACH), jnp.bfloat16)],
        compiler_params=pltpu.CompilerParams(vmem_limit_bytes=40 << 20),
        cost_estimate=pl.CostEstimate(flops=15_000_000_000, bytes_accessed=20_000_000, transcendentals=8_000_000),
        name="self_forward",
    )(need, proj, proj, proj, halo_kv, halo_kv, rel, doc, aug, skew)


def self_bwd_kernel(nq, plan, shifts, q_ref, ko_ref, vo_ref, kh_ref, vh_ref, hot_ref, mix_ref, up_ref, pr_ref,
                    wq_ref, wk_ref, wv_ref, wb_ref, *refs):
    arrays, handed, refs = refs[: plan.many], refs[plan.many], refs[plan.many + 1 :]
    (dq_ref, dkv_ref, drel_ref, back_ref, got), refs = refs[:5], refs[5:]
    outs = len(plan.out_shapes())
    results, (kx, vx, dp, ds, cb, st, dkt, dvt, cv, acc), scratch = refs[:outs], refs[outs : outs + 10], refs[outs + 10 :]
    g = pl.program_id(0)
    comm = Comm(plan, arrays, results, scratch[:-1])
    hand = Handing(shifts, 8 * nq, handed, got, scratch[-1])

    @pl.when(g == 0)
    def _():
        comm.barrier()

    local = nq * TILE
    kx[:HALO, :] = kh_ref[...]
    kx[HALO:, :] = ko_ref[:local, :]
    vx[:HALO, :] = vh_ref[...]
    vx[HALO:, :] = vo_ref[:local, :]
    dkt[...] = jnp.zeros_like(dkt)
    dvt[...] = jnp.zeros_like(dvt)
    masks = head_masks()
    lane = iota((TILE, TILE), 1)
    row = iota((TILE, TILE), 0)
    flip = (row + lane == TILE - 1).astype(jnp.float32).astype(jnp.bfloat16)
    gl = pl.multiple_of(g * PAIR, PAIR)
    third = q_ref.shape[1] * pl.num_programs(0)

    def step(n, _):
        i, p = n // 2, n % 2
        here = pl.multiple_of(i * TILE, TILE)
        lanes = pl.ds(pl.multiple_of(p * TILE, TILE), TILE)
        hand.step(g * 2 * nq + n)
        comm.step(g * 2 * nq + n)
        qs = stack_heads(q_ref, local, here, lanes, masks, None, SCALE)
        ups = stack_heads(up_ref, local, here, lanes, masks)
        qt = qs.T
        upt = ups.T

        keys = pl.ds(pl.multiple_of(here, TILE), REACH)
        dp[...] = halves(ups, vx[keys, lanes], 1, 1)
        for b in range(2 * STREAMS):
            s = b // 2
            rows = stream_rows(s, local, here)
            upf = ups[part(b)].astype(jnp.float32)
            centre = lane_sum(upf * mix_ref[rows, lanes].astype(jnp.float32))
            xs = [pr_ref[0, n, part(b), part(m)].astype(jnp.float32) for m in range(5)]
            ys = [(xs[m] * (dp[part(b), part(m)] - centre)).astype(jnp.bfloat16) for m in range(5)]
            for m in range(4):
                ds[part(b), part(m)] = ys[m]
            ys = [y.astype(jnp.float32) for y in ys]
            band = jnp.where(lane > row, ys[3], 0.0)
            st[2, part(b), :] = ys[0] + ys[1] + ys[2] + (ys[3] - band)
            if s > 0:
                own_weight = lane_sum(jnp.where(lane == row, xs[4], 0.0))
                own_grad = own_weight * (lane_sum(upf * vo_ref[rows, lanes].astype(jnp.float32)) - centre)
                own_grad = own_grad.astype(jnp.bfloat16).astype(jnp.float32)
                st[0, part(b), :] = own_weight
                st[1, part(b), :] = own_grad
                band = band + jnp.where(lane == row, own_grad, ys[4])
                ds[part(b), part(4)] = jnp.where(lane == row, 0.0, ys[4]).astype(jnp.bfloat16)
            else:
                band = band + ys[4]
                ds[part(b), part(4)] = ys[4].astype(jnp.bfloat16)
            cb[:, part(b)] = band.astype(jnp.bfloat16)
        dkt[p, :, keys] += dot(qt, ds[...], 1, 0)
        dvt[p, :, keys] += dot(upt, pr_ref[0, n], 1, 0)
        dq = dot(ds[...], kx[keys, lanes], 1, 0)
        turned = dot(flip, cb[...], 1, 0)
        rolled = [roll_rows(turned[:, part(b)]).astype(jnp.bfloat16) for b in range(2 * STREAMS)]
        rolled = jnp.concatenate([jnp.concatenate(rolled[2 * s : 2 * s + 2], axis=1) for s in range(STREAMS)], axis=0)
        table = dot(rolled, hot_ref[pl.ds(pl.multiple_of(p * PAIR, PAIR), PAIR), :], 1, 0).astype(jnp.bfloat16)
        table = dot(flip, jnp.concatenate([table[part(s)] for s in range(STREAMS)], axis=1), 1, 0)

        excess = None
        for s in range(STREAMS):
            rows = stream_rows(s, local, here)
            a, b = part(2 * s), part(2 * s + 1)
            dqs = jnp.where(lane < HEAD_DIM, dq[a], dq[b])
            col = pl.multiple_of(gl + p * TILE, TILE)
            kept = pl.ds(pl.multiple_of(HALO + s * local + here, TILE), TILE)
            if s > 0:
                own_weight = jnp.where(lane < HEAD_DIM, st[0, a, :], st[0, b, :])
                own_grad = jnp.where(lane < HEAD_DIM, st[1, a, :], st[1, b, :])
                dqs = dqs + own_grad * ko_ref[rows, lanes].astype(jnp.float32)
                own_value = own_weight * up_ref[rows, lanes].astype(jnp.float32)
                excess = own_value if excess is None else excess + own_value
                dkv_ref[kept, pl.ds(col, TILE)] = (
                    own_grad * (SCALE * q_ref[rows, lanes].astype(jnp.float32))
                ).astype(jnp.bfloat16)
                dkv_ref[kept, pl.ds(pl.multiple_of(col + third, TILE), TILE)] = own_value.astype(jnp.bfloat16)
            dq_ref[rows, lanes] = (SCALE * dqs).astype(jnp.bfloat16)
            dr = table[:, part(s)]
            for j, blk in enumerate((a, b)):
                dr = dr + jnp.where(lane == BUCKETS * (2 * p + j) + BUCKETS - 1, lane_sum(st[2, blk, :]), 0.0)

            @pl.when(p == 0)
            def _():
                drel_ref[rows, :] = dr.astype(jnp.bfloat16)

            @pl.when(p == 1)
            def _():
                drel_ref[rows, :] = (drel_ref[rows, :].astype(jnp.float32) + dr).astype(jnp.bfloat16)
        cv[pl.ds(here, TILE), lanes] = excess
        return 0

    lax.fori_loop(0, 2 * nq, step, 0)
    for p in range(2):
        for j, grads in enumerate((dkt, dvt)):
            col = pl.multiple_of(gl + p * TILE + third * j, TILE)
            full = grads[p, :, :].T
            main = full[HALO:] if j == 0 else full[HALO:] - cv[:, part(p)]
            dkv_ref[:HALO, pl.ds(col, TILE)] = full[:HALO].astype(jnp.bfloat16)
            dkv_ref[HALO : HALO + local, pl.ds(col, TILE)] = main.astype(jnp.bfloat16)

    @pl.when(g == 0)
    def _():
        acc[...] = jnp.zeros_like(acc)

    rows = acc.shape[0]
    for r in range(0, rows, PAIR):
        at = slice(r, r + PAIR)
        part_sum = dot(dkv_ref[at, pl.ds(gl, PAIR)], wk_ref[...], 1, 1)
        part_sum = part_sum + dot(dkv_ref[at, pl.ds(pl.multiple_of(gl + third, PAIR), PAIR)], wv_ref[...], 1, 1)
        if r >= HALO:
            own = slice(r - HALO, r - HALO + PAIR)
            part_sum = part_sum + dot(dq_ref[own, :], wq_ref[...], 1, 1) + dot(drel_ref[own, :], wb_ref[...], 1, 1)
        acc[at, :] += part_sum

    @pl.when(g == pl.num_programs(0) - 1)
    def _():
        back_ref[...] = acc[...].astype(jnp.bfloat16)
        comm.rest(4 * 2 * nq)
        hand.finish()


def self_backward(plan, arrays, shifts, handed, proj, halo_kv, hot, mix, up, weights, qkv, bucket):
    tokens = proj.shape[0]
    local = tokens // STREAMS
    width = proj.shape[1] // 3
    grid = width // PAIR
    steps = 2 * local // TILE
    return pl.pallas_call(
        functools.partial(self_bwd_kernel, local // TILE, plan, shifts),
        grid=(grid,),
        in_specs=[
            columns(tokens, 0), columns(tokens, grid), columns(tokens, 2 * grid), columns(HALO, 0), columns(HALO, grid),
            whole(4 * TILE, TILE), columns(tokens, 0), columns(tokens, 0), weights_spec(steps, REACH),
            columns(width, 0), columns(width, grid), columns(width, 2 * grid), pl.BlockSpec((width, TILE), lambda g, *_: (0, g)),
        ] + plan.in_specs() + [pl.BlockSpec(memory_space=pl.ANY)],
        out_specs=[
            columns(tokens, 0), whole(HALO + tokens, 2 * width), pl.BlockSpec((tokens, TILE), lambda g, *_: (0, g)),
            whole(HALO + tokens, width), pl.BlockSpec(memory_space=pl.ANY),
        ] + plan.out_specs(),
        scratch_shapes=[
            pltpu.VMEM((HALO + local, PAIR), jnp.bfloat16), pltpu.VMEM((HALO + local, PAIR), jnp.bfloat16),
            pltpu.VMEM((ROWS, REACH), jnp.float32), pltpu.VMEM((ROWS, REACH), jnp.bfloat16),
            pltpu.VMEM((TILE, ROWS), jnp.bfloat16), pltpu.VMEM((3, ROWS, TILE), jnp.float32),
            pltpu.VMEM((2, TILE, HALO + local), jnp.float32), pltpu.VMEM((2, TILE, HALO + local), jnp.float32),
            pltpu.VMEM((local, PAIR), jnp.float32), pltpu.VMEM((HALO + tokens, width), jnp.float32),
        ] + plan.scratch() + handing_scratch(len(shifts), 8 * local // TILE),
        out_shape=[
            jax.ShapeDtypeStruct((tokens, width), jnp.bfloat16), jax.ShapeDtypeStruct((HALO + tokens, 2 * width), jnp.bfloat16),
            jax.ShapeDtypeStruct((tokens, width // 2), jnp.bfloat16),
            jax.ShapeDtypeStruct((HALO + tokens, width), jnp.bfloat16), jax.ShapeDtypeStruct(handed.shape, handed.dtype),
        ] + plan.out_shapes(),
        compiler_params=pltpu.CompilerParams(collective_id=plan.number, has_side_effects=True, vmem_limit_bytes=62 << 20),
        cost_estimate=pl.CostEstimate(flops=40_000_000_000, bytes_accessed=30_000_000, transcendentals=8_000_000),
        name="self_backward",
    )(proj, proj, proj, halo_kv, halo_kv, hot, mix, up, weights, qkv, qkv, qkv, bucket, *plan.views(arrays), handed)


def gather_shards(local, ref, place):
    shards = ref.shape[0] // local
    z = lax.axis_index("seq")
    for k in range(shards):
        at = pl.ds(pl.multiple_of(lax.rem(z - k + shards, shards) * local, TILE), local)
        place(at, ref[k * local : (k + 1) * local, :])


def cross_fwd_kernel(nq, lo_ref, count_ref, q_ref, k_ref, v_ref, doc_ref, aug_ref, mix_ref, pr_ref, kx, vx, sc):
    local = nq * TILE
    across = k_ref.shape[0] // PAIR

    def place_key(at, block):
        for p in range(2):
            kx[p, at, :TILE] = block[:, part(p)]

    def place_value(at, block):
        vx[at, :] = block

    gather_shards(local, k_ref, place_key)
    gather_shards(local, v_ref, place_value)
    for p in range(2):
        kx[p, :, TILE:] = aug_ref[...]
    masks = head_masks()
    lane = iota((TILE, TILE), 1)

    def step(n, _):
        i, p = n // 2, n % 2
        here = pl.multiple_of(i * TILE, TILE)
        lanes = pl.ds(pl.multiple_of(p * TILE, TILE), TILE)
        qs = stack_heads(q_ref, local, here, lanes, masks, doc_ref[pl.ds(here, TILE), :], SCALE)

        def window(w):
            return pl.ds(pl.multiple_of((lo_ref[i] + w) * PAIR, PAIR), PAIR)

        def path(count):
            keys = pl.ds(pl.multiple_of(lo_ref[i] * PAIR, PAIR), count * PAIR)
            sc[:, : count * PAIR] = halves(qs, kx[p, keys, :], 1, 1)
            for b in range(2 * STREAMS):
                xs = [sc[part(b), part(m)] for m in range(2 * count)]
                top = xs[0]
                for x in xs[1:]:
                    top = jnp.maximum(top, x)
                top = lane_max(top)
                xs = [jnp.exp(x - top) for x in xs]
                total = xs[0]
                for x in xs[1:]:
                    total = total + x
                inverse = 1.0 / lane_sum(total)
                xs = [(x * inverse).astype(jnp.bfloat16) for x in xs]
                for w in range(count):
                    pr_ref[0, n, part(b), window(w)] = jnp.concatenate(xs[2 * w : 2 * w + 2], axis=1)
            total = halves(pr_ref[0, n, :, keys], vx[keys, lanes], 1, 0)
            for s in range(STREAMS):
                mixed = jnp.where(lane < HEAD_DIM, total[part(2 * s)], total[part(2 * s + 1)])
                mix_ref[stream_rows(s, local, here), lanes] = mixed.astype(jnp.bfloat16)

        for count in range(1, across + 1):
            @pl.when(count_ref[i] == count)
            def _():
                path(count)

        for w in range(across):
            @pl.when((w < lo_ref[i]) | (w >= lo_ref[i] + count_ref[i]))
            def _():
                pr_ref[0, n, :, w * PAIR : (w + 1) * PAIR] = jnp.zeros((ROWS, PAIR), jnp.bfloat16)
        return 0

    lax.fori_loop(0, 2 * nq, step, 0)


def cross_forward(lo, count, q, kv, doc, aug):
    tokens, width = q.shape
    local = tokens // STREAMS
    full = kv.shape[0]
    grid = width // PAIR
    steps = 2 * local // TILE
    return pl.pallas_call(
        functools.partial(cross_fwd_kernel, local // TILE),
        grid_spec=pltpu.PrefetchScalarGridSpec(
            num_scalar_prefetch=2, grid=(grid,),
            in_specs=[columns(tokens, 0), columns(full, 0), columns(full, grid), whole(local, TILE), whole(full, TILE)],
            out_specs=[columns(tokens, 0), weights_spec(steps, full)],
            scratch_shapes=[
                pltpu.VMEM((2, full, PAIR), jnp.bfloat16), pltpu.VMEM((full, PAIR), jnp.bfloat16),
                pltpu.VMEM((ROWS, full), jnp.float32),
            ]),
        out_shape=[jax.ShapeDtypeStruct((tokens, width), jnp.bfloat16), jax.ShapeDtypeStruct((grid, steps, ROWS, full), jnp.bfloat16)],
        compiler_params=pltpu.CompilerParams(vmem_limit_bytes=48 << 20),
        cost_estimate=pl.CostEstimate(flops=15_000_000_000, bytes_accessed=20_000_000, transcendentals=8_000_000),
        name="cross_forward",
    )(lo, count, q, kv, kv, doc, aug)


def cross_bwd_kernel(nq, plan, q_ref, k_ref, v_ref, mix_ref, up_ref, pr_ref, *refs):
    arrays, (dq_ref, dkv_ref), refs = refs[: plan.many], refs[plan.many : plan.many + 2], refs[plan.many + 2 :]
    outs = len(plan.out_shapes())
    results, (kx, vx, dp, ds, st, dkt, dvt), scratch = refs[:outs], refs[outs : outs + 7], refs[outs + 7 :]
    g = pl.program_id(0)
    comm = Comm(plan, arrays, results, scratch)

    @pl.when(g == 0)
    def _():
        comm.barrier()

    local = nq * TILE

    def place_key(at, block):
        kx[at, :] = block

    def place_value(at, block):
        vx[at, :] = block

    gather_shards(local, k_ref, place_key)
    gather_shards(local, v_ref, place_value)
    dkt[...] = jnp.zeros_like(dkt)
    dvt[...] = jnp.zeros_like(dvt)
    masks = head_masks()
    lane = iota((TILE, TILE), 1)

    def step(n, _):
        i, p = n // 2, n % 2
        here = pl.multiple_of(i * TILE, TILE)
        lanes = pl.ds(pl.multiple_of(p * TILE, TILE), TILE)
        comm.step(g * 2 * nq + n)
        qs = stack_heads(q_ref, local, here, lanes, masks, None, SCALE)
        ups = stack_heads(up_ref, local, here, lanes, masks)
        qt = qs.T
        upt = ups.T
        for b in range(2 * STREAMS):
            rows = stream_rows(b // 2, local, here)
            st[part(b), :] = lane_sum(ups[part(b)].astype(jnp.float32) * mix_ref[rows, lanes].astype(jnp.float32))
        dp[...] = halves(ups, vx[:, lanes], 1, 1)
        for b in range(2 * STREAMS):
            for m in range(dp.shape[1] // TILE):
                x = pr_ref[0, n, part(b), part(m)].astype(jnp.float32)
                ds[part(b), part(m)] = (x * (dp[part(b), part(m)] - st[part(b), :])).astype(jnp.bfloat16)
        dkt[p, :, :] += dot(qt, ds[...], 1, 0)
        dvt[p, :, :] += dot(upt, pr_ref[0, n], 1, 0)
        dqa = dot(ds[...], kx[:, lanes], 1, 0)
        for s in range(STREAMS):
            dq = jnp.where(lane < HEAD_DIM, dqa[part(2 * s)], dqa[part(2 * s + 1)])
            dq_ref[stream_rows(s, local, here), lanes] = (SCALE * dq).astype(jnp.bfloat16)
        return 0

    lax.fori_loop(0, 2 * nq, step, 0)
    third = q_ref.shape[1] * pl.num_programs(0)
    shards = k_ref.shape[0] // local
    z = lax.axis_index("seq")
    for p in range(2):
        for j, acc in enumerate((dkt, dvt)):
            col = pl.multiple_of(g * PAIR + p * TILE + third * j, TILE)
            for k in range(shards):
                at = pl.ds(pl.multiple_of(lax.rem(z - k + shards, shards) * local, TILE), local)
                dkv_ref[k * local : (k + 1) * local, pl.ds(col, TILE)] = acc[p, :, at].T.astype(jnp.bfloat16)

    @pl.when(g == pl.num_programs(0) - 1)
    def _():
        comm.rest(4 * 2 * nq)


def cross_backward(plan, arrays, q, kv, mix, up, weights):
    tokens, width = q.shape
    local = tokens // STREAMS
    full = kv.shape[0]
    grid = width // PAIR
    steps = 2 * local // TILE
    return pl.pallas_call(
        functools.partial(cross_bwd_kernel, local // TILE, plan),
        grid=(grid,),
        in_specs=[
            columns(tokens, 0), columns(full, 0), columns(full, grid),
            columns(tokens, 0), columns(tokens, 0), weights_spec(steps, full),
        ] + plan.in_specs(),
        out_specs=[columns(tokens, 0), whole(full, 2 * width)] + plan.out_specs(),
        scratch_shapes=[
            pltpu.VMEM((full, PAIR), jnp.bfloat16), pltpu.VMEM((full, PAIR), jnp.bfloat16),
            pltpu.VMEM((ROWS, full), jnp.float32), pltpu.VMEM((ROWS, full), jnp.bfloat16),
            pltpu.VMEM((ROWS, TILE), jnp.float32),
            pltpu.VMEM((2, TILE, full), jnp.float32), pltpu.VMEM((2, TILE, full), jnp.float32),
        ] + plan.scratch(),
        out_shape=[
            jax.ShapeDtypeStruct((tokens, width), jnp.bfloat16), jax.ShapeDtypeStruct((full, 2 * width), jnp.bfloat16),
        ] + plan.out_shapes(),
        compiler_params=pltpu.CompilerParams(collective_id=plan.number, has_side_effects=True, vmem_limit_bytes=58 << 20),
        cost_estimate=pl.CostEstimate(flops=40_000_000_000, bytes_accessed=30_000_000, transcendentals=8_000_000),
        name="cross_backward",
    )(q, kv, kv, mix, up, weights, *plan.views(arrays))


CHUNK = 256
SLOTS = 6


class Route:
    def __init__(self, dp, seq):
        self.dp_bits = dp.bit_length() - 1
        self.bits = self.dp_bits + seq.bit_length() - 1
        core = self.dp_bits - 1
        rest = list(reversed(range(core)))
        tail = list(reversed(range(self.dp_bits, self.bits)))
        self.orders = ([core] + rest + tail, [core] + rest[::-1] + tail)
        steps = self.bits
        self.lags = [0, 1] + [min(1 + 2 * k, 5) + max(0, k - 2) for k in range(1, steps)]

    def place(self, bit):
        if bit < self.dp_bits:
            return "dp", self.dp_bits - 1 - bit
        return "seq", self.bits - 1 - bit

    def mine(self, bit):
        axis, k = self.place(bit)
        return lax.rem(lax.axis_index(axis) // (1 << k), 2)

    def partner(self, bit):
        axis, k = self.place(bit)
        index = lax.axis_index(axis)
        return {axis: index + (1 - 2 * self.mine(bit)) * (1 << k)}

    def left(self, kind, k):
        return sorted(set(range(self.bits)) - set(self.orders[kind][:k]))


class Plan:
    def __init__(self, route, shapes, number, outs=None, chunk=CHUNK, kind=jnp.bfloat16):
        self.route, self.number, self.chunk, self.kind = route, number, chunk, kind
        self.outs = outs or [(n, 0) for n in range(len(shapes))]
        rows = min(shape[0] for shape in shapes)
        self.deep = rows >> route.bits
        self.subs = [shape[0] // rows for shape in shapes]
        self.pairs = [sub * (shape[1] // (2 * chunk)) for sub, shape in zip(self.subs, shapes)]
        self.total, self.many = sum(self.pairs), len(shapes)
        self.iterations = self.total + route.lags[route.bits]

    def views(self, arrays):
        lead = lambda sub: (2,) * self.route.bits + ((sub,) if sub > 1 else ())
        return [a.reshape(lead(sub) + (self.deep, a.shape[1])) for a, sub in zip(arrays, self.subs)]

    def in_specs(self):
        return [pl.BlockSpec(memory_space=pl.ANY)] * self.many

    def out_shapes(self):
        shapes = {}
        for (out, first), sub, pairs in zip(self.outs, self.subs, self.pairs):
            columns = first + pairs * 2 * self.chunk // sub
            shapes[out] = (sub * self.deep, max(columns, shapes.get(out, (0, 0))[1]))
        return [jax.ShapeDtypeStruct(shapes[out], jnp.float32) for out in sorted(shapes)]

    def out_specs(self):
        return [pl.BlockSpec(shape.shape, lambda *_: (0, 0)) for shape in self.out_shapes()]

    def scratch(self):
        bits = self.route.bits
        shape = lambda lead: (SLOTS, 2) + (2,) * lead + (self.deep, self.chunk)
        own = [pltpu.VMEM(shape(bits - 1), self.kind)]
        got = [pltpu.VMEM(shape(bits - 1 - k), self.kind) for k in range(bits)]
        out = [pltpu.VMEM(shape(bits - 1 - k), self.kind) for k in range(1, bits)]
        kept = [pltpu.VMEM(shape(bits - 1 - k), self.kind) for k in range(1, bits)]
        sems = [pltpu.SemaphoreType.DMA((2, SLOTS))] + [pltpu.SemaphoreType.DMA((bits, 2, SLOTS))] * 2
        return own + got + out + kept + sems


class Comm:
    def __init__(self, plan, arrays, results, scratch):
        route = plan.route
        bits = route.bits
        self.plan, self.route, self.arrays, self.results = plan, route, arrays, results
        self.pairs, self.subs, self.chunk, self.total = plan.pairs, plan.subs, plan.chunk, plan.total
        self.own = scratch[0]
        self.got = scratch[1 : 1 + bits]
        self.out = (None,) + tuple(scratch[1 + bits : 2 * bits])
        self.kept = (None,) + tuple(scratch[2 * bits : 3 * bits - 1])
        self.own_sem, self.send_sem, self.got_sem = scratch[3 * bits - 1 : 3 * bits + 2]

    def barrier(self):
        sem = pltpu.get_barrier_semaphore()
        size = 1 << (self.route.bits - self.route.dp_bits)
        others = [self.route.partner(bit) for bit in range(self.route.dp_bits)]
        others += [{"seq": lax.rem(lax.axis_index("seq") + k, size)} for k in range(1, size)]
        for other in others:
            pl.semaphore_signal(sem, inc=1, device_id=other, device_id_type=pl.DeviceIdType.MESH)
        pl.semaphore_wait(sem, len(others))

    def source(self, n, pair, kind, side):
        core = self.route.dp_bits - 1
        ref, subs = self.arrays[n], self.subs[n]
        across = ref.shape[-1] // (2 * self.chunk)
        col = pl.ds(pl.multiple_of(lax.rem(pair, across) * 2 * self.chunk + kind * self.chunk, self.chunk), self.chunk)
        index = [slice(None)] * self.route.bits
        index[core] = side
        if subs > 1:
            index.append(pair // across)
        return ref.at[tuple(index) + (slice(None), col)]

    def copy(self, k, kind, slot, src):
        return pltpu.make_async_remote_copy(
            src_ref=src,
            dst_ref=self.got[k].at[slot, kind],
            send_sem=self.send_sem.at[k, kind, slot],
            recv_sem=self.got_sem.at[k, kind, slot],
            device_id=self.route.partner(self.route.orders[kind][k]),
            device_id_type=pl.DeviceIdType.MESH,
        )

    def fetch(self, kind, slot, src):
        return pltpu.make_async_copy(src, self.own.at[slot, kind], self.own_sem.at[kind, slot])

    def begin(self, u):
        slot = lax.rem(u, SLOTS)
        side = self.route.mine(self.route.dp_bits - 1)
        first = 0
        for n, pairs in enumerate(self.pairs):
            @pl.when((u >= first) & (u < first + pairs))
            def _():
                for kind in range(2):
                    self.copy(0, kind, slot, self.source(n, u - first, kind, 1 - side)).start()
                    self.fetch(kind, slot, self.source(n, u - first, kind, side)).start()

            first += pairs

    def advance(self, k, u):
        route = self.route
        slot = lax.rem(u, SLOTS)
        for kind in range(2):
            if k == 1:
                filler = self.source(0, 0, kind, 0)
                self.fetch(kind, slot, filler).wait()
                self.copy(0, kind, slot, filler).wait()
                held = self.own
            else:
                self.copy(k - 1, kind, slot, self.out[k - 1].at[slot, kind]).wait()
                held = self.kept[k - 1]
            came = self.got[k - 1]
            if k == route.bits:
                total = held[slot, kind].astype(jnp.float32) + came[slot, kind].astype(jnp.float32)
                self.store(u, kind, total)
                continue
            bit = route.orders[kind][k]
            at = route.left(kind, k).index(bit)
            me = route.mine(bit)
            where = lambda side: (slot, kind) + (slice(None),) * at + (side,)
            theirs = where(1 - me)
            self.out[k][slot, kind] = held[theirs] + came[theirs]
            self.copy(k, kind, slot, self.out[k].at[slot, kind]).start()
            ours = where(me)
            self.kept[k][slot, kind] = held[ours] + came[ours]

    def store(self, u, kind, value):
        first, deep = 0, self.plan.deep
        for n, pairs in enumerate(self.pairs):
            out, column = self.plan.outs[n]
            across = pairs // self.subs[n]

            @pl.when((u >= first) & (u < first + pairs))
            def _():
                pair = u - first
                at = pl.multiple_of(column + (2 * lax.rem(pair, across) + kind) * self.chunk, self.chunk)
                rows = pl.ds(pl.multiple_of(pair // across * deep, deep), deep)
                self.results[out][rows, pl.ds(at, self.chunk)] = value

            first += pairs

    def step(self, t):
        @pl.when(t < self.total)
        def _():
            self.begin(t)

        for k in range(1, self.route.bits + 1):
            u = t - self.route.lags[k]

            @pl.when((u >= 0) & (u < self.total))
            def _():
                self.advance(k, u)


    def rest(self, begin):
        def body(t, _):
            self.step(t)
            return 0

        lax.fori_loop(begin, self.plan.iterations, body, 0)


class HeldComm(Comm):
    def source(self, n, pair, kind, side):
        index = [slice(None)] * self.route.bits
        index[self.route.dp_bits - 1] = side
        columns = slice(kind * self.chunk, (kind + 1) * self.chunk)
        return self.arrays[0].at[(lax.rem(pair, 2),) + tuple(index) + (slice(None), columns)]


class Handing:
    def __init__(self, shifts, pieces, source, target, sems):
        self.shifts, self.pieces = shifts, pieces
        self.source, self.target, self.sems = source, target, sems

    def copies(self, piece):
        z, size = lax.axis_index("seq"), lax.axis_size("seq")
        deep = self.source.shape[1] // self.pieces
        rows = pl.ds(pl.multiple_of(piece * deep, deep), deep)
        for n, shift in enumerate(self.shifts):
            yield pltpu.make_async_remote_copy(
                src_ref=self.source.at[n, rows],
                dst_ref=self.target.at[n, rows],
                send_sem=self.sems.at[0, n, piece],
                recv_sem=self.sems.at[1, n, piece],
                device_id={"seq": lax.rem(z - shift + size, size)},
                device_id_type=pl.DeviceIdType.MESH,
            )

    def step(self, t):
        @pl.when(t < self.pieces)
        def _():
            for copy in self.copies(t):
                copy.start()

    def finish(self):
        def body(t, _):
            for copy in self.copies(t):
                copy.wait()
            return 0

        lax.fori_loop(0, self.pieces, body, 0)


def handing_scratch(count, pieces):
    return [pltpu.SemaphoreType.DMA((2, count, pieces))]


def scatter_kernel(plan, few, shifts, *refs):
    many, outs = plan.many, len(plan.out_shapes())
    arrays, small, handed = refs[:many], refs[many], refs[many + 1]
    results, small_result, got = refs[many + 2 : many + 2 + outs], refs[many + 2 + outs], refs[many + 3 + outs]
    scratch = refs[many + 4 + outs : -1]
    half = len(scratch) // 2
    comm = Comm(plan, arrays, results, scratch[:half])
    other = Comm(few, [small], [small_result], scratch[half:])
    hand = Handing(shifts, 8, handed, got, refs[-1])
    comm.barrier()

    def body(t, _):
        hand.step(t)
        other.step(t)
        comm.step(t)
        return 0

    lax.fori_loop(0, plan.iterations, body, 0)
    hand.finish()


def scatter_sums(plan, few, shifts, arrays, small, handed):
    anywhere = pl.BlockSpec(memory_space=pl.ANY)
    return pl.pallas_call(
        functools.partial(scatter_kernel, plan, few, shifts),
        grid=(1,),
        in_specs=plan.in_specs() + few.in_specs() + [anywhere],
        out_specs=plan.out_specs() + few.out_specs() + [anywhere],
        out_shape=plan.out_shapes() + few.out_shapes() + [jax.ShapeDtypeStruct(handed.shape, handed.dtype)],
        scratch_shapes=plan.scratch() + few.scratch() + handing_scratch(len(shifts), 8),
        compiler_params=pltpu.CompilerParams(
            collective_id=plan.number, has_side_effects=True, vmem_limit_bytes=56 << 20
        ),
        cost_estimate=pl.CostEstimate(flops=20_000_000_000, bytes_accessed=60_000_000, transcendentals=0),
        name="weight_sums",
    )(*plan.views(arrays), *few.views([small]), handed)


def gelu_parts(x):
    t = 1.0 / (1.0 + jnp.abs(x) * (0.43 * 0.5**0.5))
    poly = jnp.float32(0.5 * 0.0709100743822703)
    for coef in (
        -0.2990317761502629, 0.3647352526676159, -0.06881910419857572, 0.23820862557883588,
        0.2074695458910066, 0.24398848761768033, 0.2425387164715943,
    ):
        poly = poly * t + 0.5 * coef
    bell = jnp.exp(x * x * -0.5)
    half = poly * t * bell
    below = jnp.where(x >= 0, 1.0 - half, half)
    return x * below, below + x * (bell * (1.0 / math.sqrt(2.0 * math.pi)))


def row_mean(x):
    return jnp.mean(x, axis=1, keepdims=True)


def column_sum(x):
    return jnp.sum(x, axis=0, keepdims=True)


def norm_back(upstream, unit, scale_inv, gain):
    along = upstream * gain
    return scale_inv * (along - row_mean(along) - unit * row_mean(along * unit))


def row_blocks(rows):
    return [slice(r, r + TILE) for r in range(0, rows, TILE)]


def mlp_fwd_kernel(x_ref, wu_ref, bu_ref, wd_ref, bd_ref, hidden_ref, gain_ref, shift_ref, cot_ref,
                   act_ref, slope_ref, result_ref, grad_ref, low_ref, sums_ref, acc):
    j = pl.program_id(0)
    rows = x_ref.shape[0]

    @pl.when(j == 0)
    def _():
        acc[...] = jnp.zeros_like(acc)

    step = 3 * TILE if rows % (3 * TILE) == 0 else TILE
    for r in range(0, rows, step):
        at = slice(r, r + step)
        pre = halves(x_ref[at, :], wu_ref[...], 1, 0) + bu_ref[...]
        value, slope = gelu_parts(pre)
        value = value.astype(jnp.bfloat16)
        act_ref[at, :] = value
        slope_ref[at, :] = slope.astype(jnp.bfloat16)
        acc[at, :] += halves(value, wd_ref[...], 1, 0)

    @pl.when(j == pl.num_programs(0) - 1)
    def _():
        sums_ref[...] = jnp.zeros_like(sums_ref)
        for at in row_blocks(rows):
            hidden = hidden_ref[at, :] + (acc[at, :] + bd_ref[...])
            centre = hidden - row_mean(hidden)
            scale_inv = lax.rsqrt(row_mean(centre * centre) + 1e-05)
            unit = centre * scale_inv
            result_ref[at, :] = (unit * gain_ref[...] + shift_ref[...]).astype(jnp.bfloat16)
            upstream = cot_ref[at, :].astype(jnp.float32)
            grad = norm_back(upstream, unit, scale_inv, gain_ref[...])
            grad_ref[at, :] = grad
            low_ref[at, :] = grad.astype(jnp.bfloat16)
            sums_ref[0:1, :] += column_sum(upstream * unit)
            sums_ref[1:2, :] += column_sum(upstream)
            sums_ref[2:3, :] += column_sum(grad)


HIDDEN_BLOCK = 512


def mlp_forward(x, wu, bu, wd, bd, hidden, gain, shift, cot):
    tokens, width = x.shape
    inner = wu.shape[1]
    block = HIDDEN_BLOCK
    full = lambda r, c: pl.BlockSpec((r, c), lambda j: (0, 0))
    across = pl.BlockSpec((tokens, block), lambda j: (0, j))
    return pl.pallas_call(
        mlp_fwd_kernel,
        grid=(inner // block,),
        in_specs=[
            full(tokens, width), pl.BlockSpec((width, block), lambda j: (0, j)), pl.BlockSpec((1, block), lambda j: (0, j)),
            pl.BlockSpec((block, width), lambda j: (j, 0)), full(1, width), full(tokens, width), full(1, width),
            full(1, width), full(tokens, width),
        ],
        out_specs=[across, across, full(tokens, width), full(tokens, width), full(tokens, width), full(8, width)],
        out_shape=[
            jax.ShapeDtypeStruct((tokens, inner), jnp.bfloat16), jax.ShapeDtypeStruct((tokens, inner), jnp.bfloat16),
            jax.ShapeDtypeStruct((tokens, width), jnp.bfloat16), jax.ShapeDtypeStruct((tokens, width), jnp.float32),
            jax.ShapeDtypeStruct((tokens, width), jnp.bfloat16), jax.ShapeDtypeStruct((8, width), jnp.float32),
        ],
        scratch_shapes=[pltpu.VMEM((tokens, width), jnp.float32)],
        compiler_params=pltpu.CompilerParams(vmem_limit_bytes=56 << 20),
        cost_estimate=pl.CostEstimate(flops=4 * tokens * width * inner, bytes_accessed=50_000_000, transcendentals=6_000_000),
        name="mlp_forward",
    )(x, wu, bu.reshape(1, -1), wd, bd.reshape(1, -1), hidden, gain.reshape(1, -1), shift.reshape(1, -1), cot)


def mlp_bwd_kernel(plan, low_ref, wd_ref, slope_ref, act_ref, x_ref, wu_ref, grad_ref, unit_ref, inv_ref, gain_ref,
                   up_ref, down_ref, bias_ref, two_ref, two_low_ref, sums_ref, result_ref, xt, acc, held, *scratch):
    j = pl.program_id(0)
    rows = x_ref.shape[0]
    comm = HeldComm(plan, [held], [result_ref], scratch)

    @pl.when(j == 0)
    def _():
        comm.barrier()
        acc[...] = jnp.zeros_like(acc)
        for c in range(0, x_ref.shape[1], TILE):
            xt[c : c + TILE, :] = x_ref[:, c : c + TILE].T

    grad = dot(low_ref[...], wd_ref[...], 1, 1).astype(jnp.bfloat16).astype(jnp.float32)
    grad = grad * slope_ref[...].astype(jnp.float32)
    bias_ref[...] = column_sum(grad)
    grad = grad.astype(jnp.bfloat16)
    acc[...] += dot(grad, wu_ref[...], 1, 1)
    up = dot(xt[...], grad, 1, 0).astype(jnp.bfloat16)

    @pl.when(j < plan.total)
    def _():
        held[lax.rem(j, 2)] = up.reshape(held.shape[1:])

    @pl.when(j >= plan.total)
    def _():
        up_ref[...] = up

    comm.step(j)
    down_ref[...] = dot(act_ref[...].T, low_ref[...], 1, 0).astype(jnp.bfloat16)

    @pl.when(j == pl.num_programs(0) - 1)
    def _():
        sums_ref[...] = jnp.zeros_like(sums_ref)
        for at in row_blocks(rows):
            upstream = grad_ref[at, :] + acc[at, :].astype(jnp.bfloat16).astype(jnp.float32)
            unit = unit_ref[at, :]
            two = norm_back(upstream, unit, inv_ref[at, :], gain_ref[...])
            two_ref[at, :] = two
            two_low_ref[at, :] = two.astype(jnp.bfloat16)
            sums_ref[0:1, :] += column_sum(upstream * unit)
            sums_ref[1:2, :] += column_sum(upstream)
        comm.rest(pl.num_programs(0))


def mlp_backward(plan, low, wd, slope, act, x, wu, grad, unit, inv, gain):
    tokens, width = x.shape
    inner = wu.shape[1]
    block = HIDDEN_BLOCK
    done = plan.total
    full = lambda r, c: pl.BlockSpec((r, c), lambda j: (0, 0))
    once = lambda r, c: pl.BlockSpec((r, c), lambda j: (0, 0), pipeline_mode=pl.Buffered(1))
    across = lambda r: pl.BlockSpec((r, block), lambda j: (0, j))
    down = pl.BlockSpec((block, width), lambda j: (j, 0))
    return pl.pallas_call(
        functools.partial(mlp_bwd_kernel, plan),
        grid=(inner // block,),
        in_specs=[
            once(tokens, width), down, across(tokens), across(tokens), once(tokens, width), across(width),
            once(tokens, width), once(tokens, width), once(tokens, 1), full(1, width),
        ],
        out_specs=[
            pl.BlockSpec((width, block), lambda j: (0, jnp.maximum(j - done, 0))), down, across(1),
            full(tokens, width), full(tokens, width), full(8, width),
        ] + plan.out_specs(),
        out_shape=[
            jax.ShapeDtypeStruct((width, inner - done * block), jnp.bfloat16), jax.ShapeDtypeStruct((inner, width), jnp.bfloat16),
            jax.ShapeDtypeStruct((1, inner), jnp.float32), jax.ShapeDtypeStruct((tokens, width), jnp.float32),
            jax.ShapeDtypeStruct((tokens, width), jnp.bfloat16), jax.ShapeDtypeStruct((8, width), jnp.float32),
        ] + plan.out_shapes(),
        scratch_shapes=[
            pltpu.VMEM((width, tokens), jnp.bfloat16), pltpu.VMEM((tokens, width), jnp.float32),
            pltpu.VMEM((2,) + (2,) * plan.route.bits + (plan.deep, block), jnp.bfloat16),
        ] + plan.scratch(),
        compiler_params=pltpu.CompilerParams(collective_id=plan.number, has_side_effects=True, vmem_limit_bytes=60 << 20),
        cost_estimate=pl.CostEstimate(flops=8 * tokens * width * inner, bytes_accessed=70_000_000, transcendentals=0),
        name="mlp_backward",
    )(low, wd, slope, act, x, wu, grad, unit, inv, gain.reshape(1, -1))


EARLY = 5


def normalize(hidden, gain, shift):
    centre = hidden - jnp.mean(hidden, axis=-1, keepdims=True)
    scale_inv = lax.rsqrt(jnp.mean(centre * centre, axis=-1, keepdims=True) + 1e-05)
    unit = centre * scale_inv
    return (unit * gain + shift, unit, scale_inv)


def normalize_back(upstream, unit, scale_inv, gain):
    along = upstream * gain
    inner = (
        along
        - jnp.mean(along, axis=-1, keepdims=True)
        - unit * jnp.mean(along * unit, axis=-1, keepdims=True)
    )
    return (scale_inv * inner, jnp.sum(upstream * unit, axis=0), jnp.sum(upstream, axis=0))


def gate(value, *others):
    return lax.optimization_barrier((value,) + others)[0]


def shards(
    inputs,
    encoded,
    target_lengths,
    source_lengths,
    query_key_value,
    bucket_weight,
    self_output,
    cross_query,
    cross_key_value,
    cross_output,
    up_weight,
    up_bias,
    down_weight,
    down_bias,
    norm_gain,
    norm_shift,
    cotangent,
):
    row_count, streams, local, width = inputs.shape
    parts, size = lax.axis_size("dp"), lax.axis_size("seq")
    route = Route(parts, size)
    full = local * size
    z = lax.axis_index("seq")
    begin = z * local
    bf16, f32 = jnp.bfloat16, jnp.float32
    tokens = streams * local
    up_chain = [(i, i + 1) for i in range(size - 1)]
    down_chain = [(i + 1, i) for i in range(size - 1)]

    def mm(left, right):
        return jnp.dot(left, right, preferred_element_type=f32)

    def mm_t(left, right):
        return lax.dot_general(left, right, (((1,), (1,)), ((), ())), preferred_element_type=f32)

    def wgrad(left, right):
        return dot(left, right, 0, 0).astype(bf16)

    flat = inputs.reshape(tokens, width)
    main = flat[:local]
    hops = HALO // local
    passing, pieces = main, []
    for _ in range(hops):
        passing = lax.ppermute(passing, "seq", up_chain)
        pieces.insert(0, passing)
    halo = jnp.concatenate(pieces, axis=0)
    extended = jnp.concatenate([halo, flat], axis=0)
    own_source = encoded.reshape(local, width)
    waiting, halo = lax.optimization_barrier((own_source, halo))
    sources = [own_source] + [
        lax.ppermute(waiting, "seq", [(i, (i + k) % size) for i in range(size)]) for k in range(1, size)
    ]
    source = jnp.concatenate(sources, axis=0)

    here = begin + jnp.arange(local, dtype=jnp.int32)
    ends = jnp.cumsum(target_lengths[0])
    source_ends = jnp.cumsum(source_lengths[0])
    passed = here[:, None] >= ends[None, :]
    number = jnp.sum(passed.astype(jnp.int32), axis=1)
    start = jnp.max(jnp.where(passed, ends[None, :], 0), axis=1) - begin + HALO
    is_doc = number[:, None] == jnp.arange(ends.shape[0] + 1, dtype=jnp.int32)[None, :]
    zero = jnp.zeros((1,), jnp.int32)
    first = jnp.sum(jnp.where(is_doc, jnp.concatenate([zero, source_ends])[None, :], 0), axis=1)
    last = jnp.sum(jnp.where(is_doc, jnp.concatenate([source_ends, zero + full])[None, :], 0), axis=1)
    edge = start[::TILE]
    at = HALO + TILE * jnp.arange(local // TILE, dtype=jnp.int32)
    need = 1 + (edge < at - TILE).astype(jnp.int32) + (edge < at - 3 * TILE).astype(jnp.int32)
    low_key = first[::TILE] // PAIR
    count = (last[TILE - 1 :: TILE] + PAIR - 1) // PAIR - low_key

    names = jnp.arange(TILE, dtype=jnp.int32)[None, :]
    place = begin - HALO + jnp.arange(HALO + local, dtype=jnp.int32)
    key_doc = jnp.where(place >= 0, jnp.sum((place[:, None] >= ends[None, :]).astype(jnp.int32), axis=1), TILE)
    place = jnp.arange(full, dtype=jnp.int32)
    source_doc = jnp.sum((place[:, None] >= source_ends[None, :]).astype(jnp.int32), axis=1)
    doc = (number[:, None] == names).astype(bf16)
    block = lambda of: jnp.where((names < 8) & (of[:, None] != names), NEG, 0.0).astype(bf16)
    target_aug, source_aug = block(key_doc), block(source_doc)
    skew, hot = bias_tables()

    query_main = mm(flat, query_key_value).astype(bf16)
    relative = mm(flat, bucket_weight)
    proj = query_main
    halo_kv = mm(halo, query_key_value[:, width:]).astype(bf16)
    self_mix, self_weights = self_forward(need, proj, halo_kv, relative, doc, target_aug, skew)
    hidden_one, unit_one, inv_one = normalize(flat.astype(f32) + mm(self_mix, self_output), norm_gain[0], norm_shift[0])
    low_one = hidden_one.astype(bf16)
    cross_q = mm(low_one, cross_query).astype(bf16)
    source_kv = mm(source, cross_key_value).astype(bf16)
    cross_mix, cross_weights = cross_forward(low_key, count, cross_q, source_kv, doc, source_aug)
    hidden_two, unit_two, inv_two = normalize(hidden_one + mm(cross_mix, cross_output), norm_gain[1], norm_shift[1])
    low_two = hidden_two.astype(bf16)
    activated, slope, result, three_grad, three_low, three_sums = mlp_forward(
        low_two, up_weight, up_bias, down_weight, down_bias, hidden_two, norm_gain[2], norm_shift[2],
        cotangent.reshape(tokens, width),
    )
    gain_three, shift_three, down_bias_grad = three_sums[0], three_sums[1], three_sums[2]

    early = (width, EARLY * HIDDEN_BLOCK)
    early_plan = Plan(route, [early], 3)
    up_part, down_part, up_bias_grad, two_grad, two_low, two_sums, up_early = mlp_backward(
        early_plan, three_low, down_weight, slope, activated, low_two, up_weight, three_grad, unit_two, inv_two, norm_gain[1]
    )
    gain_two, shift_two = two_sums[0], two_sums[1]
    up_bias_grad = up_bias_grad.reshape(-1)
    cross_up = mm_t(two_low, cross_output).astype(bf16)
    wide = [up_part, down_part]
    wide_plan = Plan(route, [a.shape for a in wide], 0)
    query_low, source_low, up_late, down_grad = cross_backward(
        wide_plan, wide, cross_q, source_kv, cross_mix, cross_up, cross_weights
    )
    up_grad = jnp.concatenate([up_early, up_late], axis=1)
    source_back = mm_t(source_low, cross_key_value).astype(bf16)
    far = size // 2
    shifts = [k for k in range(1, size) if k != far]
    block = lambda k: source_back[k * local : (k + 1) * local]
    hidden_one_grad = two_grad + mm_t(query_low, cross_query).astype(bf16).astype(f32)
    one_grad, gain_one, shift_one = normalize_back(hidden_one_grad, unit_one, inv_one, norm_gain[0])
    one_low = one_grad.astype(bf16)
    self_up = mm_t(one_low, self_output).astype(bf16)
    square = [
        wgrad(source, source_low),
        wgrad(cross_mix, two_low),
        wgrad(low_one, query_low),
        wgrad(self_mix, one_low),
    ]
    square_plan = Plan(route, [a.shape for a in square], 1)
    query_low, kv_low, table_low, back, came, *square_sums = self_backward(
        square_plan, square, shifts, jnp.stack([block(k) for k in shifts]), proj, halo_kv, hot, self_mix, self_up, self_weights,
        query_key_value, bucket_weight,
    )
    cross_kv_grad, cross_out_grad, cross_query_grad, self_out_grad = square_sums
    returned = []
    for k in range(1, hops + 1):
        piece = back[HALO - k * local : HALO - (k - 1) * local]
        returned.append(lax.ppermute(piece, "seq", [(i, i - k) for i in range(k, size)]))
    back = back[HALO:].astype(f32).reshape(streams, local, width)
    passing = sum(got.astype(f32) for got in returned)
    back = jnp.concatenate([back[:1] + passing[None], back[1:]], axis=0).reshape(tokens, width)
    inputs_grad = (one_grad + back.astype(bf16).astype(f32)).astype(bf16)
    devices = parts * size
    gains = jnp.stack([gain_one, gain_two, gain_three]).reshape(3, devices, -1).transpose(1, 0, 2)
    shifts = jnp.stack([shift_one, shift_two, shift_three]).reshape(3, devices, -1).transpose(1, 0, 2)
    each = width // devices
    small = jnp.concatenate(
        [
            up_bias_grad.reshape(devices, -1),
            down_bias_grad.reshape(devices, -1),
            gains.reshape(devices, -1),
            shifts.reshape(devices, -1),
        ],
        axis=1,
    )
    used = small.shape[1]
    small = jnp.pad(small, ((0, 0), (0, 16 * TILE - used))).reshape(devices * 8, 2 * TILE)
    arrays = [
        wgrad(flat, query_low),
        wgrad(extended, kv_low),
        wgrad(flat, gate(table_low, inputs_grad)),
    ]
    plan = Plan(route, [a.shape for a in arrays], 2, [(0, 0), (0, width), (1, 0)])
    few = Plan(route, [small.shape], 2, chunk=TILE, kind=f32)
    qkv_grad, bucket_grad, small, last_came = scatter_sums(plan, few, [far], arrays, small, block(far)[None])
    encoded_grad = source_back[:local].astype(f32) + jnp.sum(came.astype(f32), axis=0) + last_came[0].astype(f32)
    small = small.reshape(-1)
    wide_each = up_bias_grad.shape[0] // devices
    cuts = [wide_each, wide_each + each, wide_each + 4 * each, used]
    up_bias_grad, down_bias_grad, gains, shifts, _ = jnp.split(small, cuts)
    return (
        result.reshape(inputs.shape),
        inputs_grad.reshape(inputs.shape),
        encoded_grad.astype(bf16).reshape(encoded.shape),
        qkv_grad,
        bucket_grad,
        self_out_grad,
        cross_query_grad,
        cross_kv_grad,
        cross_out_grad,
        up_grad,
        up_bias_grad,
        down_grad,
        down_bias_grad,
        gains.reshape(3, each),
        shifts.reshape(3, each),
    )


def solution(mesh):
    placed = (
        P("dp", None, "seq", None),
        P("dp", "seq", None),
        P("dp", None),
        P("dp", None),
        P(),
        P(),
        P(),
        P(),
        P(),
        P(),
        P(),
        P(),
        P(),
        P(),
        P(),
        P(),
        P("dp", None, "seq", None),
    )
    return jax.shard_map(
        shards,
        mesh=mesh,
        in_specs=placed,
        out_specs=(
            P("dp", None, "seq", None),
            P("dp", None, "seq", None),
            P("dp", "seq", None),
            P(("dp", "seq"), None),
            P(("dp", "seq"), None),
            P(("dp", "seq"), None),
            P(("dp", "seq"), None),
            P(("dp", "seq"), None),
            P(("dp", "seq"), None),
            P(("dp", "seq"), None),
            P(("dp", "seq")),
            P(("dp", "seq"), None),
            P(("dp", "seq")),
            P(None, ("dp", "seq")),
            P(None, ("dp", "seq")),
        ),
        check_vma=False,
    )
```

```python
import functools
import math

import jax
import jax.numpy as jnp
from jax import lax
from jax.experimental import pallas as pl
from jax.experimental.pallas import tpu as pltpu
from jax.sharding import PartitionSpec as P

HEAD_DIM = 64
BUCKETS = 32
STREAMS = 3
HALO = 512
TILE = 128
PAIR = 2 * TILE
ROWS = 2 * STREAMS * TILE
NEG = -1e30
SCALE = HEAD_DIM ** (-0.5)

bucket_edges = [
    int(math.ceil(16.0 * 8.0 ** (bucket_level / 16.0))) for bucket_level in range(1, 16)
]


def bucket_of(distance):
    forward_gap = jnp.maximum(distance, 0)
    far_bucket = jnp.full_like(forward_gap, 16)
    for bucket_edge in bucket_edges:
        far_bucket = far_bucket + (forward_gap >= bucket_edge).astype(jnp.int32)
    return jnp.where(forward_gap < 16, forward_gap, far_bucket)


def iota(shape, axis):
    return lax.broadcasted_iota(jnp.int32, shape, axis)


def dot(a, b, ca, cb):
    return lax.dot_general(a, b, (((ca,), (cb,)), ((), ())), preferred_element_type=jnp.float32)


def bias_tables():
    col = iota((PAIR, PAIR), 1)
    gap = jnp.where(col < TILE, (TILE - col) % TILE, PAIR)
    row = iota((PAIR, PAIR), 0) % TILE
    back = TILE - 1 - iota((TILE, TILE), 0)
    lane = iota((TILE, TILE), 1)
    skews = [(bucket_of(gap) + BUCKETS * h == row).astype(jnp.bfloat16) for h in range(4)]
    hots = [(bucket_of(back) + BUCKETS * h == lane).astype(jnp.bfloat16) for h in range(4)]
    return jnp.concatenate(skews, axis=0), jnp.concatenate(hots, axis=0)


def halves(a, b, ca, cb):
    half = a.shape[0] // 2
    return jnp.concatenate([dot(a[:half], b, ca, cb), dot(a[half:], b, ca, cb)], axis=0)


def head_masks():
    low = (iota((TILE, TILE), 1) < HEAD_DIM).astype(jnp.float32)
    return low.astype(jnp.bfloat16), (1.0 - low).astype(jnp.bfloat16)


def stream_rows(s, local, here):
    return pl.ds(pl.multiple_of(s * local + here, TILE), TILE)


def stack_heads(ref, local, here, lanes, masks, extra=None, scale=None):
    out = []
    for s in range(STREAMS):
        x = ref[stream_rows(s, local, here), lanes]
        if scale is not None:
            x = x * jnp.bfloat16(scale)
        for mask in masks:
            y = x * mask
            out.append(y if extra is None else jnp.concatenate([y, extra], axis=1))
    return jnp.concatenate(out, axis=0)


def part(n):
    return slice(n * TILE, (n + 1) * TILE)


def lane_max(x):
    return jnp.broadcast_to(jnp.max(x, axis=1, keepdims=True), (TILE, TILE))


def lane_sum(x):
    return jnp.broadcast_to(jnp.sum(x, axis=1, keepdims=True), (TILE, TILE))


def roll_rows(x):
    return pltpu.roll(x, 0, 1, stride=1, stride_axis=0)


REACH = HALO + TILE
FIRST = (3 * TILE, TILE, 0)


def columns(rows, base):
    return pl.BlockSpec((rows, PAIR), lambda g, *_: (0, base + g))


def whole(rows, cols):
    return pl.BlockSpec((rows, cols), lambda g, *_: (0, 0))


def weights_spec(steps, reach):
    return pl.BlockSpec((1, steps, ROWS, reach), lambda g, *_: (g, 0, 0, 0))


def self_fwd_kernel(nq, need_ref, q_ref, ko_ref, vo_ref, kh_ref, vh_ref, rel_ref, doc_ref, aug_ref, skew_ref,
                    mix_ref, pr_ref, kx, vx, sc, st, bz):
    local = nq * TILE
    for p in range(2):
        kx[p, :HALO, :TILE] = kh_ref[:, part(p)]
        kx[p, HALO:, :TILE] = ko_ref[:local, part(p)]
        kx[p, :, TILE:] = aug_ref[...]
    vx[:HALO, :] = vh_ref[...]
    vx[HALO:, :] = vo_ref[:local, :]
    masks = head_masks()
    lane = iota((TILE, TILE), 1)
    row = iota((TILE, TILE), 0)

    def step(n, _):
        i, p = n // 2, n % 2
        here = pl.multiple_of(i * TILE, TILE)
        lanes = pl.ds(pl.multiple_of(p * TILE, TILE), TILE)
        qs = stack_heads(q_ref, local, here, lanes, masks, doc_ref[pl.ds(here, TILE), :], SCALE)
        table = []
        for s in range(STREAMS):
            rel = rel_ref[stream_rows(s, local, here), :]
            high = rel.astype(jnp.bfloat16)
            table.append(jnp.concatenate([high, (rel - high.astype(jnp.float32)).astype(jnp.bfloat16)], axis=1))
        table = jnp.concatenate(table, axis=0)
        for j in range(2):
            bz[j, :, :] = halves(table, skew_ref[pl.ds(pl.multiple_of((2 * p + j) * PAIR, PAIR), PAIR), :], 1, 0)

        def path(count):
            first = FIRST[count - 1]
            keys = pl.ds(pl.multiple_of(here + first, TILE), REACH - first)
            sc[:, first:] = halves(qs, kx[p, keys, :], 1, 1)
            acc, tiles = [], []
            for b in range(2 * STREAMS):
                s, j = b // 2, b % 2
                rows = stream_rows(s, local, here)
                near = roll_rows(bz[j, part(s), :TILE])
                steady = bz[j, part(s), TILE:]
                left = sc[part(b), part(3)] + jnp.where(lane > row, near, steady)
                right = sc[part(b), part(4)]
                if s > 0:
                    own = lane_sum(qs[part(b), :TILE].astype(jnp.float32) * ko_ref[rows, lanes].astype(jnp.float32))
                    right = jnp.where(lane == row, own, right)
                right = right + jnp.where(lane <= row, near, NEG)
                far = [sc[part(b), part(m)] for m in range(first // TILE, 3)]
                top = jnp.maximum(left, right)
                if far:
                    most = far[0]
                    for x in far[1:]:
                        most = jnp.maximum(most, x)
                    top = jnp.maximum(top, most + steady)
                top = lane_max(top)
                base = top - steady
                weights = [jnp.exp(x - base) for x in far] + [jnp.exp(left - top), jnp.exp(right - top)]
                total = weights[0]
                for x in weights[1:]:
                    total = total + x
                inverse = 1.0 / lane_sum(total)
                weights = [(x * inverse).astype(jnp.bfloat16) for x in weights]
                tiles.append(jnp.concatenate(weights, axis=1))
                for m, x in enumerate(weights, first // TILE):
                    pr_ref[0, n, part(b), part(m)] = x
                    if m == 4 and s > 0:
                        st[part(b), :] = lane_sum(jnp.where(lane == row, x.astype(jnp.float32), 0.0))
                acc.append(dot(tiles[b], vx[keys, lanes], 1, 0))
            if first:
                pr_ref[0, n, :, :first] = jnp.zeros((ROWS, first), jnp.bfloat16)
            main = vo_ref[stream_rows(0, local, here), lanes].astype(jnp.float32)
            for s in range(STREAMS):
                rows = stream_rows(s, local, here)
                a, b = part(2 * s), part(2 * s + 1)
                mixed = jnp.where(lane < HEAD_DIM, acc[2 * s], acc[2 * s + 1])
                if s > 0:
                    own = jnp.where(lane < HEAD_DIM, st[a, :], st[b, :])
                    mixed = mixed + own * (vo_ref[rows, lanes].astype(jnp.float32) - main)
                mix_ref[rows, lanes] = mixed.astype(jnp.bfloat16)

        for count in range(1, 4):
            @pl.when(need_ref[i] == count)
            def _():
                path(count)
        return 0

    lax.fori_loop(0, 2 * nq, step, 0)


def self_forward(need, proj, halo_kv, rel, doc, aug, skew):
    tokens = proj.shape[0]
    local = tokens // STREAMS
    width = proj.shape[1] // 3
    grid = width // PAIR
    steps = 2 * local // TILE
    return pl.pallas_call(
        functools.partial(self_fwd_kernel, local // TILE),
        grid_spec=pltpu.PrefetchScalarGridSpec(
            num_scalar_prefetch=1, grid=(grid,),
            in_specs=[
                columns(tokens, 0), columns(tokens, grid), columns(tokens, 2 * grid), columns(HALO, 0), columns(HALO, grid),
                pl.BlockSpec((tokens, TILE), lambda g, *_: (0, g)),
                whole(local, TILE), whole(HALO + local, TILE), whole(4 * PAIR, PAIR),
            ],
            out_specs=[columns(tokens, 0), weights_spec(steps, REACH)],
            scratch_shapes=[
                pltpu.VMEM((2, HALO + local, PAIR), jnp.bfloat16), pltpu.VMEM((HALO + local, PAIR), jnp.bfloat16),
                pltpu.VMEM((ROWS, REACH), jnp.float32), pltpu.VMEM((ROWS, TILE), jnp.float32),
                pltpu.VMEM((2, STREAMS * TILE, PAIR), jnp.float32),
            ]),
        out_shape=[jax.ShapeDtypeStruct((tokens, width), jnp.bfloat16),
                   jax.ShapeDtypeStruct((grid, steps, ROWS, REACH), jnp.bfloat16)],
        compiler_params=pltpu.CompilerParams(vmem_limit_bytes=40 << 20),
        cost_estimate=pl.CostEstimate(flops=15_000_000_000, bytes_accessed=20_000_000, transcendentals=8_000_000),
        name="self_forward",
    )(need, proj, proj, proj, halo_kv, halo_kv, rel, doc, aug, skew)


def self_bwd_kernel(nq, plan, shifts, q_ref, ko_ref, vo_ref, kh_ref, vh_ref, hot_ref, mix_ref, up_ref, pr_ref,
                    wq_ref, wk_ref, wv_ref, wb_ref, *refs):
    arrays, handed, refs = refs[: plan.many], refs[plan.many], refs[plan.many + 1 :]
    (dq_ref, dkv_ref, drel_ref, back_ref, got), refs = refs[:5], refs[5:]
    outs = len(plan.out_shapes())
    results, (kx, vx, dp, ds, cb, st, dkt, dvt, cv, acc), scratch = refs[:outs], refs[outs : outs + 10], refs[outs + 10 :]
    g = pl.program_id(0)
    comm = Comm(plan, arrays, results, scratch[:-1])
    hand = Handing(shifts, 8 * nq, handed, got, scratch[-1])

    @pl.when(g == 0)
    def _():
        comm.barrier()

    local = nq * TILE
    kx[:HALO, :] = kh_ref[...]
    kx[HALO:, :] = ko_ref[:local, :]
    vx[:HALO, :] = vh_ref[...]
    vx[HALO:, :] = vo_ref[:local, :]
    dkt[...] = jnp.zeros_like(dkt)
    dvt[...] = jnp.zeros_like(dvt)
    masks = head_masks()
    lane = iota((TILE, TILE), 1)
    row = iota((TILE, TILE), 0)
    flip = (row + lane == TILE - 1).astype(jnp.float32).astype(jnp.bfloat16)
    gl = pl.multiple_of(g * PAIR, PAIR)
    third = q_ref.shape[1] * pl.num_programs(0)

    def step(n, _):
        i, p = n // 2, n % 2
        here = pl.multiple_of(i * TILE, TILE)
        lanes = pl.ds(pl.multiple_of(p * TILE, TILE), TILE)
        hand.step(g * 2 * nq + n)
        comm.step(g * 2 * nq + n)
        qs = stack_heads(q_ref, local, here, lanes, masks, None, SCALE)
        ups = stack_heads(up_ref, local, here, lanes, masks)
        qt = qs.T
        upt = ups.T

        keys = pl.ds(pl.multiple_of(here, TILE), REACH)
        dp[...] = halves(ups, vx[keys, lanes], 1, 1)
        for b in range(2 * STREAMS):
            s = b // 2
            rows = stream_rows(s, local, here)
            upf = ups[part(b)].astype(jnp.float32)
            centre = lane_sum(upf * mix_ref[rows, lanes].astype(jnp.float32))
            xs = [pr_ref[0, n, part(b), part(m)].astype(jnp.float32) for m in range(5)]
            ys = [(xs[m] * (dp[part(b), part(m)] - centre)).astype(jnp.bfloat16) for m in range(5)]
            for m in range(4):
                ds[part(b), part(m)] = ys[m]
            ys = [y.astype(jnp.float32) for y in ys]
            band = jnp.where(lane > row, ys[3], 0.0)
            st[2, part(b), :] = ys[0] + ys[1] + ys[2] + (ys[3] - band)
            if s > 0:
                own_weight = lane_sum(jnp.where(lane == row, xs[4], 0.0))
                own_grad = own_weight * (lane_sum(upf * vo_ref[rows, lanes].astype(jnp.float32)) - centre)
                own_grad = own_grad.astype(jnp.bfloat16).astype(jnp.float32)
                st[0, part(b), :] = own_weight
                st[1, part(b), :] = own_grad
                band = band + jnp.where(lane == row, own_grad, ys[4])
                ds[part(b), part(4)] = jnp.where(lane == row, 0.0, ys[4]).astype(jnp.bfloat16)
            else:
                band = band + ys[4]
                ds[part(b), part(4)] = ys[4].astype(jnp.bfloat16)
            cb[:, part(b)] = band.astype(jnp.bfloat16)
        dkt[p, :, keys] += dot(qt, ds[...], 1, 0)
        dvt[p, :, keys] += dot(upt, pr_ref[0, n], 1, 0)
        dq = dot(ds[...], kx[keys, lanes], 1, 0)
        turned = dot(flip, cb[...], 1, 0)
        rolled = [roll_rows(turned[:, part(b)]).astype(jnp.bfloat16) for b in range(2 * STREAMS)]
        rolled = jnp.concatenate([jnp.concatenate(rolled[2 * s : 2 * s + 2], axis=1) for s in range(STREAMS)], axis=0)
        table = dot(rolled, hot_ref[pl.ds(pl.multiple_of(p * PAIR, PAIR), PAIR), :], 1, 0).astype(jnp.bfloat16)
        table = dot(flip, jnp.concatenate([table[part(s)] for s in range(STREAMS)], axis=1), 1, 0)

        excess = None
        for s in range(STREAMS):
            rows = stream_rows(s, local, here)
            a, b = part(2 * s), part(2 * s + 1)
            dqs = jnp.where(lane < HEAD_DIM, dq[a], dq[b])
            col = pl.multiple_of(gl + p * TILE, TILE)
            kept = pl.ds(pl.multiple_of(HALO + s * local + here, TILE), TILE)
            if s > 0:
                own_weight = jnp.where(lane < HEAD_DIM, st[0, a, :], st[0, b, :])
                own_grad = jnp.where(lane < HEAD_DIM, st[1, a, :], st[1, b, :])
                dqs = dqs + own_grad * ko_ref[rows, lanes].astype(jnp.float32)
                own_value = own_weight * up_ref[rows, lanes].astype(jnp.float32)
                excess = own_value if excess is None else excess + own_value
                dkv_ref[kept, pl.ds(col, TILE)] = (
                    own_grad * (SCALE * q_ref[rows, lanes].astype(jnp.float32))
                ).astype(jnp.bfloat16)
                dkv_ref[kept, pl.ds(pl.multiple_of(col + third, TILE), TILE)] = own_value.astype(jnp.bfloat16)
            dq_ref[rows, lanes] = (SCALE * dqs).astype(jnp.bfloat16)
            dr = table[:, part(s)]
            for j, blk in enumerate((a, b)):
                dr = dr + jnp.where(lane == BUCKETS * (2 * p + j) + BUCKETS - 1, lane_sum(st[2, blk, :]), 0.0)

            @pl.when(p == 0)
            def _():
                drel_ref[rows, :] = dr.astype(jnp.bfloat16)

            @pl.when(p == 1)
            def _():
                drel_ref[rows, :] = (drel_ref[rows, :].astype(jnp.float32) + dr).astype(jnp.bfloat16)
        cv[pl.ds(here, TILE), lanes] = excess
        return 0

    lax.fori_loop(0, 2 * nq, step, 0)
    for p in range(2):
        for j, grads in enumerate((dkt, dvt)):
            col = pl.multiple_of(gl + p * TILE + third * j, TILE)
            full = grads[p, :, :].T
            main = full[HALO:] if j == 0 else full[HALO:] - cv[:, part(p)]
            dkv_ref[:HALO, pl.ds(col, TILE)] = full[:HALO].astype(jnp.bfloat16)
            dkv_ref[HALO : HALO + local, pl.ds(col, TILE)] = main.astype(jnp.bfloat16)

    @pl.when(g == 0)
    def _():
        acc[...] = jnp.zeros_like(acc)

    rows = acc.shape[0]
    for r in range(0, rows, PAIR):
        at = slice(r, r + PAIR)
        part_sum = dot(dkv_ref[at, pl.ds(gl, PAIR)], wk_ref[...], 1, 1)
        part_sum = part_sum + dot(dkv_ref[at, pl.ds(pl.multiple_of(gl + third, PAIR), PAIR)], wv_ref[...], 1, 1)
        if r >= HALO:
            own = slice(r - HALO, r - HALO + PAIR)
            part_sum = part_sum + dot(dq_ref[own, :], wq_ref[...], 1, 1) + dot(drel_ref[own, :], wb_ref[...], 1, 1)
        acc[at, :] += part_sum

    @pl.when(g == pl.num_programs(0) - 1)
    def _():
        back_ref[...] = acc[...].astype(jnp.bfloat16)
        comm.rest(4 * 2 * nq)
        hand.finish()


def self_backward(plan, arrays, shifts, handed, proj, halo_kv, hot, mix, up, weights, qkv, bucket):
    tokens = proj.shape[0]
    local = tokens // STREAMS
    width = proj.shape[1] // 3
    grid = width // PAIR
    steps = 2 * local // TILE
    return pl.pallas_call(
        functools.partial(self_bwd_kernel, local // TILE, plan, shifts),
        grid=(grid,),
        in_specs=[
            columns(tokens, 0), columns(tokens, grid), columns(tokens, 2 * grid), columns(HALO, 0), columns(HALO, grid),
            whole(4 * TILE, TILE), columns(tokens, 0), columns(tokens, 0), weights_spec(steps, REACH),
            columns(width, 0), columns(width, grid), columns(width, 2 * grid), pl.BlockSpec((width, TILE), lambda g, *_: (0, g)),
        ] + plan.in_specs() + [pl.BlockSpec(memory_space=pl.ANY)],
        out_specs=[
            columns(tokens, 0), whole(HALO + tokens, 2 * width), pl.BlockSpec((tokens, TILE), lambda g, *_: (0, g)),
            whole(HALO + tokens, width), pl.BlockSpec(memory_space=pl.ANY),
        ] + plan.out_specs(),
        scratch_shapes=[
            pltpu.VMEM((HALO + local, PAIR), jnp.bfloat16), pltpu.VMEM((HALO + local, PAIR), jnp.bfloat16),
            pltpu.VMEM((ROWS, REACH), jnp.float32), pltpu.VMEM((ROWS, REACH), jnp.bfloat16),
            pltpu.VMEM((TILE, ROWS), jnp.bfloat16), pltpu.VMEM((3, ROWS, TILE), jnp.float32),
            pltpu.VMEM((2, TILE, HALO + local), jnp.float32), pltpu.VMEM((2, TILE, HALO + local), jnp.float32),
            pltpu.VMEM((local, PAIR), jnp.float32), pltpu.VMEM((HALO + tokens, width), jnp.float32),
        ] + plan.scratch() + handing_scratch(len(shifts), 8 * local // TILE),
        out_shape=[
            jax.ShapeDtypeStruct((tokens, width), jnp.bfloat16), jax.ShapeDtypeStruct((HALO + tokens, 2 * width), jnp.bfloat16),
            jax.ShapeDtypeStruct((tokens, width // 2), jnp.bfloat16),
            jax.ShapeDtypeStruct((HALO + tokens, width), jnp.bfloat16), jax.ShapeDtypeStruct(handed.shape, handed.dtype),
        ] + plan.out_shapes(),
        compiler_params=pltpu.CompilerParams(collective_id=plan.number, has_side_effects=True, vmem_limit_bytes=62 << 20),
        cost_estimate=pl.CostEstimate(flops=40_000_000_000, bytes_accessed=30_000_000, transcendentals=8_000_000),
        name="self_backward",
    )(proj, proj, proj, halo_kv, halo_kv, hot, mix, up, weights, qkv, qkv, qkv, bucket, *plan.views(arrays), handed)


def gather_shards(local, ref, place):
    shards = ref.shape[0] // local
    z = lax.axis_index("seq")
    for k in range(shards):
        at = pl.ds(pl.multiple_of(lax.rem(z - k + shards, shards) * local, TILE), local)
        place(at, ref[k * local : (k + 1) * local, :])


def cross_fwd_kernel(nq, lo_ref, count_ref, q_ref, k_ref, v_ref, doc_ref, aug_ref, mix_ref, pr_ref, kx, vx, sc):
    local = nq * TILE
    across = k_ref.shape[0] // PAIR

    def place_key(at, block):
        for p in range(2):
            kx[p, at, :TILE] = block[:, part(p)]

    def place_value(at, block):
        vx[at, :] = block

    gather_shards(local, k_ref, place_key)
    gather_shards(local, v_ref, place_value)
    for p in range(2):
        kx[p, :, TILE:] = aug_ref[...]
    masks = head_masks()
    lane = iota((TILE, TILE), 1)

    def step(n, _):
        i, p = n // 2, n % 2
        here = pl.multiple_of(i * TILE, TILE)
        lanes = pl.ds(pl.multiple_of(p * TILE, TILE), TILE)
        qs = stack_heads(q_ref, local, here, lanes, masks, doc_ref[pl.ds(here, TILE), :], SCALE)

        def window(w):
            return pl.ds(pl.multiple_of((lo_ref[i] + w) * PAIR, PAIR), PAIR)

        def path(count):
            keys = pl.ds(pl.multiple_of(lo_ref[i] * PAIR, PAIR), count * PAIR)
            sc[:, : count * PAIR] = halves(qs, kx[p, keys, :], 1, 1)
            total_of = []
            for b in range(2 * STREAMS):
                xs = [sc[part(b), part(m)] for m in range(2 * count)]
                top = xs[0]
                for x in xs[1:]:
                    top = jnp.maximum(top, x)
                top = lane_max(top)
                xs = [jnp.exp(x - top) for x in xs]
                total = xs[0]
                for x in xs[1:]:
                    total = total + x
                inverse = 1.0 / lane_sum(total)
                xs = [(x * inverse).astype(jnp.bfloat16) for x in xs]
                for w in range(count):
                    pr_ref[0, n, part(b), window(w)] = jnp.concatenate(xs[2 * w : 2 * w + 2], axis=1)
                total_of.append(dot(jnp.concatenate(xs, axis=1), vx[keys, lanes], 1, 0))
            for s in range(STREAMS):
                mixed = jnp.where(lane < HEAD_DIM, total_of[2 * s], total_of[2 * s + 1])
                mix_ref[stream_rows(s, local, here), lanes] = mixed.astype(jnp.bfloat16)

        for count in range(1, across + 1):
            @pl.when(count_ref[i] == count)
            def _():
                path(count)

        for w in range(across):
            @pl.when((w < lo_ref[i]) | (w >= lo_ref[i] + count_ref[i]))
            def _():
                pr_ref[0, n, :, w * PAIR : (w + 1) * PAIR] = jnp.zeros((ROWS, PAIR), jnp.bfloat16)
        return 0

    lax.fori_loop(0, 2 * nq, step, 0)


def cross_forward(lo, count, q, kv, doc, aug):
    tokens, width = q.shape
    local = tokens // STREAMS
    full = kv.shape[0]
    grid = width // PAIR
    steps = 2 * local // TILE
    return pl.pallas_call(
        functools.partial(cross_fwd_kernel, local // TILE),
        grid_spec=pltpu.PrefetchScalarGridSpec(
            num_scalar_prefetch=2, grid=(grid,),
            in_specs=[columns(tokens, 0), columns(full, 0), columns(full, grid), whole(local, TILE), whole(full, TILE)],
            out_specs=[columns(tokens, 0), weights_spec(steps, full)],
            scratch_shapes=[
                pltpu.VMEM((2, full, PAIR), jnp.bfloat16), pltpu.VMEM((full, PAIR), jnp.bfloat16),
                pltpu.VMEM((ROWS, full), jnp.float32),
            ]),
        out_shape=[jax.ShapeDtypeStruct((tokens, width), jnp.bfloat16), jax.ShapeDtypeStruct((grid, steps, ROWS, full), jnp.bfloat16)],
        compiler_params=pltpu.CompilerParams(vmem_limit_bytes=48 << 20),
        cost_estimate=pl.CostEstimate(flops=15_000_000_000, bytes_accessed=20_000_000, transcendentals=8_000_000),
        name="cross_forward",
    )(lo, count, q, kv, kv, doc, aug)


def cross_bwd_kernel(nq, plan, q_ref, k_ref, v_ref, mix_ref, up_ref, pr_ref, *refs):
    arrays, (dq_ref, dkv_ref), refs = refs[: plan.many], refs[plan.many : plan.many + 2], refs[plan.many + 2 :]
    outs = len(plan.out_shapes())
    results, (kx, vx, dp, ds, st, dkt, dvt), scratch = refs[:outs], refs[outs : outs + 7], refs[outs + 7 :]
    g = pl.program_id(0)
    comm = Comm(plan, arrays, results, scratch)

    @pl.when(g == 0)
    def _():
        comm.barrier()

    local = nq * TILE

    def place_key(at, block):
        kx[at, :] = block

    def place_value(at, block):
        vx[at, :] = block

    gather_shards(local, k_ref, place_key)
    gather_shards(local, v_ref, place_value)
    dkt[...] = jnp.zeros_like(dkt)
    dvt[...] = jnp.zeros_like(dvt)
    masks = head_masks()
    lane = iota((TILE, TILE), 1)

    def step(n, _):
        i, p = n // 2, n % 2
        here = pl.multiple_of(i * TILE, TILE)
        lanes = pl.ds(pl.multiple_of(p * TILE, TILE), TILE)
        comm.step(g * 2 * nq + n)
        qs = stack_heads(q_ref, local, here, lanes, masks, None, SCALE)
        ups = stack_heads(up_ref, local, here, lanes, masks)
        qt = qs.T
        upt = ups.T
        for b in range(2 * STREAMS):
            rows = stream_rows(b // 2, local, here)
            st[part(b), :] = lane_sum(ups[part(b)].astype(jnp.float32) * mix_ref[rows, lanes].astype(jnp.float32))
        dp[...] = halves(ups, vx[:, lanes], 1, 1)
        for b in range(2 * STREAMS):
            for m in range(dp.shape[1] // TILE):
                x = pr_ref[0, n, part(b), part(m)].astype(jnp.float32)
                ds[part(b), part(m)] = (x * (dp[part(b), part(m)] - st[part(b), :])).astype(jnp.bfloat16)
        dkt[p, :, :] += dot(qt, ds[...], 1, 0)
        dvt[p, :, :] += dot(upt, pr_ref[0, n], 1, 0)
        dqa = dot(ds[...], kx[:, lanes], 1, 0)
        for s in range(STREAMS):
            dq = jnp.where(lane < HEAD_DIM, dqa[part(2 * s)], dqa[part(2 * s + 1)])
            dq_ref[stream_rows(s, local, here), lanes] = (SCALE * dq).astype(jnp.bfloat16)
        return 0

    lax.fori_loop(0, 2 * nq, step, 0)
    third = q_ref.shape[1] * pl.num_programs(0)
    shards = k_ref.shape[0] // local
    z = lax.axis_index("seq")
    for p in range(2):
        for j, acc in enumerate((dkt, dvt)):
            col = pl.multiple_of(g * PAIR + p * TILE + third * j, TILE)
            for k in range(shards):
                at = pl.ds(pl.multiple_of(lax.rem(z - k + shards, shards) * local, TILE), local)
                dkv_ref[k * local : (k + 1) * local, pl.ds(col, TILE)] = acc[p, :, at].T.astype(jnp.bfloat16)

    @pl.when(g == pl.num_programs(0) - 1)
    def _():
        comm.rest(4 * 2 * nq)


def cross_backward(plan, arrays, q, kv, mix, up, weights):
    tokens, width = q.shape
    local = tokens // STREAMS
    full = kv.shape[0]
    grid = width // PAIR
    steps = 2 * local // TILE
    return pl.pallas_call(
        functools.partial(cross_bwd_kernel, local // TILE, plan),
        grid=(grid,),
        in_specs=[
            columns(tokens, 0), columns(full, 0), columns(full, grid),
            columns(tokens, 0), columns(tokens, 0), weights_spec(steps, full),
        ] + plan.in_specs(),
        out_specs=[columns(tokens, 0), whole(full, 2 * width)] + plan.out_specs(),
        scratch_shapes=[
            pltpu.VMEM((full, PAIR), jnp.bfloat16), pltpu.VMEM((full, PAIR), jnp.bfloat16),
            pltpu.VMEM((ROWS, full), jnp.float32), pltpu.VMEM((ROWS, full), jnp.bfloat16),
            pltpu.VMEM((ROWS, TILE), jnp.float32),
            pltpu.VMEM((2, TILE, full), jnp.float32), pltpu.VMEM((2, TILE, full), jnp.float32),
        ] + plan.scratch(),
        out_shape=[
            jax.ShapeDtypeStruct((tokens, width), jnp.bfloat16), jax.ShapeDtypeStruct((full, 2 * width), jnp.bfloat16),
        ] + plan.out_shapes(),
        compiler_params=pltpu.CompilerParams(collective_id=plan.number, has_side_effects=True, vmem_limit_bytes=58 << 20),
        cost_estimate=pl.CostEstimate(flops=40_000_000_000, bytes_accessed=30_000_000, transcendentals=8_000_000),
        name="cross_backward",
    )(q, kv, kv, mix, up, weights, *plan.views(arrays))


CHUNK = 256
SLOTS = 6


class Route:
    def __init__(self, dp, seq):
        self.dp_bits = dp.bit_length() - 1
        self.bits = self.dp_bits + seq.bit_length() - 1
        core = self.dp_bits - 1
        rest = list(reversed(range(core)))
        tail = list(reversed(range(self.dp_bits, self.bits)))
        self.orders = ([core] + rest + tail, [core] + rest[::-1] + tail)
        steps = self.bits
        self.lags = [0, 1] + [min(1 + 2 * k, 5) + max(0, k - 2) for k in range(1, steps)]

    def place(self, bit):
        if bit < self.dp_bits:
            return "dp", self.dp_bits - 1 - bit
        return "seq", self.bits - 1 - bit

    def mine(self, bit):
        axis, k = self.place(bit)
        return lax.rem(lax.axis_index(axis) // (1 << k), 2)

    def partner(self, bit):
        axis, k = self.place(bit)
        index = lax.axis_index(axis)
        return {axis: index + (1 - 2 * self.mine(bit)) * (1 << k)}

    def left(self, kind, k):
        return sorted(set(range(self.bits)) - set(self.orders[kind][:k]))


class Plan:
    def __init__(self, route, shapes, number, outs=None, chunk=CHUNK, kind=jnp.bfloat16):
        self.route, self.number, self.chunk, self.kind = route, number, chunk, kind
        self.outs = outs or [(n, 0) for n in range(len(shapes))]
        rows = min(shape[0] for shape in shapes)
        self.deep = rows >> route.bits
        self.subs = [shape[0] // rows for shape in shapes]
        self.pairs = [sub * (shape[1] // (2 * chunk)) for sub, shape in zip(self.subs, shapes)]
        self.total, self.many = sum(self.pairs), len(shapes)
        self.iterations = self.total + route.lags[route.bits]

    def views(self, arrays):
        lead = lambda sub: (2,) * self.route.bits + ((sub,) if sub > 1 else ())
        return [a.reshape(lead(sub) + (self.deep, a.shape[1])) for a, sub in zip(arrays, self.subs)]

    def in_specs(self):
        return [pl.BlockSpec(memory_space=pl.ANY)] * self.many

    def out_shapes(self):
        shapes = {}
        for (out, first), sub, pairs in zip(self.outs, self.subs, self.pairs):
            columns = first + pairs * 2 * self.chunk // sub
            shapes[out] = (sub * self.deep, max(columns, shapes.get(out, (0, 0))[1]))
        return [jax.ShapeDtypeStruct(shapes[out], jnp.float32) for out in sorted(shapes)]

    def out_specs(self):
        return [pl.BlockSpec(shape.shape, lambda *_: (0, 0)) for shape in self.out_shapes()]

    def scratch(self):
        bits = self.route.bits
        shape = lambda lead: (SLOTS, 2) + (2,) * lead + (self.deep, self.chunk)
        own = [pltpu.VMEM(shape(bits - 1), self.kind)]
        got = [pltpu.VMEM(shape(bits - 1 - k), self.kind) for k in range(bits)]
        out = [pltpu.VMEM(shape(bits - 1 - k), self.kind) for k in range(1, bits)]
        kept = [pltpu.VMEM(shape(bits - 1 - k), self.kind) for k in range(1, bits)]
        sems = [pltpu.SemaphoreType.DMA((2, SLOTS))] + [pltpu.SemaphoreType.DMA((bits, 2, SLOTS))] * 2
        return own + got + out + kept + sems


class Comm:
    def __init__(self, plan, arrays, results, scratch):
        route = plan.route
        bits = route.bits
        self.plan, self.route, self.arrays, self.results = plan, route, arrays, results
        self.pairs, self.subs, self.chunk, self.total = plan.pairs, plan.subs, plan.chunk, plan.total
        self.own = scratch[0]
        self.got = scratch[1 : 1 + bits]
        self.out = (None,) + tuple(scratch[1 + bits : 2 * bits])
        self.kept = (None,) + tuple(scratch[2 * bits : 3 * bits - 1])
        self.own_sem, self.send_sem, self.got_sem = scratch[3 * bits - 1 : 3 * bits + 2]

    def barrier(self):
        sem = pltpu.get_barrier_semaphore()
        size = 1 << (self.route.bits - self.route.dp_bits)
        others = [self.route.partner(bit) for bit in range(self.route.dp_bits)]
        others += [{"seq": lax.rem(lax.axis_index("seq") + k, size)} for k in range(1, size)]
        for other in others:
            pl.semaphore_signal(sem, inc=1, device_id=other, device_id_type=pl.DeviceIdType.MESH)
        pl.semaphore_wait(sem, len(others))

    def source(self, n, pair, kind, side):
        core = self.route.dp_bits - 1
        ref, subs = self.arrays[n], self.subs[n]
        across = ref.shape[-1] // (2 * self.chunk)
        col = pl.ds(pl.multiple_of(lax.rem(pair, across) * 2 * self.chunk + kind * self.chunk, self.chunk), self.chunk)
        index = [slice(None)] * self.route.bits
        index[core] = side
        if subs > 1:
            index.append(pair // across)
        return ref.at[tuple(index) + (slice(None), col)]

    def copy(self, k, kind, slot, src):
        return pltpu.make_async_remote_copy(
            src_ref=src,
            dst_ref=self.got[k].at[slot, kind],
            send_sem=self.send_sem.at[k, kind, slot],
            recv_sem=self.got_sem.at[k, kind, slot],
            device_id=self.route.partner(self.route.orders[kind][k]),
            device_id_type=pl.DeviceIdType.MESH,
        )

    def fetch(self, kind, slot, src):
        return pltpu.make_async_copy(src, self.own.at[slot, kind], self.own_sem.at[kind, slot])

    def begin(self, u):
        slot = lax.rem(u, SLOTS)
        side = self.route.mine(self.route.dp_bits - 1)
        first = 0
        for n, pairs in enumerate(self.pairs):
            @pl.when((u >= first) & (u < first + pairs))
            def _():
                for kind in range(2):
                    self.copy(0, kind, slot, self.source(n, u - first, kind, 1 - side)).start()
                    self.fetch(kind, slot, self.source(n, u - first, kind, side)).start()

            first += pairs

    def advance(self, k, u):
        route = self.route
        slot = lax.rem(u, SLOTS)
        for kind in range(2):
            if k == 1:
                filler = self.source(0, 0, kind, 0)
                self.fetch(kind, slot, filler).wait()
                self.copy(0, kind, slot, filler).wait()
                held = self.own
            else:
                self.copy(k - 1, kind, slot, self.out[k - 1].at[slot, kind]).wait()
                held = self.kept[k - 1]
            came = self.got[k - 1]
            if k == route.bits:
                total = held[slot, kind].astype(jnp.float32) + came[slot, kind].astype(jnp.float32)
                self.store(u, kind, total)
                continue
            bit = route.orders[kind][k]
            at = route.left(kind, k).index(bit)
            me = route.mine(bit)
            where = lambda side: (slot, kind) + (slice(None),) * at + (side,)
            theirs = where(1 - me)
            self.out[k][slot, kind] = held[theirs] + came[theirs]
            self.copy(k, kind, slot, self.out[k].at[slot, kind]).start()
            ours = where(me)
            self.kept[k][slot, kind] = held[ours] + came[ours]

    def store(self, u, kind, value):
        first, deep = 0, self.plan.deep
        for n, pairs in enumerate(self.pairs):
            out, column = self.plan.outs[n]
            across = pairs // self.subs[n]

            @pl.when((u >= first) & (u < first + pairs))
            def _():
                pair = u - first
                at = pl.multiple_of(column + (2 * lax.rem(pair, across) + kind) * self.chunk, self.chunk)
                rows = pl.ds(pl.multiple_of(pair // across * deep, deep), deep)
                self.results[out][rows, pl.ds(at, self.chunk)] = value

            first += pairs

    def step(self, t):
        @pl.when(t < self.total)
        def _():
            self.begin(t)

        for k in range(1, self.route.bits + 1):
            u = t - self.route.lags[k]

            @pl.when((u >= 0) & (u < self.total))
            def _():
                self.advance(k, u)


    def rest(self, begin):
        def body(t, _):
            self.step(t)
            return 0

        lax.fori_loop(begin, self.plan.iterations, body, 0)


class HeldComm(Comm):
    def source(self, n, pair, kind, side):
        index = [slice(None)] * self.route.bits
        index[self.route.dp_bits - 1] = side
        columns = slice(kind * self.chunk, (kind + 1) * self.chunk)
        return self.arrays[0].at[(lax.rem(pair, 2),) + tuple(index) + (slice(None), columns)]


class Handing:
    def __init__(self, shifts, pieces, source, target, sems):
        self.shifts, self.pieces = shifts, pieces
        self.source, self.target, self.sems = source, target, sems

    def copies(self, piece):
        z, size = lax.axis_index("seq"), lax.axis_size("seq")
        deep = self.source.shape[1] // self.pieces
        rows = pl.ds(pl.multiple_of(piece * deep, deep), deep)
        for n, shift in enumerate(self.shifts):
            yield pltpu.make_async_remote_copy(
                src_ref=self.source.at[n, rows],
                dst_ref=self.target.at[n, rows],
                send_sem=self.sems.at[0, n, piece],
                recv_sem=self.sems.at[1, n, piece],
                device_id={"seq": lax.rem(z - shift + size, size)},
                device_id_type=pl.DeviceIdType.MESH,
            )

    def step(self, t):
        @pl.when(t < self.pieces)
        def _():
            for copy in self.copies(t):
                copy.start()

    def finish(self):
        def body(t, _):
            for copy in self.copies(t):
                copy.wait()
            return 0

        lax.fori_loop(0, self.pieces, body, 0)


def handing_scratch(count, pieces):
    return [pltpu.SemaphoreType.DMA((2, count, pieces))]


def scatter_kernel(plan, few, shifts, *refs):
    many, outs = plan.many, len(plan.out_shapes())
    arrays, small, handed = refs[:many], refs[many], refs[many + 1]
    results, small_result, got = refs[many + 2 : many + 2 + outs], refs[many + 2 + outs], refs[many + 3 + outs]
    scratch = refs[many + 4 + outs : -1]
    half = len(scratch) // 2
    comm = Comm(plan, arrays, results, scratch[:half])
    other = Comm(few, [small], [small_result], scratch[half:])
    hand = Handing(shifts, 8, handed, got, refs[-1])
    comm.barrier()

    def body(t, _):
        hand.step(t)
        other.step(t)
        comm.step(t)
        return 0

    lax.fori_loop(0, plan.iterations, body, 0)
    hand.finish()


def scatter_sums(plan, few, shifts, arrays, small, handed):
    anywhere = pl.BlockSpec(memory_space=pl.ANY)
    return pl.pallas_call(
        functools.partial(scatter_kernel, plan, few, shifts),
        grid=(1,),
        in_specs=plan.in_specs() + few.in_specs() + [anywhere],
        out_specs=plan.out_specs() + few.out_specs() + [anywhere],
        out_shape=plan.out_shapes() + few.out_shapes() + [jax.ShapeDtypeStruct(handed.shape, handed.dtype)],
        scratch_shapes=plan.scratch() + few.scratch() + handing_scratch(len(shifts), 8),
        compiler_params=pltpu.CompilerParams(
            collective_id=plan.number, has_side_effects=True, vmem_limit_bytes=56 << 20
        ),
        cost_estimate=pl.CostEstimate(flops=20_000_000_000, bytes_accessed=60_000_000, transcendentals=0),
        name="weight_sums",
    )(*plan.views(arrays), *few.views([small]), handed)


def gelu_parts(x):
    t = 1.0 / (1.0 + jnp.abs(x) * (0.43 * 0.5**0.5))
    poly = jnp.float32(0.5 * 0.0709100743822703)
    for coef in (
        -0.2990317761502629, 0.3647352526676159, -0.06881910419857572, 0.23820862557883588,
        0.2074695458910066, 0.24398848761768033, 0.2425387164715943,
    ):
        poly = poly * t + 0.5 * coef
    bell = jnp.exp(x * x * -0.5)
    half = poly * t * bell
    below = jnp.where(x >= 0, 1.0 - half, half)
    return x * below, below + x * (bell * (1.0 / math.sqrt(2.0 * math.pi)))


def row_mean(x):
    return jnp.mean(x, axis=1, keepdims=True)


def column_sum(x):
    return jnp.sum(x, axis=0, keepdims=True)


def norm_back(upstream, unit, scale_inv, gain):
    along = upstream * gain
    return scale_inv * (along - row_mean(along) - unit * row_mean(along * unit))


def row_blocks(rows):
    return [slice(r, r + TILE) for r in range(0, rows, TILE)]


def mlp_fwd_kernel(x_ref, wu_ref, bu_ref, wd_ref, bd_ref, hidden_ref, gain_ref, shift_ref, cot_ref,
                   act_ref, slope_ref, result_ref, grad_ref, low_ref, sums_ref, acc):
    j = pl.program_id(0)
    rows = x_ref.shape[0]

    @pl.when(j == 0)
    def _():
        acc[...] = jnp.zeros_like(acc)

    step = 3 * TILE if rows % (3 * TILE) == 0 else TILE
    for r in range(0, rows, step):
        at = slice(r, r + step)
        pre = halves(x_ref[at, :], wu_ref[...], 1, 0) + bu_ref[...]
        value, slope = gelu_parts(pre)
        value = value.astype(jnp.bfloat16)
        act_ref[at, :] = value
        slope_ref[at, :] = slope.astype(jnp.bfloat16)
        acc[at, :] += halves(value, wd_ref[...], 1, 0)

    @pl.when(j == pl.num_programs(0) - 1)
    def _():
        sums_ref[...] = jnp.zeros_like(sums_ref)
        for at in row_blocks(rows):
            hidden = hidden_ref[at, :] + (acc[at, :] + bd_ref[...])
            centre = hidden - row_mean(hidden)
            scale_inv = lax.rsqrt(row_mean(centre * centre) + 1e-05)
            unit = centre * scale_inv
            result_ref[at, :] = (unit * gain_ref[...] + shift_ref[...]).astype(jnp.bfloat16)
            upstream = cot_ref[at, :].astype(jnp.float32)
            grad = norm_back(upstream, unit, scale_inv, gain_ref[...])
            grad_ref[at, :] = grad
            low_ref[at, :] = grad.astype(jnp.bfloat16)
            sums_ref[0:1, :] += column_sum(upstream * unit)
            sums_ref[1:2, :] += column_sum(upstream)
            sums_ref[2:3, :] += column_sum(grad)


HIDDEN_BLOCK = 512


def mlp_forward(x, wu, bu, wd, bd, hidden, gain, shift, cot):
    tokens, width = x.shape
    inner = wu.shape[1]
    block = HIDDEN_BLOCK
    full = lambda r, c: pl.BlockSpec((r, c), lambda j: (0, 0))
    across = pl.BlockSpec((tokens, block), lambda j: (0, j))
    return pl.pallas_call(
        mlp_fwd_kernel,
        grid=(inner // block,),
        in_specs=[
            full(tokens, width), pl.BlockSpec((width, block), lambda j: (0, j)), pl.BlockSpec((1, block), lambda j: (0, j)),
            pl.BlockSpec((block, width), lambda j: (j, 0)), full(1, width), full(tokens, width), full(1, width),
            full(1, width), full(tokens, width),
        ],
        out_specs=[across, across, full(tokens, width), full(tokens, width), full(tokens, width), full(8, width)],
        out_shape=[
            jax.ShapeDtypeStruct((tokens, inner), jnp.bfloat16), jax.ShapeDtypeStruct((tokens, inner), jnp.bfloat16),
            jax.ShapeDtypeStruct((tokens, width), jnp.bfloat16), jax.ShapeDtypeStruct((tokens, width), jnp.float32),
            jax.ShapeDtypeStruct((tokens, width), jnp.bfloat16), jax.ShapeDtypeStruct((8, width), jnp.float32),
        ],
        scratch_shapes=[pltpu.VMEM((tokens, width), jnp.float32)],
        compiler_params=pltpu.CompilerParams(vmem_limit_bytes=56 << 20),
        cost_estimate=pl.CostEstimate(flops=4 * tokens * width * inner, bytes_accessed=50_000_000, transcendentals=6_000_000),
        name="mlp_forward",
    )(x, wu, bu.reshape(1, -1), wd, bd.reshape(1, -1), hidden, gain.reshape(1, -1), shift.reshape(1, -1), cot)


def mlp_bwd_kernel(plan, low_ref, wd_ref, slope_ref, act_ref, x_ref, wu_ref, grad_ref, unit_ref, inv_ref, gain_ref,
                   up_ref, down_ref, bias_ref, two_ref, two_low_ref, sums_ref, result_ref, xt, acc, held, *scratch):
    j = pl.program_id(0)
    rows = x_ref.shape[0]
    comm = HeldComm(plan, [held], [result_ref], scratch)

    @pl.when(j == 0)
    def _():
        comm.barrier()
        acc[...] = jnp.zeros_like(acc)
        for c in range(0, x_ref.shape[1], TILE):
            xt[c : c + TILE, :] = x_ref[:, c : c + TILE].T

    grad = dot(low_ref[...], wd_ref[...], 1, 1).astype(jnp.bfloat16).astype(jnp.float32)
    grad = grad * slope_ref[...].astype(jnp.float32)
    bias_ref[...] = column_sum(grad)
    grad = grad.astype(jnp.bfloat16)
    acc[...] += dot(grad, wu_ref[...], 1, 1)
    up = dot(xt[...], grad, 1, 0).astype(jnp.bfloat16)

    @pl.when(j < plan.total)
    def _():
        held[lax.rem(j, 2)] = up.reshape(held.shape[1:])

    @pl.when(j >= plan.total)
    def _():
        up_ref[...] = up

    comm.step(j)
    down_ref[...] = dot(act_ref[...].T, low_ref[...], 1, 0).astype(jnp.bfloat16)

    @pl.when(j == pl.num_programs(0) - 1)
    def _():
        sums_ref[...] = jnp.zeros_like(sums_ref)
        for at in row_blocks(rows):
            upstream = grad_ref[at, :] + acc[at, :].astype(jnp.bfloat16).astype(jnp.float32)
            unit = unit_ref[at, :]
            two = norm_back(upstream, unit, inv_ref[at, :], gain_ref[...])
            two_ref[at, :] = two
            two_low_ref[at, :] = two.astype(jnp.bfloat16)
            sums_ref[0:1, :] += column_sum(upstream * unit)
            sums_ref[1:2, :] += column_sum(upstream)
        comm.rest(pl.num_programs(0))


def mlp_backward(plan, low, wd, slope, act, x, wu, grad, unit, inv, gain):
    tokens, width = x.shape
    inner = wu.shape[1]
    block = HIDDEN_BLOCK
    done = plan.total
    full = lambda r, c: pl.BlockSpec((r, c), lambda j: (0, 0))
    once = lambda r, c: pl.BlockSpec((r, c), lambda j: (0, 0), pipeline_mode=pl.Buffered(1))
    across = lambda r: pl.BlockSpec((r, block), lambda j: (0, j))
    down = pl.BlockSpec((block, width), lambda j: (j, 0))
    return pl.pallas_call(
        functools.partial(mlp_bwd_kernel, plan),
        grid=(inner // block,),
        in_specs=[
            once(tokens, width), down, across(tokens), across(tokens), once(tokens, width), across(width),
            once(tokens, width), once(tokens, width), once(tokens, 1), full(1, width),
        ],
        out_specs=[
            pl.BlockSpec((width, block), lambda j: (0, jnp.maximum(j - done, 0))), down, across(1),
            full(tokens, width), full(tokens, width), full(8, width),
        ] + plan.out_specs(),
        out_shape=[
            jax.ShapeDtypeStruct((width, inner - done * block), jnp.bfloat16), jax.ShapeDtypeStruct((inner, width), jnp.bfloat16),
            jax.ShapeDtypeStruct((1, inner), jnp.float32), jax.ShapeDtypeStruct((tokens, width), jnp.float32),
            jax.ShapeDtypeStruct((tokens, width), jnp.bfloat16), jax.ShapeDtypeStruct((8, width), jnp.float32),
        ] + plan.out_shapes(),
        scratch_shapes=[
            pltpu.VMEM((width, tokens), jnp.bfloat16), pltpu.VMEM((tokens, width), jnp.float32),
            pltpu.VMEM((2,) + (2,) * plan.route.bits + (plan.deep, block), jnp.bfloat16),
        ] + plan.scratch(),
        compiler_params=pltpu.CompilerParams(collective_id=plan.number, has_side_effects=True, vmem_limit_bytes=60 << 20),
        cost_estimate=pl.CostEstimate(flops=8 * tokens * width * inner, bytes_accessed=70_000_000, transcendentals=0),
        name="mlp_backward",
    )(low, wd, slope, act, x, wu, grad, unit, inv, gain.reshape(1, -1))


EARLY = 5


def normalize(hidden, gain, shift):
    centre = hidden - jnp.mean(hidden, axis=-1, keepdims=True)
    scale_inv = lax.rsqrt(jnp.mean(centre * centre, axis=-1, keepdims=True) + 1e-05)
    unit = centre * scale_inv
    return (unit * gain + shift, unit, scale_inv)


def normalize_back(upstream, unit, scale_inv, gain):
    along = upstream * gain
    inner = (
        along
        - jnp.mean(along, axis=-1, keepdims=True)
        - unit * jnp.mean(along * unit, axis=-1, keepdims=True)
    )
    return (scale_inv * inner, jnp.sum(upstream * unit, axis=0), jnp.sum(upstream, axis=0))


def gate(value, *others):
    return lax.optimization_barrier((value,) + others)[0]


def shards(
    inputs,
    encoded,
    target_lengths,
    source_lengths,
    query_key_value,
    bucket_weight,
    self_output,
    cross_query,
    cross_key_value,
    cross_output,
    up_weight,
    up_bias,
    down_weight,
    down_bias,
    norm_gain,
    norm_shift,
    cotangent,
):
    row_count, streams, local, width = inputs.shape
    parts, size = lax.axis_size("dp"), lax.axis_size("seq")
    route = Route(parts, size)
    full = local * size
    z = lax.axis_index("seq")
    begin = z * local
    bf16, f32 = jnp.bfloat16, jnp.float32
    tokens = streams * local
    up_chain = [(i, i + 1) for i in range(size - 1)]
    down_chain = [(i + 1, i) for i in range(size - 1)]

    def mm(left, right):
        return jnp.dot(left, right, preferred_element_type=f32)

    def mm_t(left, right):
        return lax.dot_general(left, right, (((1,), (1,)), ((), ())), preferred_element_type=f32)

    def wgrad(left, right):
        return dot(left, right, 0, 0).astype(bf16)

    flat = inputs.reshape(tokens, width)
    main = flat[:local]
    hops = HALO // local
    passing, pieces = main, []
    for _ in range(hops):
        passing = lax.ppermute(passing, "seq", up_chain)
        pieces.insert(0, passing)
    halo = jnp.concatenate(pieces, axis=0)
    extended = jnp.concatenate([halo, flat], axis=0)
    own_source = encoded.reshape(local, width)
    waiting, halo = lax.optimization_barrier((own_source, halo))
    sources = [own_source] + [
        lax.ppermute(waiting, "seq", [(i, (i + k) % size) for i in range(size)]) for k in range(1, size)
    ]
    source = jnp.concatenate(sources, axis=0)

    here = begin + jnp.arange(local, dtype=jnp.int32)
    ends = jnp.cumsum(target_lengths[0])
    source_ends = jnp.cumsum(source_lengths[0])
    passed = here[:, None] >= ends[None, :]
    number = jnp.sum(passed.astype(jnp.int32), axis=1)
    start = jnp.max(jnp.where(passed, ends[None, :], 0), axis=1) - begin + HALO
    is_doc = number[:, None] == jnp.arange(ends.shape[0] + 1, dtype=jnp.int32)[None, :]
    zero = jnp.zeros((1,), jnp.int32)
    first = jnp.sum(jnp.where(is_doc, jnp.concatenate([zero, source_ends])[None, :], 0), axis=1)
    last = jnp.sum(jnp.where(is_doc, jnp.concatenate([source_ends, zero + full])[None, :], 0), axis=1)
    edge = start[::TILE]
    at = HALO + TILE * jnp.arange(local // TILE, dtype=jnp.int32)
    need = 1 + (edge < at - TILE).astype(jnp.int32) + (edge < at - 3 * TILE).astype(jnp.int32)
    low_key = first[::TILE] // PAIR
    count = (last[TILE - 1 :: TILE] + PAIR - 1) // PAIR - low_key

    names = jnp.arange(TILE, dtype=jnp.int32)[None, :]
    place = begin - HALO + jnp.arange(HALO + local, dtype=jnp.int32)
    key_doc = jnp.where(place >= 0, jnp.sum((place[:, None] >= ends[None, :]).astype(jnp.int32), axis=1), TILE)
    place = jnp.arange(full, dtype=jnp.int32)
    source_doc = jnp.sum((place[:, None] >= source_ends[None, :]).astype(jnp.int32), axis=1)
    doc = (number[:, None] == names).astype(bf16)
    block = lambda of: jnp.where((names < 8) & (of[:, None] != names), NEG, 0.0).astype(bf16)
    target_aug, source_aug = block(key_doc), block(source_doc)
    skew, hot = bias_tables()

    query_main = mm(flat, query_key_value).astype(bf16)
    relative = mm(flat, bucket_weight)
    proj = query_main
    halo_kv = mm(halo, query_key_value[:, width:]).astype(bf16)
    self_mix, self_weights = self_forward(need, proj, halo_kv, relative, doc, target_aug, skew)
    hidden_one, unit_one, inv_one = normalize(flat.astype(f32) + mm(self_mix, self_output), norm_gain[0], norm_shift[0])
    low_one = hidden_one.astype(bf16)
    cross_q = mm(low_one, cross_query).astype(bf16)
    source_kv = mm(source, cross_key_value).astype(bf16)
    cross_mix, cross_weights = cross_forward(low_key, count, cross_q, source_kv, doc, source_aug)
    hidden_two, unit_two, inv_two = normalize(hidden_one + mm(cross_mix, cross_output), norm_gain[1], norm_shift[1])
    low_two = hidden_two.astype(bf16)
    activated, slope, result, three_grad, three_low, three_sums = mlp_forward(
        low_two, up_weight, up_bias, down_weight, down_bias, hidden_two, norm_gain[2], norm_shift[2],
        cotangent.reshape(tokens, width),
    )
    gain_three, shift_three, down_bias_grad = three_sums[0], three_sums[1], three_sums[2]

    early = (width, EARLY * HIDDEN_BLOCK)
    early_plan = Plan(route, [early], 3)
    up_part, down_part, up_bias_grad, two_grad, two_low, two_sums, up_early = mlp_backward(
        early_plan, three_low, down_weight, slope, activated, low_two, up_weight, three_grad, unit_two, inv_two, norm_gain[1]
    )
    gain_two, shift_two = two_sums[0], two_sums[1]
    up_bias_grad = up_bias_grad.reshape(-1)
    cross_up = mm_t(two_low, cross_output).astype(bf16)
    wide = [up_part, down_part]
    wide_plan = Plan(route, [a.shape for a in wide], 0)
    query_low, source_low, up_late, down_grad = cross_backward(
        wide_plan, wide, cross_q, source_kv, cross_mix, cross_up, cross_weights
    )
    up_grad = jnp.concatenate([up_early, up_late], axis=1)
    source_back = mm_t(source_low, cross_key_value).astype(bf16)
    far = size // 2
    shifts = [k for k in range(1, size) if k != far]
    block = lambda k: source_back[k * local : (k + 1) * local]
    hidden_one_grad = two_grad + mm_t(query_low, cross_query).astype(bf16).astype(f32)
    one_grad, gain_one, shift_one = normalize_back(hidden_one_grad, unit_one, inv_one, norm_gain[0])
    one_low = one_grad.astype(bf16)
    self_up = mm_t(one_low, self_output).astype(bf16)
    square = [
        wgrad(source, source_low),
        wgrad(cross_mix, two_low),
        wgrad(low_one, query_low),
        wgrad(self_mix, one_low),
    ]
    square_plan = Plan(route, [a.shape for a in square], 1)
    query_low, kv_low, table_low, back, came, *square_sums = self_backward(
        square_plan, square, shifts, jnp.stack([block(k) for k in shifts]), proj, halo_kv, hot, self_mix, self_up, self_weights,
        query_key_value, bucket_weight,
    )
    cross_kv_grad, cross_out_grad, cross_query_grad, self_out_grad = square_sums
    returned = []
    for k in range(1, hops + 1):
        piece = back[HALO - k * local : HALO - (k - 1) * local]
        returned.append(lax.ppermute(piece, "seq", [(i, i - k) for i in range(k, size)]))
    back = back[HALO:].astype(f32).reshape(streams, local, width)
    passing = sum(got.astype(f32) for got in returned)
    back = jnp.concatenate([back[:1] + passing[None], back[1:]], axis=0).reshape(tokens, width)
    inputs_grad = (one_grad + back.astype(bf16).astype(f32)).astype(bf16)
    devices = parts * size
    gains = jnp.stack([gain_one, gain_two, gain_three]).reshape(3, devices, -1).transpose(1, 0, 2)
    shifts = jnp.stack([shift_one, shift_two, shift_three]).reshape(3, devices, -1).transpose(1, 0, 2)
    each = width // devices
    small = jnp.concatenate(
        [
            up_bias_grad.reshape(devices, -1),
            down_bias_grad.reshape(devices, -1),
            gains.reshape(devices, -1),
            shifts.reshape(devices, -1),
        ],
        axis=1,
    )
    used = small.shape[1]
    small = jnp.pad(small, ((0, 0), (0, 16 * TILE - used))).reshape(devices * 8, 2 * TILE)
    arrays = [
        wgrad(flat, query_low),
        wgrad(extended, kv_low),
        wgrad(flat, gate(table_low, inputs_grad)),
    ]
    plan = Plan(route, [a.shape for a in arrays], 2, [(0, 0), (0, width), (1, 0)])
    few = Plan(route, [small.shape], 2, chunk=TILE, kind=f32)
    qkv_grad, bucket_grad, small, last_came = scatter_sums(plan, few, [far], arrays, small, block(far)[None])
    encoded_grad = source_back[:local].astype(f32) + jnp.sum(came.astype(f32), axis=0) + last_came[0].astype(f32)
    small = small.reshape(-1)
    wide_each = up_bias_grad.shape[0] // devices
    cuts = [wide_each, wide_each + each, wide_each + 4 * each, used]
    up_bias_grad, down_bias_grad, gains, shifts, _ = jnp.split(small, cuts)
    return (
        result.reshape(inputs.shape),
        inputs_grad.reshape(inputs.shape),
        encoded_grad.astype(bf16).reshape(encoded.shape),
        qkv_grad,
        bucket_grad,
        self_out_grad,
        cross_query_grad,
        cross_kv_grad,
        cross_out_grad,
        up_grad,
        up_bias_grad,
        down_grad,
        down_bias_grad,
        gains.reshape(3, each),
        shifts.reshape(3, each),
    )


def solution(mesh):
    placed = (
        P("dp", None, "seq", None),
        P("dp", "seq", None),
        P("dp", None),
        P("dp", None),
        P(),
        P(),
        P(),
        P(),
        P(),
        P(),
        P(),
        P(),
        P(),
        P(),
        P(),
        P(),
        P("dp", None, "seq", None),
    )
    return jax.shard_map(
        shards,
        mesh=mesh,
        in_specs=placed,
        out_specs=(
            P("dp", None, "seq", None),
            P("dp", None, "seq", None),
            P("dp", "seq", None),
            P(("dp", "seq"), None),
            P(("dp", "seq"), None),
            P(("dp", "seq"), None),
            P(("dp", "seq"), None),
            P(("dp", "seq"), None),
            P(("dp", "seq"), None),
            P(("dp", "seq"), None),
            P(("dp", "seq")),
            P(("dp", "seq"), None),
            P(("dp", "seq")),
            P(None, ("dp", "seq")),
            P(None, ("dp", "seq")),
        ),
        check_vma=False,
    )
```
